256 devices in a mesh: copy: 4 (over x_hi, core), space: 64 (over y, z, x_lo).
Axes of the slice: x: 4 (x_hi: 2, x_lo: 2; x = x_hi * 2 + x_lo), y: 4, z: 8, core: 2. Of those that a mesh axis runs over, the one named last changes fastest.
Arguments:
- noisy_tokens: bfloat16 [4, 256, 256, 384], P('copy', 'space'), may hold values from -6 to 6
- grad_out: bfloat16 [4, 256, 256, 384], P('copy', 'space'), may hold values from -6 to 6
- filter_weight: bfloat16 [2, 256, 256, 384], P(None, None, 'space'), may hold values from -4 to 4
- weight_in: bfloat16 [384, 1536], replicated, may hold values from -0.3125 to 0.3125
- weight_out: bfloat16 [1536, 384], replicated, may hold values from -0.15625 to 0.15625
- gain_one: float32 [384], replicated, may hold values from 0.1 to 1.9
- gain_two: float32 [384], replicated, may hold values from 0.1 to 1.9
Outputs:
- block_out: bfloat16 [4, 256, 256, 384], P('copy', 'space')
- grad_tokens: bfloat16 [4, 256, 256, 384], P('copy', 'space')
- grad_filter: float32 [2, 256, 256, 384], P(None, None, 'space')
- grad_weight_in: bfloat16 [384, 1536], replicated
- grad_weight_out: bfloat16 [1536, 384], replicated
- grad_gain_one: float32 [384], replicated
- grad_gain_two: float32 [384], replicated
The draws below stay inside these ranges and needn't reach their ends.
All inputs are finite; a program needn't handle non-finite values.
Results may differ from the reference program's by a relative error of at most 0.024.
Values may be sent and summed in bfloat16 or wider, within the bound.
A program may use at most 128 MiB of HBM per device.

```python
import math
import jax
import jax.numpy as jnp
from jax import lax

C = 384
FF = 1536
H = 256
W = 256
COPIES = 4


def shard_levels(stream_key, dims, shards, least, largest):
    level = 1.0
    for position, shards_of in shards:
        heights = jax.random.uniform(jax.random.fold_in(jax.random.fold_in(stream_key, 6), position), (shards_of,), jnp.float32, least / len(shards), largest / len(shards))
        level = level * jnp.repeat(jnp.exp(heights), dims[position] // shards_of).reshape((-1,) + (1,) * (len(dims) - 1 - position))
    return level


def normal_values(stream_key, dims, deviation, most, shards=(), kind=jnp.bfloat16):
    array = deviation * jax.random.normal(stream_key, dims, jnp.float32)
    if shards:
        array = array * shard_levels(stream_key, dims, shards, -0.22, 0.18)
    return jnp.clip(array, -most, most).astype(kind)


def setup_inputs(seed: int = 0) -> dict:
    arg_keys = jax.random.split(jax.random.key(seed), 8)
    return {
        "noisy_tokens": normal_values(arg_keys[0], (COPIES, H, W, C), 1.0, 6.0, ((0, 4), (1, 64))),
        "grad_out": normal_values(arg_keys[1], (COPIES, H, W, C), 1.0, 6.0, ((0, 4), (1, 64))),
        "filter_weight": normal_values(arg_keys[2], (2, H, W, C), 0.7, 4.0, ((2, 64),)),
        "weight_in": normal_values(arg_keys[3], (C, FF), C ** -0.5, 0.3125),
        "weight_out": normal_values(arg_keys[4], (FF, C), FF ** -0.5, 0.15625),
        "gain_one": jnp.clip(1.0 + 0.18 * jax.random.normal(arg_keys[5], (C,), jnp.float32), 0.1, 1.9),
        "gain_two": jnp.clip(1.0 + 0.18 * jax.random.normal(arg_keys[6], (C,), jnp.float32), 0.1, 1.9),
    }


EPS = 1e-06

def dft_parts(length):
    index = jnp.arange(length, dtype=jnp.int32)
    phase = index[:, None] * index[None, :] % length
    angle = phase.astype(jnp.float32) * (2.0 * math.pi / length)
    factor = 1.0 / math.sqrt(length)
    return ((jnp.cos(angle) * factor).astype(jnp.bfloat16), (jnp.sin(angle) * factor).astype(jnp.bfloat16))

def row_table(length):
    cosine, sine = dft_parts(length)
    return jnp.stack([cosine, -sine])

def column_table(length, direction):
    cosine, sine = dft_parts(length)
    upper = jnp.stack([cosine, direction * sine], axis=1)
    lower = jnp.stack([-direction * sine, cosine], axis=1)
    return jnp.stack([upper, lower])

def layer_norm(values):
    centre = lax.optimization_barrier(jnp.mean(values, axis=-1, keepdims=True))
    centred = values - centre
    variance = lax.optimization_barrier(jnp.mean(centred * centred, axis=-1, keepdims=True))
    rstd_value = lax.rsqrt(variance + EPS)
    return (centred * rstd_value, rstd_value)

def norm_backward(upstream, normed, rstd_value, gain):
    scaled = upstream * gain
    result = (scaled - lax.optimization_barrier(jnp.mean(scaled, axis=-1, keepdims=True)) - normed * lax.optimization_barrier(jnp.mean(scaled * normed, axis=-1, keepdims=True))) * rstd_value
    lead = tuple(range(upstream.ndim - 1))
    return (result, lax.optimization_barrier(jnp.sum(upstream * normed, axis=lead)))

def apply_filter(spectrum, filter_weight, direction):
    real_part = spectrum[0].astype(jnp.float32)
    imag_part = spectrum[1].astype(jnp.float32)
    kernel_real = filter_weight[0].astype(jnp.float32)
    kernel_imag = direction * filter_weight[1].astype(jnp.float32)
    return jnp.stack([kernel_real * real_part - kernel_imag * imag_part, kernel_real * imag_part + kernel_imag * real_part])

def exact_gelu(values):
    return jax.nn.gelu(values, approximate=False)

def spectral(values, filter_weight, direction):
    highest = lax.Precision.HIGHEST
    rows_tab = row_table(W).astype(jnp.float32)
    rows = jnp.einsum('pkw,hwc->phkc', rows_tab, values.astype(jnp.float32), precision=highest).astype(jnp.bfloat16)
    spectrum = jnp.einsum('qmph,phkc->qmkc', column_table(H, 1).astype(jnp.float32), rows.astype(jnp.float32), precision=highest).astype(jnp.bfloat16)
    weighted = apply_filter(spectrum, filter_weight, direction).astype(jnp.bfloat16)
    returned = jnp.einsum('qmph,phkc->qmkc', column_table(H, -1).astype(jnp.float32), weighted.astype(jnp.float32), precision=highest).astype(jnp.bfloat16)
    output = jnp.einsum('pkw,phkc->hwc', rows_tab, returned.astype(jnp.float32), precision=highest)
    return (output, spectrum)

def one_copy(carry, pair):
    noisy, upstream_grad = pair
    filter_weight, weight_in, weight_out, gain_one, gain_two, totals = carry
    inputs = noisy.astype(jnp.float32)
    normed_one, rstd_one = layer_norm(inputs)
    mixed_in = (normed_one * gain_one).astype(jnp.bfloat16)
    spatial, spectrum = spectral(mixed_in, filter_weight, 1)
    normed_two, rstd_two = layer_norm(spatial)
    mlp_in = (normed_two * gain_two).astype(jnp.bfloat16).reshape(-1, C)
    preact = jnp.dot(mlp_in, weight_in, preferred_element_type=jnp.float32)
    activated = exact_gelu(preact).astype(jnp.bfloat16)
    mlp_out = jnp.dot(activated, weight_out, preferred_element_type=jnp.float32)
    block_out = (inputs + mlp_out.reshape(inputs.shape)).astype(jnp.bfloat16)
    upstream = upstream_grad.reshape(-1, C)
    grad_act = jnp.dot(upstream, weight_out.T, preferred_element_type=jnp.float32)
    grad_pre = jax.vjp(exact_gelu, preact)[1](grad_act)[0].astype(jnp.bfloat16)
    sum_out = jnp.dot(activated.T, upstream, preferred_element_type=jnp.float32)
    sum_in = jnp.dot(mlp_in.T, grad_pre, preferred_element_type=jnp.float32)
    grad_mlp = jnp.dot(grad_pre, weight_in.T, preferred_element_type=jnp.float32).reshape(inputs.shape)
    grad_spatial, sum_gain_two = norm_backward(grad_mlp, normed_two, rstd_two, gain_two)
    back_spatial, adjoint = spectral(grad_spatial.astype(jnp.bfloat16), filter_weight, -1)
    spec_f = spectrum.astype(jnp.float32)
    adj_f = adjoint.astype(jnp.float32)
    filter_terms = jnp.stack([adj_f[0] * spec_f[0] + adj_f[1] * spec_f[1], adj_f[1] * spec_f[0] - adj_f[0] * spec_f[1]])
    grad_normed, sum_gain_one = norm_backward(back_spatial, normed_one, rstd_one, gain_one)
    grad_tokens = (upstream_grad.astype(jnp.float32) + grad_normed).astype(jnp.bfloat16)
    new_totals = (totals[0] + filter_terms, totals[1] + sum_in, totals[2] + sum_out, totals[3] + sum_gain_one, totals[4] + sum_gain_two)
    return ((filter_weight, weight_in, weight_out, gain_one, gain_two, new_totals), (block_out, grad_tokens))

def reference(noisy_tokens, grad_out, filter_weight, weight_in, weight_out, gain_one, gain_two):
    totals = (jnp.zeros((2, H, W, C), jnp.float32), jnp.zeros((C, FF), jnp.float32), jnp.zeros((FF, C), jnp.float32), jnp.zeros((C,), jnp.float32), jnp.zeros((C,), jnp.float32))
    carry = (filter_weight, weight_in, weight_out, gain_one, gain_two, totals)
    carry, outputs = lax.scan(one_copy, carry, (noisy_tokens, grad_out))
    totals = carry[5]
    factor = 1.0 / math.sqrt(COPIES * H * W)
    return (outputs[0], outputs[1], totals[0], (totals[1] * factor).astype(jnp.bfloat16), (totals[2] * factor).astype(jnp.bfloat16), totals[3] * factor, totals[4] * factor)
```

```python
import functools
import math

import jax
import jax.numpy as jnp
from jax import lax
from jax.experimental import pallas as pl
from jax.experimental.pallas import tpu as pltpu
from jax.sharding import PartitionSpec as P

MESH = pl.DeviceIdType.MESH

EPS = 1e-06


def _copy_sum_kernel(n, rows, x_ref, o_ref, slots, send_sem, recv_sem, local_sem):
    me = lax.axis_index("copy")
    sp = lax.axis_index("space")
    barrier = pltpu.get_barrier_semaphore()
    for d in range(1, n):
        peer = lax.rem(me + d, n)
        pl.semaphore_signal(barrier, inc=1, device_id=(peer, sp), device_id_type=MESH)
    pl.semaphore_wait(barrier, n - 1)
    local = pltpu.make_async_copy(x_ref, slots.at[me], local_sem)
    local.start()
    sends = []
    for d in range(1, n):
        peer = lax.rem(me + d, n)
        c = pltpu.make_async_remote_copy(
            src_ref=x_ref,
            dst_ref=slots.at[me],
            send_sem=send_sem.at[d - 1],
            recv_sem=recv_sem.at[me],
            device_id=(peer, sp),
            device_id_type=MESH,
        )
        c.start()
        sends.append(c)
    for d in range(1, n):
        src = lax.rem(me + n - d, n)
        pltpu.make_async_remote_copy(
            src_ref=x_ref,
            dst_ref=slots.at[src],
            send_sem=send_sem.at[d - 1],
            recv_sem=recv_sem.at[src],
            device_id=(src, sp),
            device_id_type=MESH,
        ).wait_recv()
    local.wait()
    for c in sends:
        c.wait_send()
    block = 64

    def body(i, carry):
        r = pl.ds(pl.multiple_of(i * block, block), block)
        acc = slots[0, r, :].astype(jnp.float32)
        for j in range(1, n):
            acc = acc + slots[j, r, :].astype(jnp.float32)
        o_ref[r, :] = acc
        return carry

    lax.fori_loop(0, rows // block, body, 0)


def copy_sum(x, n):
    rows, cols = x.shape
    return pl.pallas_call(
        functools.partial(_copy_sum_kernel, n, rows),
        out_shape=jax.ShapeDtypeStruct((rows, cols), jnp.float32),
        in_specs=[pl.BlockSpec(memory_space=pltpu.VMEM)],
        out_specs=pl.BlockSpec(memory_space=pltpu.VMEM),
        scratch_shapes=[
            pltpu.VMEM((n, rows, cols), x.dtype),
            pltpu.SemaphoreType.DMA((n - 1,)),
            pltpu.SemaphoreType.DMA((n,)),
            pltpu.SemaphoreType.DMA,
        ],
        compiler_params=pltpu.CompilerParams(
            collective_id=1, has_side_effects=True, vmem_limit_bytes=48 * 1024 * 1024
        ),
        cost_estimate=pl.CostEstimate(
            flops=n * rows * cols, transcendentals=0, bytes_accessed=(n + 2) * rows * cols * 2
        ),
    )(x)


def dft_parts(length):
    index = jnp.arange(length, dtype=jnp.int32)
    phase = index[:, None] * index[None, :] % length
    angle = phase.astype(jnp.float32) * (2.0 * math.pi / length)
    factor = 1.0 / math.sqrt(length)
    return (
        (jnp.cos(angle) * factor).astype(jnp.bfloat16),
        (jnp.sin(angle) * factor).astype(jnp.bfloat16),
    )


def row_table(length):
    cosine, sine = dft_parts(length)
    return jnp.stack([cosine, -sine])


def column_table(length, direction):
    cosine, sine = dft_parts(length)
    upper = jnp.stack([cosine, direction * sine], axis=1)
    lower = jnp.stack([-direction * sine, cosine], axis=1)
    return jnp.stack([upper, lower])


def layer_norm(values):
    centre = jnp.mean(values, axis=-1, keepdims=True)
    centred = values - centre
    variance = jnp.mean(centred * centred, axis=-1, keepdims=True)
    rstd_value = lax.rsqrt(variance + EPS)
    return (centred * rstd_value, rstd_value)


def norm_backward(upstream, normed, rstd_value, gain):
    scaled = upstream * gain
    result = (
        scaled
        - jnp.mean(scaled, axis=-1, keepdims=True)
        - normed * jnp.mean(scaled * normed, axis=-1, keepdims=True)
    ) * rstd_value
    lead = tuple(range(upstream.ndim - 1))
    return (result, jnp.sum(upstream * normed, axis=lead))


def apply_filter(spectrum, filter_weight, direction):
    real_part = spectrum[0].astype(jnp.float32)
    imag_part = spectrum[1].astype(jnp.float32)
    kernel_real = filter_weight[0].astype(jnp.float32)
    kernel_imag = direction * filter_weight[1].astype(jnp.float32)
    return jnp.stack(
        [
            kernel_real * real_part - kernel_imag * imag_part,
            kernel_real * imag_part + kernel_imag * real_part,
        ]
    )


def exact_gelu(values):
    return jax.nn.gelu(values, approximate=False)


def spectral(values, filter_weight, direction):
    width = values.shape[2]
    rows_tab = row_table(width)
    rows = jnp.einsum(
        "pkw,bhwc->pbhkc", rows_tab, values, preferred_element_type=jnp.float32
    ).astype(jnp.bfloat16)
    columns = lax.all_to_all(rows, "space", split_axis=3, concat_axis=2, tiled=True)
    height = columns.shape[2]
    spectrum = jnp.einsum(
        "qmph,pbhkc->qbmkc", column_table(height, 1), columns, preferred_element_type=jnp.float32
    ).astype(jnp.bfloat16)
    weighted = apply_filter(spectrum, filter_weight[:, None], direction).astype(jnp.bfloat16)
    returned = jnp.einsum(
        "qmph,pbhkc->qbmkc", column_table(height, -1), weighted, preferred_element_type=jnp.float32
    ).astype(jnp.bfloat16)
    back_rows = lax.all_to_all(returned, "space", split_axis=2, concat_axis=3, tiled=True)
    output = jnp.einsum("pkw,pbhkc->bhwc", rows_tab, back_rows, preferred_element_type=jnp.float32)
    return (output, spectrum)


def body(noisy_tokens, grad_out, filter_weight, weight_in, weight_out, gain_one, gain_two):
    batch, rows_dev, width, chans = noisy_tokens.shape
    inputs = noisy_tokens.astype(jnp.float32)
    normed_one, rstd_one = layer_norm(inputs)
    mixed_in = (normed_one * gain_one).astype(jnp.bfloat16)
    spatial, spectrum = spectral(mixed_in, filter_weight, 1)
    normed_two, rstd_two = layer_norm(spatial)
    mlp_in = (normed_two * gain_two).astype(jnp.bfloat16).reshape(-1, chans)
    preact = jnp.dot(mlp_in, weight_in, preferred_element_type=jnp.float32)
    activated = exact_gelu(preact).astype(jnp.bfloat16)
    mlp_out = jnp.dot(activated, weight_out, preferred_element_type=jnp.float32)
    block_out = (inputs + mlp_out.reshape(inputs.shape)).astype(jnp.bfloat16)
    upstream = grad_out.reshape(-1, chans)
    grad_act = jnp.dot(upstream, weight_out.T, preferred_element_type=jnp.float32)
    grad_pre = jax.vjp(exact_gelu, preact)[1](grad_act)[0].astype(jnp.bfloat16)
    sum_out = jnp.dot(activated.T, upstream, preferred_element_type=jnp.float32)
    sum_in = jnp.dot(mlp_in.T, grad_pre, preferred_element_type=jnp.float32)
    grad_mlp = jnp.dot(grad_pre, weight_in.T, preferred_element_type=jnp.float32).reshape(
        inputs.shape
    )
    grad_spatial, sum_gain_two = norm_backward(grad_mlp, normed_two, rstd_two, gain_two)
    back_spatial, adjoint = spectral(grad_spatial.astype(jnp.bfloat16), filter_weight, -1)
    spec_f = spectrum.astype(jnp.float32)
    adj_f = adjoint.astype(jnp.float32)
    filter_terms = jnp.stack(
        [
            jnp.sum(adj_f[0] * spec_f[0] + adj_f[1] * spec_f[1], axis=0),
            jnp.sum(adj_f[1] * spec_f[0] - adj_f[0] * spec_f[1], axis=0),
        ]
    )
    fshape = filter_terms.shape
    grad_filter = copy_sum(
        filter_terms.astype(jnp.bfloat16).reshape(fshape[0] * fshape[1], fshape[2] * fshape[3]),
        lax.axis_size("copy"),
    ).reshape(fshape)
    grad_normed, sum_gain_one = norm_backward(back_spatial, normed_one, rstd_one, gain_one)
    grad_tokens = (grad_out.astype(jnp.float32) + grad_normed).astype(jnp.bfloat16)
    total_tokens = batch * lax.axis_size("copy") * rows_dev * lax.axis_size("space") * width
    factor = 1.0 / math.sqrt(total_tokens)
    both = ("copy", "space")
    weight_sums = lax.psum((sum_in.astype(jnp.bfloat16), sum_out.astype(jnp.bfloat16)), both)
    weight_sums = [(s.astype(jnp.float32) * factor).astype(jnp.bfloat16) for s in weight_sums]
    gains = lax.psum(lax.psum(jnp.stack([sum_gain_one, sum_gain_two]), "copy"), "space")
    return (
        block_out,
        grad_tokens,
        grad_filter,
        weight_sums[0],
        weight_sums[1],
        gains[0] * factor,
        gains[1] * factor,
    )


def solution(mesh):
    return jax.shard_map(
        body,
        mesh=mesh,
        in_specs=(
            P("copy", "space", None, None),
            P("copy", "space", None, None),
            P(None, None, "space", None),
            P(),
            P(),
            P(),
            P(),
        ),
        out_specs=(
            P("copy", "space", None, None),
            P("copy", "space", None, None),
            P(None, None, "space", None),
            P(),
            P(),
            P(),
            P(),
        ),
        check_vma=False,
    )
```

```python
import functools
import math

import jax
import jax.numpy as jnp
from jax import lax
from jax.experimental import pallas as pl
from jax.experimental.pallas import tpu as pltpu
from jax.sharding import PartitionSpec as P

MESH = pl.DeviceIdType.MESH

EPS = 1e-06


def _partner(idx, bit):
    step = 1 << bit
    flip = 1 - 2 * ((idx // step) % 2)
    return idx + flip * step


def _tree_sum_kernel(n_copy, n_space, x_ref, o_ref, send_buf, recv_buf, send_sem, recv_sem):
    me_c = lax.axis_index("copy")
    me_s = lax.axis_index("space")
    bits = []
    for b in range(n_space.bit_length() - 1):
        bits.append(("space", b))
    for b in range(n_copy.bit_length() - 1):
        bits.append(("copy", b))

    def peer(axis, b):
        if axis == "space":
            return (me_c, _partner(me_s, b))
        return (_partner(me_c, b), me_s)

    barrier = pltpu.get_barrier_semaphore()
    for axis, b in bits:
        pl.semaphore_signal(barrier, inc=1, device_id=peer(axis, b), device_id_type=MESH)
    pl.semaphore_wait(barrier, len(bits))
    acc = x_ref[...]
    copies = []
    for s, (axis, b) in enumerate(bits):
        send_buf[s] = acc
        c = pltpu.make_async_remote_copy(
            src_ref=send_buf.at[s],
            dst_ref=recv_buf.at[s],
            send_sem=send_sem.at[s],
            recv_sem=recv_sem.at[s],
            device_id=peer(axis, b),
            device_id_type=MESH,
        )
        c.start()
        c.wait_recv()
        copies.append(c)
        acc = acc + recv_buf[s]
    for c in copies:
        c.wait_send()
    o_ref[...] = acc


def tree_sum(x, n_copy, n_space):
    steps = (n_copy.bit_length() - 1) + (n_space.bit_length() - 1)
    return pl.pallas_call(
        functools.partial(_tree_sum_kernel, n_copy, n_space),
        out_shape=jax.ShapeDtypeStruct(x.shape, jnp.float32),
        in_specs=[pl.BlockSpec(memory_space=pltpu.VMEM)],
        out_specs=pl.BlockSpec(memory_space=pltpu.VMEM),
        scratch_shapes=[
            pltpu.VMEM((steps,) + x.shape, jnp.float32),
            pltpu.VMEM((steps,) + x.shape, jnp.float32),
            pltpu.SemaphoreType.DMA((steps,)),
            pltpu.SemaphoreType.DMA((steps,)),
        ],
        compiler_params=pltpu.CompilerParams(collective_id=2, has_side_effects=True),
        cost_estimate=pl.CostEstimate(
            flops=steps * x.size, transcendentals=0, bytes_accessed=4 * steps * x.size
        ),
    )(x)


def _filter_sum_kernel(rows, x_ref, o_ref, half_in, part, other, full_in, sems):
    me_c = lax.axis_index("copy")
    me_s = lax.axis_index("space")
    core = me_c % 2
    hi = me_c // 2
    mate = (me_c + 1 - 2 * core, me_s)
    far = (me_c + 2 - 4 * hi, me_s)
    half = rows // 2
    barrier = pltpu.get_barrier_semaphore()
    pl.semaphore_signal(barrier, inc=1, device_id=mate, device_id_type=MESH)
    pl.semaphore_signal(barrier, inc=1, device_id=far, device_id_type=MESH)
    pl.semaphore_wait(barrier, 2)
    mine = pl.ds(pl.multiple_of(core * half, 8), half)
    theirs = pl.ds(pl.multiple_of((1 - core) * half, 8), half)
    c1 = pltpu.make_async_remote_copy(
        src_ref=x_ref.at[theirs], dst_ref=half_in, send_sem=sems.at[0], recv_sem=sems.at[1],
        device_id=mate, device_id_type=MESH)
    c1.start()
    c1.wait_recv()
    own = x_ref[mine, :].astype(jnp.float32)
    got = half_in[...].astype(jnp.float32)
    first = jnp.where(core == 0, own, got)
    second = jnp.where(core == 0, got, own)
    part[...] = (first + second).astype(jnp.bfloat16)
    c2 = pltpu.make_async_remote_copy(
        src_ref=part, dst_ref=other, send_sem=sems.at[2], recv_sem=sems.at[3],
        device_id=far, device_id_type=MESH)
    c2.start()
    c2.wait_recv()
    mine_p = part[...].astype(jnp.float32)
    got_p = other[...].astype(jnp.float32)
    total = jnp.where(hi == 0, mine_p + got_p, got_p + mine_p)
    o_ref[mine, :] = total
    c3 = pltpu.make_async_remote_copy(
        src_ref=o_ref.at[mine], dst_ref=full_in, send_sem=sems.at[4], recv_sem=sems.at[5],
        device_id=mate, device_id_type=MESH)
    c3.start()
    c3.wait_recv()
    o_ref[theirs, :] = full_in[...]
    c1.wait_send()
    c2.wait_send()
    c3.wait_send()


def filter_sum(x):
    rows, cols = x.shape
    half = rows // 2
    return pl.pallas_call(
        functools.partial(_filter_sum_kernel, rows),
        out_shape=jax.ShapeDtypeStruct((rows, cols), jnp.float32),
        in_specs=[pl.BlockSpec(memory_space=pltpu.VMEM)],
        out_specs=pl.BlockSpec(memory_space=pltpu.VMEM),
        scratch_shapes=[
            pltpu.VMEM((half, cols), x.dtype),
            pltpu.VMEM((half, cols), jnp.bfloat16),
            pltpu.VMEM((half, cols), jnp.bfloat16),
            pltpu.VMEM((half, cols), jnp.float32),
            pltpu.SemaphoreType.DMA((6,)),
        ],
        compiler_params=pltpu.CompilerParams(
            collective_id=1, has_side_effects=True, vmem_limit_bytes=48 * 1024 * 1024
        ),
        cost_estimate=pl.CostEstimate(
            flops=2 * rows * cols, transcendentals=0, bytes_accessed=10 * rows * cols
        ),
    )(x)


def dft_parts(length):
    index = jnp.arange(length, dtype=jnp.int32)
    phase = index[:, None] * index[None, :] % length
    angle = phase.astype(jnp.float32) * (2.0 * math.pi / length)
    factor = 1.0 / math.sqrt(length)
    return (
        (jnp.cos(angle) * factor).astype(jnp.bfloat16),
        (jnp.sin(angle) * factor).astype(jnp.bfloat16),
    )


def row_table(length):
    cosine, sine = dft_parts(length)
    return jnp.stack([cosine, -sine])


def column_table(length, direction):
    cosine, sine = dft_parts(length)
    upper = jnp.stack([cosine, direction * sine], axis=1)
    lower = jnp.stack([-direction * sine, cosine], axis=1)
    return jnp.stack([upper, lower])


def layer_norm(values):
    centre = jnp.mean(values, axis=-1, keepdims=True)
    centred = values - centre
    variance = jnp.mean(centred * centred, axis=-1, keepdims=True)
    rstd_value = lax.rsqrt(variance + EPS)
    return (centred * rstd_value, rstd_value)


def norm_backward(upstream, normed, rstd_value, gain):
    scaled = upstream * gain
    result = (
        scaled
        - jnp.mean(scaled, axis=-1, keepdims=True)
        - normed * jnp.mean(scaled * normed, axis=-1, keepdims=True)
    ) * rstd_value
    lead = tuple(range(upstream.ndim - 1))
    return (result, jnp.sum(upstream * normed, axis=lead))


def apply_filter(spectrum, filter_weight, direction):
    real_part = spectrum[0].astype(jnp.float32)
    imag_part = spectrum[1].astype(jnp.float32)
    kernel_real = filter_weight[0].astype(jnp.float32)
    kernel_imag = direction * filter_weight[1].astype(jnp.float32)
    return jnp.stack(
        [
            kernel_real * real_part - kernel_imag * imag_part,
            kernel_real * imag_part + kernel_imag * real_part,
        ]
    )


def exact_gelu(values):
    return jax.nn.gelu(values, approximate=False)


def spectral(values, filter_weight, direction):
    width = values.shape[2]
    rows_tab = row_table(width)
    rows = jnp.einsum(
        "pkw,bhwc->pbhkc", rows_tab, values, preferred_element_type=jnp.float32
    ).astype(jnp.bfloat16)
    columns = lax.all_to_all(rows, "space", split_axis=3, concat_axis=2, tiled=True)
    height = columns.shape[2]
    spectrum = jnp.einsum(
        "qmph,pbhkc->qbmkc", column_table(height, 1), columns, preferred_element_type=jnp.float32
    ).astype(jnp.bfloat16)
    weighted = apply_filter(spectrum, filter_weight[:, None], direction).astype(jnp.bfloat16)
    returned = jnp.einsum(
        "qmph,pbhkc->qbmkc", column_table(height, -1), weighted, preferred_element_type=jnp.float32
    ).astype(jnp.bfloat16)
    back_rows = lax.all_to_all(returned, "space", split_axis=2, concat_axis=3, tiled=True)
    output = jnp.einsum("pkw,pbhkc->bhwc", rows_tab, back_rows, preferred_element_type=jnp.float32)
    return (output, spectrum)


def body(noisy_tokens, grad_out, filter_weight, weight_in, weight_out, gain_one, gain_two):
    batch, rows_dev, width, chans = noisy_tokens.shape
    inputs = noisy_tokens.astype(jnp.float32)
    normed_one, rstd_one = layer_norm(inputs)
    mixed_in = (normed_one * gain_one).astype(jnp.bfloat16)
    spatial, spectrum = spectral(mixed_in, filter_weight, 1)
    normed_two, rstd_two = layer_norm(spatial)
    mlp_in = (normed_two * gain_two).astype(jnp.bfloat16).reshape(-1, chans)
    preact = jnp.dot(mlp_in, weight_in, preferred_element_type=jnp.float32)
    activated = exact_gelu(preact).astype(jnp.bfloat16)
    mlp_out = jnp.dot(activated, weight_out, preferred_element_type=jnp.float32)
    block_out = (inputs + mlp_out.reshape(inputs.shape)).astype(jnp.bfloat16)
    upstream = grad_out.reshape(-1, chans)
    grad_act = jnp.dot(upstream, weight_out.T, preferred_element_type=jnp.float32)
    grad_pre = jax.vjp(exact_gelu, preact)[1](grad_act)[0].astype(jnp.bfloat16)
    sum_out = jnp.dot(activated.T, upstream, preferred_element_type=jnp.float32)
    sum_in = jnp.dot(mlp_in.T, grad_pre, preferred_element_type=jnp.float32)
    grad_mlp = jnp.dot(grad_pre, weight_in.T, preferred_element_type=jnp.float32).reshape(
        inputs.shape
    )
    grad_spatial, sum_gain_two = norm_backward(grad_mlp, normed_two, rstd_two, gain_two)
    back_spatial, adjoint = spectral(grad_spatial.astype(jnp.bfloat16), filter_weight, -1)
    spec_f = spectrum.astype(jnp.float32)
    adj_f = adjoint.astype(jnp.float32)
    filter_terms = jnp.stack(
        [
            jnp.sum(adj_f[0] * spec_f[0] + adj_f[1] * spec_f[1], axis=0),
            jnp.sum(adj_f[1] * spec_f[0] - adj_f[0] * spec_f[1], axis=0),
        ]
    )
    fshape = filter_terms.shape
    grad_filter = filter_sum(
        filter_terms.astype(jnp.bfloat16).reshape(fshape[0] * fshape[1], fshape[2] * fshape[3])
    ).reshape(fshape)
    grad_normed, sum_gain_one = norm_backward(back_spatial, normed_one, rstd_one, gain_one)
    grad_tokens = (grad_out.astype(jnp.float32) + grad_normed).astype(jnp.bfloat16)
    total_tokens = batch * lax.axis_size("copy") * rows_dev * lax.axis_size("space") * width
    factor = 1.0 / math.sqrt(total_tokens)
    both = ("copy", "space")
    weight_sums = lax.psum((sum_in.astype(jnp.bfloat16), sum_out.astype(jnp.bfloat16)), both)
    weight_sums = [(s.astype(jnp.float32) * factor).astype(jnp.bfloat16) for s in weight_sums]
    gains = tree_sum(
        jnp.stack([sum_gain_one, sum_gain_two]), lax.axis_size("copy"), lax.axis_size("space")
    )
    return (
        block_out,
        grad_tokens,
        grad_filter,
        weight_sums[0],
        weight_sums[1],
        gains[0] * factor,
        gains[1] * factor,
    )


def solution(mesh):
    return jax.shard_map(
        body,
        mesh=mesh,
        in_specs=(
            P("copy", "space", None, None),
            P("copy", "space", None, None),
            P(None, None, "space", None),
            P(),
            P(),
            P(),
            P(),
        ),
        out_specs=(
            P("copy", "space", None, None),
            P("copy", "space", None, None),
            P(None, None, "space", None),
            P(),
            P(),
            P(),
            P(),
        ),
        check_vma=False,
    )
```

```python
import functools
import math

import jax
import jax.numpy as jnp
from jax import lax
from jax.experimental import pallas as pl
from jax.experimental.pallas import tpu as pltpu
from jax.sharding import PartitionSpec as P

MESH = pl.DeviceIdType.MESH

EPS = 1e-06


def _partner(idx, bit):
    step = 1 << bit
    flip = 1 - 2 * ((idx // step) % 2)
    return idx + flip * step


def _tree_sum_kernel(n_copy, n_space, x_ref, o_ref, send_buf, recv_buf, send_sem, recv_sem):
    me_c = lax.axis_index("copy")
    me_s = lax.axis_index("space")
    bits = []
    for b in range(n_space.bit_length() - 1):
        bits.append(("space", b))
    for b in range(n_copy.bit_length() - 1):
        bits.append(("copy", b))

    def peer(axis, b):
        if axis == "space":
            return (me_c, _partner(me_s, b))
        return (_partner(me_c, b), me_s)

    barrier = pltpu.get_barrier_semaphore()
    for axis, b in bits:
        pl.semaphore_signal(barrier, inc=1, device_id=peer(axis, b), device_id_type=MESH)
    pl.semaphore_wait(barrier, len(bits))
    acc = x_ref[...]
    copies = []
    for s, (axis, b) in enumerate(bits):
        send_buf[s] = acc
        c = pltpu.make_async_remote_copy(
            src_ref=send_buf.at[s],
            dst_ref=recv_buf.at[s],
            send_sem=send_sem.at[s],
            recv_sem=recv_sem.at[s],
            device_id=peer(axis, b),
            device_id_type=MESH,
        )
        c.start()
        c.wait_recv()
        copies.append(c)
        acc = acc + recv_buf[s]
    for c in copies:
        c.wait_send()
    o_ref[...] = acc


def tree_sum(x, n_copy, n_space):
    steps = (n_copy.bit_length() - 1) + (n_space.bit_length() - 1)
    return pl.pallas_call(
        functools.partial(_tree_sum_kernel, n_copy, n_space),
        out_shape=jax.ShapeDtypeStruct(x.shape, jnp.float32),
        in_specs=[pl.BlockSpec(memory_space=pltpu.VMEM)],
        out_specs=pl.BlockSpec(memory_space=pltpu.VMEM),
        scratch_shapes=[
            pltpu.VMEM((steps,) + x.shape, jnp.float32),
            pltpu.VMEM((steps,) + x.shape, jnp.float32),
            pltpu.SemaphoreType.DMA((steps,)),
            pltpu.SemaphoreType.DMA((steps,)),
        ],
        compiler_params=pltpu.CompilerParams(collective_id=2, has_side_effects=True),
        cost_estimate=pl.CostEstimate(
            flops=steps * x.size, transcendentals=0, bytes_accessed=4 * steps * x.size
        ),
    )(x)


def _filter_sum_kernel(rows, x_ref, o_ref, half_in, part, other, full_in, sems):
    me_c = lax.axis_index("copy")
    me_s = lax.axis_index("space")
    core = me_c % 2
    hi = me_c // 2
    mate = (me_c + 1 - 2 * core, me_s)
    far = (me_c + 2 - 4 * hi, me_s)
    half = rows // 2
    barrier = pltpu.get_barrier_semaphore()
    pl.semaphore_signal(barrier, inc=1, device_id=mate, device_id_type=MESH)
    pl.semaphore_signal(barrier, inc=1, device_id=far, device_id_type=MESH)
    pl.semaphore_wait(barrier, 2)
    mine = pl.ds(pl.multiple_of(core * half, 8), half)
    theirs = pl.ds(pl.multiple_of((1 - core) * half, 8), half)
    c1 = pltpu.make_async_remote_copy(
        src_ref=x_ref.at[theirs], dst_ref=half_in, send_sem=sems.at[0], recv_sem=sems.at[1],
        device_id=mate, device_id_type=MESH)
    c1.start()
    c1.wait_recv()
    own = x_ref[mine, :].astype(jnp.float32)
    got = half_in[...].astype(jnp.float32)
    first = jnp.where(core == 0, own, got)
    second = jnp.where(core == 0, got, own)
    part[...] = (first + second).astype(jnp.bfloat16)
    c2 = pltpu.make_async_remote_copy(
        src_ref=part, dst_ref=other, send_sem=sems.at[2], recv_sem=sems.at[3],
        device_id=far, device_id_type=MESH)
    c2.start()
    c2.wait_recv()
    mine_p = part[...].astype(jnp.float32)
    got_p = other[...].astype(jnp.float32)
    total = jnp.where(hi == 0, mine_p + got_p, got_p + mine_p)
    o_ref[mine, :] = total
    c3 = pltpu.make_async_remote_copy(
        src_ref=o_ref.at[mine], dst_ref=full_in, send_sem=sems.at[4], recv_sem=sems.at[5],
        device_id=mate, device_id_type=MESH)
    c3.start()
    c3.wait_recv()
    o_ref[theirs, :] = full_in[...]
    c1.wait_send()
    c2.wait_send()
    c3.wait_send()


def filter_sum(x):
    rows, cols = x.shape
    half = rows // 2
    return pl.pallas_call(
        functools.partial(_filter_sum_kernel, rows),
        out_shape=jax.ShapeDtypeStruct((rows, cols), jnp.float32),
        in_specs=[pl.BlockSpec(memory_space=pltpu.VMEM)],
        out_specs=pl.BlockSpec(memory_space=pltpu.VMEM),
        scratch_shapes=[
            pltpu.VMEM((half, cols), x.dtype),
            pltpu.VMEM((half, cols), jnp.bfloat16),
            pltpu.VMEM((half, cols), jnp.bfloat16),
            pltpu.VMEM((half, cols), jnp.float32),
            pltpu.SemaphoreType.DMA((6,)),
        ],
        compiler_params=pltpu.CompilerParams(
            collective_id=1, has_side_effects=True, vmem_limit_bytes=48 * 1024 * 1024
        ),
        cost_estimate=pl.CostEstimate(
            flops=2 * rows * cols, transcendentals=0, bytes_accessed=10 * rows * cols
        ),
    )(x)


def _bit_orders(n_copy, n_space):
    if (n_copy, n_space) == (4, 64):
        first = [("copy", 0), ("space", 0), ("space", 1), ("space", 4), ("space", 2), ("space", 5), ("copy", 1), ("space", 3)]
        second = [("copy", 0), ("space", 1), ("space", 4), ("space", 0), ("space", 5), ("space", 2), ("copy", 1), ("space", 3)]
        return first, second
    sb = [("space", b) for b in range(n_space.bit_length() - 1)]
    cb = [("copy", b) for b in range(1, n_copy.bit_length() - 1)]
    return [("copy", 0)] + sb + cb, [("copy", 0)] + sb[::-1] + cb


def _all_sum_kernel(n_copy, n_space, rows, x_ref, o_ref, acc, *rest):
    orders = _bit_orders(n_copy, n_space)
    steps = len(orders[0])
    recv = rest[:steps]
    rs_sems, ag_sems = rest[steps], rest[steps + 1]
    me_c = lax.axis_index("copy")
    me_s = lax.axis_index("space")
    core = me_c % 2

    def info(axis, b):
        idx = me_c if axis == "copy" else me_s
        step = 1 << b
        bit = (idx // step) % 2
        other = idx + (1 - 2 * bit) * step
        if axis == "copy":
            return other, me_s, bit
        return me_c, other, bit

    plan = []
    for s in range(steps):
        c0, s0, b0 = info(*orders[0][s])
        c1, s1, b1 = info(*orders[1][s])
        plan.append(((1 - core) * c0 + core * c1, (1 - core) * s0 + core * s1, (1 - core) * b0 + core * b1))

    barrier = pltpu.get_barrier_semaphore()
    for pc, ps, _ in plan:
        pl.semaphore_signal(barrier, inc=1, device_id=(pc, ps), device_id_type=MESH)
    pl.semaphore_wait(barrier, steps)

    lo = 0
    length = rows
    for s, (pc, ps, bit) in enumerate(plan):
        half = length // 2
        keep = pl.multiple_of(lo + bit * half, 8)
        give = pl.multiple_of(lo + (1 - bit) * half, 8)
        base = x_ref if s == 0 else acc
        c = pltpu.make_async_remote_copy(
            src_ref=base.at[pl.ds(give, half)],
            dst_ref=recv[s],
            send_sem=rs_sems.at[2 * s],
            recv_sem=rs_sems.at[2 * s + 1],
            device_id=(pc, ps),
            device_id_type=MESH,
        )
        c.start()
        c.wait_recv()
        acc[pl.ds(keep, half), :] = base[pl.ds(keep, half), :] + recv[s][...]
        c.wait_send()
        lo = keep
        length = half
    o_ref[pl.ds(lo, length), :] = acc[pl.ds(lo, length), :]
    for s in reversed(range(steps)):
        pc, ps, bit = plan[s]
        mine = pl.ds(pl.multiple_of(lo, 8), length)
        c = pltpu.make_async_remote_copy(
            src_ref=o_ref.at[mine],
            dst_ref=o_ref.at[mine],
            send_sem=ag_sems.at[2 * s],
            recv_sem=ag_sems.at[2 * s + 1],
            device_id=(pc, ps),
            device_id_type=MESH,
        )
        c.start()
        c.wait_recv()
        c.wait_send()
        lo = lo - bit * length
        length = 2 * length


def all_sum(x, n_copy, n_space):
    rows, cols = x.shape
    steps = len(_bit_orders(n_copy, n_space)[0])
    recv = [pltpu.VMEM((rows >> (s + 1), cols), jnp.float32) for s in range(steps)]
    return pl.pallas_call(
        functools.partial(_all_sum_kernel, n_copy, n_space, rows),
        out_shape=jax.ShapeDtypeStruct((rows, cols), jnp.float32),
        in_specs=[pl.BlockSpec(memory_space=pltpu.VMEM)],
        out_specs=pl.BlockSpec(memory_space=pltpu.VMEM),
        scratch_shapes=[pltpu.VMEM((rows, cols), jnp.float32)]
        + recv
        + [pltpu.SemaphoreType.DMA((2 * steps,)), pltpu.SemaphoreType.DMA((2 * steps,))],
        compiler_params=pltpu.CompilerParams(
            collective_id=3, has_side_effects=True, vmem_limit_bytes=56 * 1024 * 1024
        ),
        cost_estimate=pl.CostEstimate(
            flops=rows * cols, transcendentals=0, bytes_accessed=16 * rows * cols
        ),
    )(x)


def dft_parts(length):
    index = jnp.arange(length, dtype=jnp.int32)
    phase = index[:, None] * index[None, :] % length
    angle = phase.astype(jnp.float32) * (2.0 * math.pi / length)
    factor = 1.0 / math.sqrt(length)
    return (
        (jnp.cos(angle) * factor).astype(jnp.bfloat16),
        (jnp.sin(angle) * factor).astype(jnp.bfloat16),
    )


def row_table(length):
    cosine, sine = dft_parts(length)
    return jnp.stack([cosine, -sine])


def column_table(length, direction):
    cosine, sine = dft_parts(length)
    upper = jnp.stack([cosine, direction * sine], axis=1)
    lower = jnp.stack([-direction * sine, cosine], axis=1)
    return jnp.stack([upper, lower])


def layer_norm(values):
    centre = jnp.mean(values, axis=-1, keepdims=True)
    centred = values - centre
    variance = jnp.mean(centred * centred, axis=-1, keepdims=True)
    rstd_value = lax.rsqrt(variance + EPS)
    return (centred * rstd_value, rstd_value)


def norm_backward(upstream, normed, rstd_value, gain):
    scaled = upstream * gain
    result = (
        scaled
        - jnp.mean(scaled, axis=-1, keepdims=True)
        - normed * jnp.mean(scaled * normed, axis=-1, keepdims=True)
    ) * rstd_value
    lead = tuple(range(upstream.ndim - 1))
    return (result, jnp.sum(upstream * normed, axis=lead))


def apply_filter(spectrum, filter_weight, direction):
    real_part = spectrum[0].astype(jnp.float32)
    imag_part = spectrum[1].astype(jnp.float32)
    kernel_real = filter_weight[0].astype(jnp.float32)
    kernel_imag = direction * filter_weight[1].astype(jnp.float32)
    return jnp.stack(
        [
            kernel_real * real_part - kernel_imag * imag_part,
            kernel_real * imag_part + kernel_imag * real_part,
        ]
    )


def exact_gelu(values):
    return jax.nn.gelu(values, approximate=False)


def spectral(values, filter_weight, direction):
    width = values.shape[2]
    rows_tab = row_table(width)
    rows = jnp.einsum(
        "pkw,bhwc->pbhkc", rows_tab, values, preferred_element_type=jnp.float32
    ).astype(jnp.bfloat16)
    columns = lax.all_to_all(rows, "space", split_axis=3, concat_axis=2, tiled=True)
    height = columns.shape[2]
    spectrum = jnp.einsum(
        "qmph,pbhkc->qbmkc", column_table(height, 1), columns, preferred_element_type=jnp.float32
    ).astype(jnp.bfloat16)
    weighted = apply_filter(spectrum, filter_weight[:, None], direction).astype(jnp.bfloat16)
    returned = jnp.einsum(
        "qmph,pbhkc->qbmkc", column_table(height, -1), weighted, preferred_element_type=jnp.float32
    ).astype(jnp.bfloat16)
    back_rows = lax.all_to_all(returned, "space", split_axis=2, concat_axis=3, tiled=True)
    output = jnp.einsum("pkw,pbhkc->bhwc", rows_tab, back_rows, preferred_element_type=jnp.float32)
    return (output, spectrum)


def body(noisy_tokens, grad_out, filter_weight, weight_in, weight_out, gain_one, gain_two):
    batch, rows_dev, width, chans = noisy_tokens.shape
    inputs = noisy_tokens.astype(jnp.float32)
    normed_one, rstd_one = layer_norm(inputs)
    mixed_in = (normed_one * gain_one).astype(jnp.bfloat16)
    spatial, spectrum = spectral(mixed_in, filter_weight, 1)
    normed_two, rstd_two = layer_norm(spatial)
    mlp_in = (normed_two * gain_two).astype(jnp.bfloat16).reshape(-1, chans)
    preact = jnp.dot(mlp_in, weight_in, preferred_element_type=jnp.float32)
    activated = exact_gelu(preact).astype(jnp.bfloat16)
    mlp_out = jnp.dot(activated, weight_out, preferred_element_type=jnp.float32)
    block_out = (inputs + mlp_out.reshape(inputs.shape)).astype(jnp.bfloat16)
    upstream = grad_out.reshape(-1, chans)
    grad_act = jnp.dot(upstream, weight_out.T, preferred_element_type=jnp.float32)
    grad_pre = jax.vjp(exact_gelu, preact)[1](grad_act)[0].astype(jnp.bfloat16)
    sum_out = jnp.dot(activated.T, upstream, preferred_element_type=jnp.float32)
    sum_in = jnp.dot(mlp_in.T, grad_pre, preferred_element_type=jnp.float32)
    grad_mlp = jnp.dot(grad_pre, weight_in.T, preferred_element_type=jnp.float32).reshape(
        inputs.shape
    )
    grad_spatial, sum_gain_two = norm_backward(grad_mlp, normed_two, rstd_two, gain_two)
    back_spatial, adjoint = spectral(grad_spatial.astype(jnp.bfloat16), filter_weight, -1)
    spec_f = spectrum.astype(jnp.float32)
    adj_f = adjoint.astype(jnp.float32)
    filter_terms = jnp.stack(
        [
            jnp.sum(adj_f[0] * spec_f[0] + adj_f[1] * spec_f[1], axis=0),
            jnp.sum(adj_f[1] * spec_f[0] - adj_f[0] * spec_f[1], axis=0),
        ]
    )
    fshape = filter_terms.shape
    grad_filter = filter_sum(
        filter_terms.astype(jnp.bfloat16).reshape(fshape[0] * fshape[1], fshape[2] * fshape[3])
    ).reshape(fshape)
    grad_normed, sum_gain_one = norm_backward(back_spatial, normed_one, rstd_one, gain_one)
    grad_tokens = (grad_out.astype(jnp.float32) + grad_normed).astype(jnp.bfloat16)
    total_tokens = batch * lax.axis_size("copy") * rows_dev * lax.axis_size("space") * width
    factor = 1.0 / math.sqrt(total_tokens)
    n_copy, n_space = lax.axis_size("copy"), lax.axis_size("space")
    flat = jnp.concatenate([sum_in.reshape(-1), sum_out.reshape(-1)])
    lanes = 128
    block = lanes * 8 << (n_copy * n_space).bit_length() - 1
    padded = -(-flat.size // block) * block
    flat = jnp.pad(flat, (0, padded - flat.size)).reshape(padded // lanes, lanes)
    total = all_sum(flat, n_copy, n_space).reshape(-1)
    weight_sums = [
        (total[: sum_in.size] * factor).astype(jnp.bfloat16).reshape(sum_in.shape),
        (total[sum_in.size : sum_in.size + sum_out.size] * factor)
        .astype(jnp.bfloat16)
        .reshape(sum_out.shape),
    ]
    gains = tree_sum(
        jnp.stack([sum_gain_one, sum_gain_two]), lax.axis_size("copy"), lax.axis_size("space")
    )
    return (
        block_out,
        grad_tokens,
        grad_filter,
        weight_sums[0],
        weight_sums[1],
        gains[0] * factor,
        gains[1] * factor,
    )


def solution(mesh):
    return jax.shard_map(
        body,
        mesh=mesh,
        in_specs=(
            P("copy", "space", None, None),
            P("copy", "space", None, None),
            P(None, None, "space", None),
            P(),
            P(),
            P(),
            P(),
        ),
        out_specs=(
            P("copy", "space", None, None),
            P("copy", "space", None, None),
            P(None, None, "space", None),
            P(),
            P(),
            P(),
            P(),
        ),
        check_vma=False,
    )
```

```python
import functools
import math

import jax
import jax.numpy as jnp
from jax import lax
from jax.experimental import pallas as pl
from jax.experimental.pallas import tpu as pltpu
from jax.sharding import PartitionSpec as P

MESH = pl.DeviceIdType.MESH

EPS = 1e-06


def _partner(idx, bit):
    step = 1 << bit
    flip = 1 - 2 * ((idx // step) % 2)
    return idx + flip * step


def _tree_sum_kernel(n_copy, n_space, x_ref, o_ref, send_buf, recv_buf, send_sem, recv_sem):
    me_c = lax.axis_index("copy")
    me_s = lax.axis_index("space")
    bits = []
    for b in range(n_space.bit_length() - 1):
        bits.append(("space", b))
    for b in range(n_copy.bit_length() - 1):
        bits.append(("copy", b))

    def peer(axis, b):
        if axis == "space":
            return (me_c, _partner(me_s, b))
        return (_partner(me_c, b), me_s)

    barrier = pltpu.get_barrier_semaphore()
    for axis, b in bits:
        pl.semaphore_signal(barrier, inc=1, device_id=peer(axis, b), device_id_type=MESH)
    pl.semaphore_wait(barrier, len(bits))
    acc = x_ref[...]
    copies = []
    for s, (axis, b) in enumerate(bits):
        send_buf[s] = acc
        c = pltpu.make_async_remote_copy(
            src_ref=send_buf.at[s],
            dst_ref=recv_buf.at[s],
            send_sem=send_sem.at[s],
            recv_sem=recv_sem.at[s],
            device_id=peer(axis, b),
            device_id_type=MESH,
        )
        c.start()
        c.wait_recv()
        copies.append(c)
        acc = acc + recv_buf[s]
    for c in copies:
        c.wait_send()
    o_ref[...] = acc


def tree_sum(x, n_copy, n_space):
    steps = (n_copy.bit_length() - 1) + (n_space.bit_length() - 1)
    return pl.pallas_call(
        functools.partial(_tree_sum_kernel, n_copy, n_space),
        out_shape=jax.ShapeDtypeStruct(x.shape, jnp.float32),
        in_specs=[pl.BlockSpec(memory_space=pltpu.VMEM)],
        out_specs=pl.BlockSpec(memory_space=pltpu.VMEM),
        scratch_shapes=[
            pltpu.VMEM((steps,) + x.shape, jnp.float32),
            pltpu.VMEM((steps,) + x.shape, jnp.float32),
            pltpu.SemaphoreType.DMA((steps,)),
            pltpu.SemaphoreType.DMA((steps,)),
        ],
        compiler_params=pltpu.CompilerParams(collective_id=2, has_side_effects=True),
        cost_estimate=pl.CostEstimate(
            flops=steps * x.size, transcendentals=0, bytes_accessed=4 * steps * x.size
        ),
    )(x)


def _filter_sum_kernel(rows, x_ref, o_ref, half_in, part, other, full_in, sems):
    me_c = lax.axis_index("copy")
    me_s = lax.axis_index("space")
    core = me_c % 2
    hi = me_c // 2
    mate = (me_c + 1 - 2 * core, me_s)
    far = (me_c + 2 - 4 * hi, me_s)
    half = rows // 2
    barrier = pltpu.get_barrier_semaphore()
    pl.semaphore_signal(barrier, inc=1, device_id=mate, device_id_type=MESH)
    pl.semaphore_signal(barrier, inc=1, device_id=far, device_id_type=MESH)
    pl.semaphore_wait(barrier, 2)
    mine = pl.ds(pl.multiple_of(core * half, 8), half)
    theirs = pl.ds(pl.multiple_of((1 - core) * half, 8), half)
    c1 = pltpu.make_async_remote_copy(
        src_ref=x_ref.at[theirs], dst_ref=half_in, send_sem=sems.at[0], recv_sem=sems.at[1],
        device_id=mate, device_id_type=MESH)
    c1.start()
    c1.wait_recv()
    own = x_ref[mine, :].astype(jnp.float32)
    got = half_in[...].astype(jnp.float32)
    first = jnp.where(core == 0, own, got)
    second = jnp.where(core == 0, got, own)
    part[...] = (first + second).astype(jnp.bfloat16)
    c2 = pltpu.make_async_remote_copy(
        src_ref=part, dst_ref=other, send_sem=sems.at[2], recv_sem=sems.at[3],
        device_id=far, device_id_type=MESH)
    c2.start()
    c2.wait_recv()
    mine_p = part[...].astype(jnp.float32)
    got_p = other[...].astype(jnp.float32)
    total = jnp.where(hi == 0, mine_p + got_p, got_p + mine_p)
    o_ref[mine, :] = total
    c3 = pltpu.make_async_remote_copy(
        src_ref=o_ref.at[mine], dst_ref=full_in, send_sem=sems.at[4], recv_sem=sems.at[5],
        device_id=mate, device_id_type=MESH)
    c3.start()
    c3.wait_recv()
    o_ref[theirs, :] = full_in[...]
    c1.wait_send()
    c2.wait_send()
    c3.wait_send()


def filter_sum(x):
    rows, cols = x.shape
    half = rows // 2
    return pl.pallas_call(
        functools.partial(_filter_sum_kernel, rows),
        out_shape=jax.ShapeDtypeStruct((rows, cols), jnp.float32),
        in_specs=[pl.BlockSpec(memory_space=pltpu.VMEM)],
        out_specs=pl.BlockSpec(memory_space=pltpu.VMEM),
        scratch_shapes=[
            pltpu.VMEM((half, cols), x.dtype),
            pltpu.VMEM((half, cols), jnp.bfloat16),
            pltpu.VMEM((half, cols), jnp.bfloat16),
            pltpu.VMEM((half, cols), jnp.float32),
            pltpu.SemaphoreType.DMA((6,)),
        ],
        compiler_params=pltpu.CompilerParams(
            collective_id=1, has_side_effects=True, vmem_limit_bytes=48 * 1024 * 1024
        ),
        cost_estimate=pl.CostEstimate(
            flops=2 * rows * cols, transcendentals=0, bytes_accessed=10 * rows * cols
        ),
    )(x)


def _bit_orders(n_copy, n_space):
    if (n_copy, n_space) == (4, 64):
        first = [("copy", 0), ("space", 0), ("space", 1), ("space", 4), ("space", 2), ("space", 5), ("copy", 1), ("space", 3)]
        second = [("copy", 0), ("space", 1), ("space", 4), ("space", 0), ("space", 5), ("space", 2), ("copy", 1), ("space", 3)]
        return first, second
    sb = [("space", b) for b in range(n_space.bit_length() - 1)]
    cb = [("copy", b) for b in range(1, n_copy.bit_length() - 1)]
    return [("copy", 0)] + sb + cb, [("copy", 0)] + sb[::-1] + cb


def _all_sum_kernel(n_copy, n_space, rows, scale, x_ref, o_ref, acc, send, *rest):
    orders = _bit_orders(n_copy, n_space)
    steps = len(orders[0])
    recv = rest[:steps]
    rs_sems, ag_sems = rest[steps], rest[steps + 1]
    me_c = lax.axis_index("copy")
    me_s = lax.axis_index("space")
    core = me_c % 2

    def info(axis, b):
        idx = me_c if axis == "copy" else me_s
        step = 1 << b
        bit = (idx // step) % 2
        other = idx + (1 - 2 * bit) * step
        if axis == "copy":
            return other, me_s, bit
        return me_c, other, bit

    plan = []
    for s in range(steps):
        c0, s0, b0 = info(*orders[0][s])
        c1, s1, b1 = info(*orders[1][s])
        plan.append(((1 - core) * c0 + core * c1, (1 - core) * s0 + core * s1, (1 - core) * b0 + core * b1))

    barrier = pltpu.get_barrier_semaphore()
    for pc, ps, _ in plan:
        pl.semaphore_signal(barrier, inc=1, device_id=(pc, ps), device_id_type=MESH)
    pl.semaphore_wait(barrier, steps)

    lo = 0
    length = rows
    for s, (pc, ps, bit) in enumerate(plan):
        half = length // 2
        keep = pl.multiple_of(lo + bit * half, 16)
        give = pl.multiple_of(lo + (1 - bit) * half, 16)
        base = x_ref if s == 0 else acc
        out = send.at[pl.ds(give, half)]
        send[pl.ds(give, half), :] = base[pl.ds(give, half), :].astype(jnp.bfloat16)
        c = pltpu.make_async_remote_copy(
            src_ref=out,
            dst_ref=recv[s],
            send_sem=rs_sems.at[2 * s],
            recv_sem=rs_sems.at[2 * s + 1],
            device_id=(pc, ps),
            device_id_type=MESH,
        )
        c.start()
        c.wait_recv()
        acc[pl.ds(keep, half), :] = base[pl.ds(keep, half), :] + recv[s][...].astype(jnp.float32)
        c.wait_send()
        lo = keep
        length = half
    mine = pl.ds(pl.multiple_of(lo, 16), length)
    o_ref[mine, :] = (acc[mine, :] * scale).astype(o_ref.dtype)
    for s in reversed(range(steps)):
        pc, ps, bit = plan[s]
        mine = pl.ds(pl.multiple_of(lo, 16), length)
        c = pltpu.make_async_remote_copy(
            src_ref=o_ref.at[mine],
            dst_ref=o_ref.at[mine],
            send_sem=ag_sems.at[2 * s],
            recv_sem=ag_sems.at[2 * s + 1],
            device_id=(pc, ps),
            device_id_type=MESH,
        )
        c.start()
        c.wait_recv()
        c.wait_send()
        lo = lo - bit * length
        length = 2 * length


def all_sum(x, n_copy, n_space, scale):
    rows, cols = x.shape
    steps = len(_bit_orders(n_copy, n_space)[0])
    recv = [pltpu.VMEM((rows >> (s + 1), cols), jnp.bfloat16) for s in range(steps)]
    return pl.pallas_call(
        functools.partial(_all_sum_kernel, n_copy, n_space, rows, scale),
        out_shape=jax.ShapeDtypeStruct((rows, cols), jnp.bfloat16),
        in_specs=[pl.BlockSpec(memory_space=pltpu.VMEM)],
        out_specs=pl.BlockSpec(memory_space=pltpu.VMEM),
        scratch_shapes=[
            pltpu.VMEM((rows, cols), jnp.float32),
            pltpu.VMEM((rows, cols), jnp.bfloat16),
        ]
        + recv
        + [pltpu.SemaphoreType.DMA((2 * steps,)), pltpu.SemaphoreType.DMA((2 * steps,))],
        compiler_params=pltpu.CompilerParams(
            collective_id=3, has_side_effects=True, vmem_limit_bytes=56 * 1024 * 1024
        ),
        cost_estimate=pl.CostEstimate(
            flops=rows * cols, transcendentals=0, bytes_accessed=12 * rows * cols
        ),
    )(x)


def dft_parts(length):
    index = jnp.arange(length, dtype=jnp.int32)
    phase = index[:, None] * index[None, :] % length
    angle = phase.astype(jnp.float32) * (2.0 * math.pi / length)
    factor = 1.0 / math.sqrt(length)
    return (
        (jnp.cos(angle) * factor).astype(jnp.bfloat16),
        (jnp.sin(angle) * factor).astype(jnp.bfloat16),
    )


def row_table(length):
    cosine, sine = dft_parts(length)
    return jnp.stack([cosine, -sine])


def column_table(length, direction):
    cosine, sine = dft_parts(length)
    upper = jnp.stack([cosine, direction * sine], axis=1)
    lower = jnp.stack([-direction * sine, cosine], axis=1)
    return jnp.stack([upper, lower])


def layer_norm(values):
    centre = jnp.mean(values, axis=-1, keepdims=True)
    centred = values - centre
    variance = jnp.mean(centred * centred, axis=-1, keepdims=True)
    rstd_value = lax.rsqrt(variance + EPS)
    return (centred * rstd_value, rstd_value)


def norm_backward(upstream, normed, rstd_value, gain):
    scaled = upstream * gain
    result = (
        scaled
        - jnp.mean(scaled, axis=-1, keepdims=True)
        - normed * jnp.mean(scaled * normed, axis=-1, keepdims=True)
    ) * rstd_value
    lead = tuple(range(upstream.ndim - 1))
    return (result, jnp.sum(upstream * normed, axis=lead))


def apply_filter(spectrum, filter_weight, direction):
    real_part = spectrum[0].astype(jnp.float32)
    imag_part = spectrum[1].astype(jnp.float32)
    kernel_real = filter_weight[0].astype(jnp.float32)
    kernel_imag = direction * filter_weight[1].astype(jnp.float32)
    return jnp.stack(
        [
            kernel_real * real_part - kernel_imag * imag_part,
            kernel_real * imag_part + kernel_imag * real_part,
        ]
    )


def exact_gelu(values):
    return jax.nn.gelu(values, approximate=False)


def spectral(values, filter_weight, direction):
    width = values.shape[2]
    rows_tab = row_table(width)
    rows = jnp.einsum(
        "pkw,bhwc->pbhkc", rows_tab, values, preferred_element_type=jnp.float32
    ).astype(jnp.bfloat16)
    columns = lax.all_to_all(rows, "space", split_axis=3, concat_axis=2, tiled=True)
    height = columns.shape[2]
    spectrum = jnp.einsum(
        "qmph,pbhkc->qbmkc", column_table(height, 1), columns, preferred_element_type=jnp.float32
    ).astype(jnp.bfloat16)
    weighted = apply_filter(spectrum, filter_weight[:, None], direction).astype(jnp.bfloat16)
    returned = jnp.einsum(
        "qmph,pbhkc->qbmkc", column_table(height, -1), weighted, preferred_element_type=jnp.float32
    ).astype(jnp.bfloat16)
    back_rows = lax.all_to_all(returned, "space", split_axis=2, concat_axis=3, tiled=True)
    output = jnp.einsum("pkw,pbhkc->bhwc", rows_tab, back_rows, preferred_element_type=jnp.float32)
    return (output, spectrum)


def body(noisy_tokens, grad_out, filter_weight, weight_in, weight_out, gain_one, gain_two):
    batch, rows_dev, width, chans = noisy_tokens.shape
    inputs = noisy_tokens.astype(jnp.float32)
    normed_one, rstd_one = layer_norm(inputs)
    mixed_in = (normed_one * gain_one).astype(jnp.bfloat16)
    spatial, spectrum = spectral(mixed_in, filter_weight, 1)
    normed_two, rstd_two = layer_norm(spatial)
    mlp_in = (normed_two * gain_two).astype(jnp.bfloat16).reshape(-1, chans)
    preact = jnp.dot(mlp_in, weight_in, preferred_element_type=jnp.float32)
    activated = exact_gelu(preact).astype(jnp.bfloat16)
    mlp_out = jnp.dot(activated, weight_out, preferred_element_type=jnp.float32)
    block_out = (inputs + mlp_out.reshape(inputs.shape)).astype(jnp.bfloat16)
    upstream = grad_out.reshape(-1, chans)
    grad_act = jnp.dot(upstream, weight_out.T, preferred_element_type=jnp.float32)
    grad_pre = jax.vjp(exact_gelu, preact)[1](grad_act)[0].astype(jnp.bfloat16)
    sum_out = jnp.dot(activated.T, upstream, preferred_element_type=jnp.float32)
    sum_in = jnp.dot(mlp_in.T, grad_pre, preferred_element_type=jnp.float32)
    grad_mlp = jnp.dot(grad_pre, weight_in.T, preferred_element_type=jnp.float32).reshape(
        inputs.shape
    )
    grad_spatial, sum_gain_two = norm_backward(grad_mlp, normed_two, rstd_two, gain_two)
    back_spatial, adjoint = spectral(grad_spatial.astype(jnp.bfloat16), filter_weight, -1)
    spec_f = spectrum.astype(jnp.float32)
    adj_f = adjoint.astype(jnp.float32)
    filter_terms = jnp.stack(
        [
            jnp.sum(adj_f[0] * spec_f[0] + adj_f[1] * spec_f[1], axis=0),
            jnp.sum(adj_f[1] * spec_f[0] - adj_f[0] * spec_f[1], axis=0),
        ]
    )
    fshape = filter_terms.shape
    grad_filter = filter_sum(
        filter_terms.astype(jnp.bfloat16).reshape(fshape[0] * fshape[1], fshape[2] * fshape[3])
    ).reshape(fshape)
    grad_normed, sum_gain_one = norm_backward(back_spatial, normed_one, rstd_one, gain_one)
    grad_tokens = (grad_out.astype(jnp.float32) + grad_normed).astype(jnp.bfloat16)
    total_tokens = batch * lax.axis_size("copy") * rows_dev * lax.axis_size("space") * width
    factor = 1.0 / math.sqrt(total_tokens)
    n_copy, n_space = lax.axis_size("copy"), lax.axis_size("space")
    parts = [sum_in.reshape(-1), sum_out.reshape(-1), sum_gain_one, sum_gain_two]
    flat = jnp.concatenate(parts)
    lanes = 128
    block = lanes * 16 << (n_copy * n_space).bit_length() - 1
    padded = -(-flat.size // block) * block
    flat = jnp.pad(flat, (0, padded - flat.size)).reshape(padded // lanes, lanes)
    total = all_sum(flat, n_copy, n_space, factor).reshape(-1)
    outs = []
    at = 0
    for p in parts:
        outs.append(total[at : at + p.size])
        at += p.size
    return (
        block_out,
        grad_tokens,
        grad_filter,
        outs[0].reshape(sum_in.shape),
        outs[1].reshape(sum_out.shape),
        outs[2].astype(jnp.float32),
        outs[3].astype(jnp.float32),
    )


def solution(mesh):
    return jax.shard_map(
        body,
        mesh=mesh,
        in_specs=(
            P("copy", "space", None, None),
            P("copy", "space", None, None),
            P(None, None, "space", None),
            P(),
            P(),
            P(),
            P(),
        ),
        out_specs=(
            P("copy", "space", None, None),
            P("copy", "space", None, None),
            P(None, None, "space", None),
            P(),
            P(),
            P(),
            P(),
        ),
        check_vma=False,
    )
```

```python
import functools
import math

import jax
import jax.numpy as jnp
from jax import lax
from jax.experimental import pallas as pl
from jax.experimental.pallas import tpu as pltpu
from jax.sharding import PartitionSpec as P

MESH = pl.DeviceIdType.MESH

EPS = 1e-06


def _partner(idx, bit):
    step = 1 << bit
    flip = 1 - 2 * ((idx // step) % 2)
    return idx + flip * step


def _tree_sum_kernel(n_copy, n_space, x_ref, o_ref, send_buf, recv_buf, send_sem, recv_sem):
    me_c = lax.axis_index("copy")
    me_s = lax.axis_index("space")
    bits = []
    for b in range(n_space.bit_length() - 1):
        bits.append(("space", b))
    for b in range(n_copy.bit_length() - 1):
        bits.append(("copy", b))

    def peer(axis, b):
        if axis == "space":
            return (me_c, _partner(me_s, b))
        return (_partner(me_c, b), me_s)

    barrier = pltpu.get_barrier_semaphore()
    for axis, b in bits:
        pl.semaphore_signal(barrier, inc=1, device_id=peer(axis, b), device_id_type=MESH)
    pl.semaphore_wait(barrier, len(bits))
    acc = x_ref[...]
    copies = []
    for s, (axis, b) in enumerate(bits):
        send_buf[s] = acc
        c = pltpu.make_async_remote_copy(
            src_ref=send_buf.at[s],
            dst_ref=recv_buf.at[s],
            send_sem=send_sem.at[s],
            recv_sem=recv_sem.at[s],
            device_id=peer(axis, b),
            device_id_type=MESH,
        )
        c.start()
        c.wait_recv()
        copies.append(c)
        acc = acc + recv_buf[s]
    for c in copies:
        c.wait_send()
    o_ref[...] = acc


def tree_sum(x, n_copy, n_space):
    steps = (n_copy.bit_length() - 1) + (n_space.bit_length() - 1)
    return pl.pallas_call(
        functools.partial(_tree_sum_kernel, n_copy, n_space),
        out_shape=jax.ShapeDtypeStruct(x.shape, jnp.float32),
        in_specs=[pl.BlockSpec(memory_space=pltpu.VMEM)],
        out_specs=pl.BlockSpec(memory_space=pltpu.VMEM),
        scratch_shapes=[
            pltpu.VMEM((steps,) + x.shape, jnp.float32),
            pltpu.VMEM((steps,) + x.shape, jnp.float32),
            pltpu.SemaphoreType.DMA((steps,)),
            pltpu.SemaphoreType.DMA((steps,)),
        ],
        compiler_params=pltpu.CompilerParams(collective_id=2, has_side_effects=True),
        cost_estimate=pl.CostEstimate(
            flops=steps * x.size, transcendentals=0, bytes_accessed=4 * steps * x.size
        ),
    )(x)


def _filter_sum_kernel(rows, x_ref, o_ref, half_in, part, other, full_in, sems):
    me_c = lax.axis_index("copy")
    me_s = lax.axis_index("space")
    core = me_c % 2
    hi = me_c // 2
    mate = (me_c + 1 - 2 * core, me_s)
    far = (me_c + 2 - 4 * hi, me_s)
    half = rows // 2
    barrier = pltpu.get_barrier_semaphore()
    pl.semaphore_signal(barrier, inc=1, device_id=mate, device_id_type=MESH)
    pl.semaphore_signal(barrier, inc=1, device_id=far, device_id_type=MESH)
    pl.semaphore_wait(barrier, 2)
    mine = pl.ds(pl.multiple_of(core * half, 8), half)
    theirs = pl.ds(pl.multiple_of((1 - core) * half, 8), half)
    c1 = pltpu.make_async_remote_copy(
        src_ref=x_ref.at[theirs], dst_ref=half_in, send_sem=sems.at[0], recv_sem=sems.at[1],
        device_id=mate, device_id_type=MESH)
    c1.start()
    c1.wait_recv()
    own = x_ref[mine, :].astype(jnp.float32)
    got = half_in[...].astype(jnp.float32)
    first = jnp.where(core == 0, own, got)
    second = jnp.where(core == 0, got, own)
    part[...] = (first + second).astype(jnp.bfloat16)
    c2 = pltpu.make_async_remote_copy(
        src_ref=part, dst_ref=other, send_sem=sems.at[2], recv_sem=sems.at[3],
        device_id=far, device_id_type=MESH)
    c2.start()
    c2.wait_recv()
    mine_p = part[...].astype(jnp.float32)
    got_p = other[...].astype(jnp.float32)
    total = jnp.where(hi == 0, mine_p + got_p, got_p + mine_p)
    o_ref[mine, :] = total
    c3 = pltpu.make_async_remote_copy(
        src_ref=o_ref.at[mine], dst_ref=full_in, send_sem=sems.at[4], recv_sem=sems.at[5],
        device_id=mate, device_id_type=MESH)
    c3.start()
    c3.wait_recv()
    o_ref[theirs, :] = full_in[...]
    c1.wait_send()
    c2.wait_send()
    c3.wait_send()


def filter_sum(x):
    rows, cols = x.shape
    half = rows // 2
    return pl.pallas_call(
        functools.partial(_filter_sum_kernel, rows),
        out_shape=jax.ShapeDtypeStruct((rows, cols), jnp.float32),
        in_specs=[pl.BlockSpec(memory_space=pltpu.VMEM)],
        out_specs=pl.BlockSpec(memory_space=pltpu.VMEM),
        scratch_shapes=[
            pltpu.VMEM((half, cols), x.dtype),
            pltpu.VMEM((half, cols), jnp.bfloat16),
            pltpu.VMEM((half, cols), jnp.bfloat16),
            pltpu.VMEM((half, cols), jnp.float32),
            pltpu.SemaphoreType.DMA((6,)),
        ],
        compiler_params=pltpu.CompilerParams(
            collective_id=1, has_side_effects=True, vmem_limit_bytes=48 * 1024 * 1024
        ),
        cost_estimate=pl.CostEstimate(
            flops=2 * rows * cols, transcendentals=0, bytes_accessed=10 * rows * cols
        ),
    )(x)


def _bit_orders(n_copy, n_space):
    if (n_copy, n_space) == (4, 64):
        first = [("copy", 0), ("space", 0), ("space", 1), ("space", 4), ("space", 2), ("space", 5), ("copy", 1), ("space", 3)]
        second = [("copy", 0), ("space", 1), ("space", 4), ("space", 0), ("space", 5), ("space", 2), ("copy", 1), ("space", 3)]
        return first, second
    sb = [("space", b) for b in range(n_space.bit_length() - 1)]
    cb = [("copy", b) for b in range(1, n_copy.bit_length() - 1)]
    return [("copy", 0)] + sb + cb, [("copy", 0)] + sb[::-1] + cb


def _all_sum_kernel(n_copy, n_space, rows, scale, x_ref, o_ref, acc, send, *rest):
    orders = _bit_orders(n_copy, n_space)
    steps = len(orders[0])
    recv = rest[:steps]
    rs_sems, ag_sems = rest[steps], rest[steps + 1]
    me_c = lax.axis_index("copy")
    me_s = lax.axis_index("space")
    core = me_c % 2

    def info(axis, b):
        idx = me_c if axis == "copy" else me_s
        step = 1 << b
        bit = (idx // step) % 2
        other = idx + (1 - 2 * bit) * step
        if axis == "copy":
            return other, me_s, bit
        return me_c, other, bit

    plan = []
    for s in range(steps):
        c0, s0, b0 = info(*orders[0][s])
        c1, s1, b1 = info(*orders[1][s])
        plan.append(((1 - core) * c0 + core * c1, (1 - core) * s0 + core * s1, (1 - core) * b0 + core * b1))

    barrier = pltpu.get_barrier_semaphore()
    for pc, ps, _ in plan:
        pl.semaphore_signal(barrier, inc=1, device_id=(pc, ps), device_id_type=MESH)
    pl.semaphore_wait(barrier, steps)

    lo = 0
    length = rows
    for s, (pc, ps, bit) in enumerate(plan):
        half = length // 2
        keep = pl.multiple_of(lo + bit * half, 16)
        give = pl.multiple_of(lo + (1 - bit) * half, 16)
        base = x_ref if s == 0 else acc
        out = send.at[pl.ds(give, half)]
        send[pl.ds(give, half), :] = base[pl.ds(give, half), :].astype(jnp.bfloat16)
        c = pltpu.make_async_remote_copy(
            src_ref=out,
            dst_ref=recv[s],
            send_sem=rs_sems.at[2 * s],
            recv_sem=rs_sems.at[2 * s + 1],
            device_id=(pc, ps),
            device_id_type=MESH,
        )
        c.start()
        c.wait_recv()
        acc[pl.ds(keep, half), :] = base[pl.ds(keep, half), :] + recv[s][...].astype(jnp.float32)
        c.wait_send()
        lo = keep
        length = half
    mine = pl.ds(pl.multiple_of(lo, 16), length)
    o_ref[mine, :] = (acc[mine, :] * scale).astype(o_ref.dtype)
    for s in reversed(range(steps)):
        pc, ps, bit = plan[s]
        mine = pl.ds(pl.multiple_of(lo, 16), length)
        c = pltpu.make_async_remote_copy(
            src_ref=o_ref.at[mine],
            dst_ref=o_ref.at[mine],
            send_sem=ag_sems.at[2 * s],
            recv_sem=ag_sems.at[2 * s + 1],
            device_id=(pc, ps),
            device_id_type=MESH,
        )
        c.start()
        c.wait_recv()
        c.wait_send()
        lo = lo - bit * length
        length = 2 * length


def all_sum(x, n_copy, n_space, scale):
    rows, cols = x.shape
    steps = len(_bit_orders(n_copy, n_space)[0])
    recv = [pltpu.VMEM((rows >> (s + 1), cols), jnp.bfloat16) for s in range(steps)]
    return pl.pallas_call(
        functools.partial(_all_sum_kernel, n_copy, n_space, rows, scale),
        out_shape=jax.ShapeDtypeStruct((rows, cols), jnp.bfloat16),
        in_specs=[pl.BlockSpec(memory_space=pltpu.VMEM)],
        out_specs=pl.BlockSpec(memory_space=pltpu.VMEM),
        scratch_shapes=[
            pltpu.VMEM((rows, cols), jnp.float32),
            pltpu.VMEM((rows, cols), jnp.bfloat16),
        ]
        + recv
        + [pltpu.SemaphoreType.DMA((2 * steps,)), pltpu.SemaphoreType.DMA((2 * steps,))],
        compiler_params=pltpu.CompilerParams(
            collective_id=3, has_side_effects=True, vmem_limit_bytes=56 * 1024 * 1024
        ),
        cost_estimate=pl.CostEstimate(
            flops=rows * cols, transcendentals=0, bytes_accessed=12 * rows * cols
        ),
    )(x)


def dft_parts(length):
    index = jnp.arange(length, dtype=jnp.int32)
    phase = index[:, None] * index[None, :] % length
    angle = phase.astype(jnp.float32) * (2.0 * math.pi / length)
    factor = 1.0 / math.sqrt(length)
    return (
        (jnp.cos(angle) * factor).astype(jnp.bfloat16),
        (jnp.sin(angle) * factor).astype(jnp.bfloat16),
    )


def row_table(length):
    cosine, sine = dft_parts(length)
    return jnp.stack([cosine, -sine])


def column_table(length, direction):
    cosine, sine = dft_parts(length)
    upper = jnp.stack([cosine, direction * sine], axis=1)
    lower = jnp.stack([-direction * sine, cosine], axis=1)
    return jnp.stack([upper, lower])


def layer_norm(values):
    centre = jnp.mean(values, axis=-1, keepdims=True)
    centred = values - centre
    variance = jnp.mean(centred * centred, axis=-1, keepdims=True)
    rstd_value = lax.rsqrt(variance + EPS)
    return (centred * rstd_value, rstd_value)


def norm_backward(upstream, normed, rstd_value, gain):
    scaled = upstream * gain
    result = (
        scaled
        - jnp.mean(scaled, axis=-1, keepdims=True)
        - normed * jnp.mean(scaled * normed, axis=-1, keepdims=True)
    ) * rstd_value
    lead = tuple(range(upstream.ndim - 1))
    return (result, jnp.sum(upstream * normed, axis=lead))


def apply_filter(spectrum, filter_weight, direction):
    real_part = spectrum[0].astype(jnp.float32)
    imag_part = spectrum[1].astype(jnp.float32)
    kernel_real = filter_weight[0].astype(jnp.float32)
    kernel_imag = direction * filter_weight[1].astype(jnp.float32)
    return jnp.stack(
        [
            kernel_real * real_part - kernel_imag * imag_part,
            kernel_real * imag_part + kernel_imag * real_part,
        ]
    )


def exact_gelu(values):
    return jax.nn.gelu(values, approximate=False)


def spectral(values, filter_weight, direction, early=None, late=None):
    width = values.shape[2]
    rows_tab = row_table(width)
    rows = jnp.einsum(
        "pkw,bhwc->pbhkc", rows_tab, values, preferred_element_type=jnp.float32
    ).astype(jnp.bfloat16)
    columns = lax.all_to_all(rows, "space", split_axis=3, concat_axis=2, tiled=True)
    held = None
    if early is not None:
        columns, held = lax.optimization_barrier((columns, early()))
    height = columns.shape[2]
    spectrum = jnp.einsum(
        "qmph,pbhkc->qbmkc", column_table(height, 1), columns, preferred_element_type=jnp.float32
    ).astype(jnp.bfloat16)
    weighted = apply_filter(spectrum, filter_weight[:, None], direction).astype(jnp.bfloat16)
    returned = jnp.einsum(
        "qmph,pbhkc->qbmkc", column_table(height, -1), weighted, preferred_element_type=jnp.float32
    ).astype(jnp.bfloat16)
    back_rows = lax.all_to_all(returned, "space", split_axis=2, concat_axis=3, tiled=True)
    tail = None
    if late is not None:
        back_rows, tail = lax.optimization_barrier((back_rows, late(spectrum)))
    output = jnp.einsum("pkw,pbhkc->bhwc", rows_tab, back_rows, preferred_element_type=jnp.float32)
    return (output, spectrum, held, tail)


def body(noisy_tokens, grad_out, filter_weight, weight_in, weight_out, gain_one, gain_two):
    batch, rows_dev, width, chans = noisy_tokens.shape
    inputs = noisy_tokens.astype(jnp.float32)
    normed_one, rstd_one = layer_norm(inputs)
    mixed_in = (normed_one * gain_one).astype(jnp.bfloat16)
    spatial, spectrum, _, _ = spectral(mixed_in, filter_weight, 1)
    normed_two, rstd_two = layer_norm(spatial)
    mlp_in = (normed_two * gain_two).astype(jnp.bfloat16).reshape(-1, chans)
    preact = jnp.dot(mlp_in, weight_in, preferred_element_type=jnp.float32)
    activated = exact_gelu(preact).astype(jnp.bfloat16)
    mlp_out = jnp.dot(activated, weight_out, preferred_element_type=jnp.float32)
    block_out = (inputs + mlp_out.reshape(inputs.shape)).astype(jnp.bfloat16)
    upstream = grad_out.reshape(-1, chans)
    grad_act = jnp.dot(upstream, weight_out.T, preferred_element_type=jnp.float32)
    grad_pre = jax.vjp(exact_gelu, preact)[1](grad_act)[0].astype(jnp.bfloat16)
    sum_out = jnp.dot(activated.T, upstream, preferred_element_type=jnp.float32)
    sum_in = jnp.dot(mlp_in.T, grad_pre, preferred_element_type=jnp.float32)
    grad_mlp = jnp.dot(grad_pre, weight_in.T, preferred_element_type=jnp.float32).reshape(
        inputs.shape
    )
    grad_spatial, sum_gain_two = norm_backward(grad_mlp, normed_two, rstd_two, gain_two)
    total_tokens = batch * lax.axis_size("copy") * rows_dev * lax.axis_size("space") * width
    factor = 1.0 / math.sqrt(total_tokens)
    n_copy, n_space = lax.axis_size("copy"), lax.axis_size("space")
    parts = [sum_in.reshape(-1), sum_out.reshape(-1), sum_gain_two]

    def weight_sums():
        flat = jnp.concatenate(parts)
        lanes = 128
        block = lanes * 16 << (n_copy * n_space).bit_length() - 1
        padded = -(-flat.size // block) * block
        flat = jnp.pad(flat, (0, padded - flat.size)).reshape(padded // lanes, lanes)
        return all_sum(flat, n_copy, n_space, factor).reshape(-1)

    def filter_grad(adjoint):
        spec_f = spectrum.astype(jnp.float32)
        adj_f = adjoint.astype(jnp.float32)
        filter_terms = jnp.stack(
            [
                jnp.sum(adj_f[0] * spec_f[0] + adj_f[1] * spec_f[1], axis=0),
                jnp.sum(adj_f[1] * spec_f[0] - adj_f[0] * spec_f[1], axis=0),
            ]
        )
        fshape = filter_terms.shape
        return filter_sum(
            filter_terms.astype(jnp.bfloat16).reshape(
                fshape[0] * fshape[1], fshape[2] * fshape[3]
            )
        ).reshape(fshape)

    back_spatial, _, total, grad_filter = spectral(
        grad_spatial.astype(jnp.bfloat16), filter_weight, -1, weight_sums, filter_grad
    )
    grad_normed, sum_gain_one = norm_backward(back_spatial, normed_one, rstd_one, gain_one)
    grad_tokens = (grad_out.astype(jnp.float32) + grad_normed).astype(jnp.bfloat16)
    gain_one_sum = tree_sum(sum_gain_one.reshape(1, -1), n_copy, n_space).reshape(-1)
    outs = []
    at = 0
    for p in parts:
        outs.append(total[at : at + p.size])
        at += p.size
    return (
        block_out,
        grad_tokens,
        grad_filter,
        outs[0].reshape(sum_in.shape),
        outs[1].reshape(sum_out.shape),
        gain_one_sum * factor,
        outs[2].astype(jnp.float32),
    )


def solution(mesh):
    return jax.shard_map(
        body,
        mesh=mesh,
        in_specs=(
            P("copy", "space", None, None),
            P("copy", "space", None, None),
            P(None, None, "space", None),
            P(),
            P(),
            P(),
            P(),
        ),
        out_specs=(
            P("copy", "space", None, None),
            P("copy", "space", None, None),
            P(None, None, "space", None),
            P(),
            P(),
            P(),
            P(),
        ),
        check_vma=False,
    )
```

```python
import functools
import math

import jax
import jax.numpy as jnp
from jax import lax
from jax.experimental import pallas as pl
from jax.experimental.pallas import tpu as pltpu
from jax.sharding import PartitionSpec as P

MESH = pl.DeviceIdType.MESH

EPS = 1e-06


def _partner(idx, bit):
    step = 1 << bit
    flip = 1 - 2 * ((idx // step) % 2)
    return idx + flip * step


def _tree_sum_kernel(n_copy, n_space, x_ref, o_ref, send_buf, recv_buf, send_sem, recv_sem):
    me_c = lax.axis_index("copy")
    me_s = lax.axis_index("space")
    bits = []
    for b in range(n_space.bit_length() - 1):
        bits.append(("space", b))
    for b in range(n_copy.bit_length() - 1):
        bits.append(("copy", b))

    def peer(axis, b):
        if axis == "space":
            return (me_c, _partner(me_s, b))
        return (_partner(me_c, b), me_s)

    barrier = pltpu.get_barrier_semaphore()
    for axis, b in bits:
        pl.semaphore_signal(barrier, inc=1, device_id=peer(axis, b), device_id_type=MESH)
    pl.semaphore_wait(barrier, len(bits))
    acc = x_ref[...]
    copies = []
    for s, (axis, b) in enumerate(bits):
        send_buf[s] = acc
        c = pltpu.make_async_remote_copy(
            src_ref=send_buf.at[s],
            dst_ref=recv_buf.at[s],
            send_sem=send_sem.at[s],
            recv_sem=recv_sem.at[s],
            device_id=peer(axis, b),
            device_id_type=MESH,
        )
        c.start()
        c.wait_recv()
        copies.append(c)
        acc = acc + recv_buf[s]
    for c in copies:
        c.wait_send()
    o_ref[...] = acc


def tree_sum(x, n_copy, n_space):
    steps = (n_copy.bit_length() - 1) + (n_space.bit_length() - 1)
    return pl.pallas_call(
        functools.partial(_tree_sum_kernel, n_copy, n_space),
        out_shape=jax.ShapeDtypeStruct(x.shape, jnp.float32),
        in_specs=[pl.BlockSpec(memory_space=pltpu.VMEM)],
        out_specs=pl.BlockSpec(memory_space=pltpu.VMEM),
        scratch_shapes=[
            pltpu.VMEM((steps,) + x.shape, jnp.float32),
            pltpu.VMEM((steps,) + x.shape, jnp.float32),
            pltpu.SemaphoreType.DMA((steps,)),
            pltpu.SemaphoreType.DMA((steps,)),
        ],
        compiler_params=pltpu.CompilerParams(collective_id=2, has_side_effects=True),
        cost_estimate=pl.CostEstimate(
            flops=steps * x.size, transcendentals=0, bytes_accessed=4 * steps * x.size
        ),
    )(x)


def _filter_sum_kernel(rows, x_ref, o_ref, half_in, part, other, full_in, sems):
    me_c = lax.axis_index("copy")
    me_s = lax.axis_index("space")
    core = me_c % 2
    hi = me_c // 2
    mate = (me_c + 1 - 2 * core, me_s)
    far = (me_c + 2 - 4 * hi, me_s)
    half = rows // 2
    barrier = pltpu.get_barrier_semaphore()
    pl.semaphore_signal(barrier, inc=1, device_id=mate, device_id_type=MESH)
    pl.semaphore_signal(barrier, inc=1, device_id=far, device_id_type=MESH)
    pl.semaphore_wait(barrier, 2)
    mine = pl.ds(pl.multiple_of(core * half, 8), half)
    theirs = pl.ds(pl.multiple_of((1 - core) * half, 8), half)
    c1 = pltpu.make_async_remote_copy(
        src_ref=x_ref.at[theirs], dst_ref=half_in, send_sem=sems.at[0], recv_sem=sems.at[1],
        device_id=mate, device_id_type=MESH)
    c1.start()
    c1.wait_recv()
    own = x_ref[mine, :].astype(jnp.float32)
    got = half_in[...].astype(jnp.float32)
    first = jnp.where(core == 0, own, got)
    second = jnp.where(core == 0, got, own)
    part[...] = (first + second).astype(jnp.bfloat16)
    c2 = pltpu.make_async_remote_copy(
        src_ref=part, dst_ref=other, send_sem=sems.at[2], recv_sem=sems.at[3],
        device_id=far, device_id_type=MESH)
    c2.start()
    c2.wait_recv()
    mine_p = part[...].astype(jnp.float32)
    got_p = other[...].astype(jnp.float32)
    total = jnp.where(hi == 0, mine_p + got_p, got_p + mine_p)
    o_ref[mine, :] = total
    c3 = pltpu.make_async_remote_copy(
        src_ref=o_ref.at[mine], dst_ref=full_in, send_sem=sems.at[4], recv_sem=sems.at[5],
        device_id=mate, device_id_type=MESH)
    c3.start()
    c3.wait_recv()
    o_ref[theirs, :] = full_in[...]
    c1.wait_send()
    c2.wait_send()
    c3.wait_send()


def filter_sum(x):
    rows, cols = x.shape
    half = rows // 2
    return pl.pallas_call(
        functools.partial(_filter_sum_kernel, rows),
        out_shape=jax.ShapeDtypeStruct((rows, cols), jnp.float32),
        in_specs=[pl.BlockSpec(memory_space=pltpu.VMEM)],
        out_specs=pl.BlockSpec(memory_space=pltpu.VMEM),
        scratch_shapes=[
            pltpu.VMEM((half, cols), x.dtype),
            pltpu.VMEM((half, cols), jnp.bfloat16),
            pltpu.VMEM((half, cols), jnp.bfloat16),
            pltpu.VMEM((half, cols), jnp.float32),
            pltpu.SemaphoreType.DMA((6,)),
        ],
        compiler_params=pltpu.CompilerParams(
            collective_id=1, has_side_effects=True, vmem_limit_bytes=48 * 1024 * 1024
        ),
        cost_estimate=pl.CostEstimate(
            flops=2 * rows * cols, transcendentals=0, bytes_accessed=10 * rows * cols
        ),
    )(x)


def _digit_orders(n_copy, n_space):
    c0, xh = ("copy", 0), ("copy", 1)
    if (n_copy, n_space) == (4, 64):
        xl, z1, z2, z4, y1, y2 = [("space", b) for b in range(6)]
        first = [[c0], [xl, z1], [y1, z2], [y2, xh], [z4]]
        second = [[c0], [y1, y2], [xl, z1], [z2, xh], [z4]]
        return first, second
    sb = [("space", b) for b in range(n_space.bit_length() - 1)]
    cb = [("copy", b) for b in range(1, n_copy.bit_length() - 1)]
    rest = sb + cb
    first = [[c0]] + [rest[i : i + 2] for i in range(0, len(rest), 2)]
    rest = rest[::-1]
    second = [[c0]] + [rest[i : i + 2] for i in range(0, len(rest), 2)]
    return first, second


def _plan(n_copy, n_space):
    orders = _digit_orders(n_copy, n_space)
    me_c = lax.axis_index("copy")
    me_s = lax.axis_index("space")
    core = me_c % 2
    plan = []
    for s in range(len(orders[0])):
        per_core = []
        for order in orders:
            digit = order[s]
            radix = 1 << len(digit)
            bits = []
            for axis, b in digit:
                idx = me_c if axis == "copy" else me_s
                bits.append((idx // (1 << b)) % 2)
            v = sum(bit << i for i, bit in enumerate(bits))
            peers = []
            for d in range(1, radix):
                u = (v + d) % radix
                pc, ps = me_c, me_s
                for i, (axis, b) in enumerate(digit):
                    delta = ((u // (1 << i)) % 2 - bits[i]) * (1 << b)
                    if axis == "copy":
                        pc = pc + delta
                    else:
                        ps = ps + delta
                peers.append((pc, ps))
            per_core.append((radix, peers, v))
        (r0, p0, v0), (r1, p1, v1) = per_core
        assert r0 == r1
        peers = [
            ((1 - core) * a[0] + core * b[0], (1 - core) * a[1] + core * b[1])
            for a, b in zip(p0, p1)
        ]
        plan.append((r0, peers, (1 - core) * v0 + core * v1))
    return plan


def _all_sum_kernel(n_copy, n_space, rows, scale, x_ref, o_ref, acc, send, *rest):
    plan = _plan(n_copy, n_space)
    steps = len(plan)
    recv = rest[:steps]
    rs_send, rs_recv, ag_send, ag_recv = rest[steps:]
    barrier = pltpu.get_barrier_semaphore()
    count = 0
    for radix, peers, _ in plan:
        for peer in peers:
            pl.semaphore_signal(barrier, inc=1, device_id=peer, device_id_type=MESH)
            count += 1
    pl.semaphore_wait(barrier, count)

    pending = []
    lo = 0
    length = rows
    slot = 0
    for s, (radix, peers, v) in enumerate(plan):
        part = length // radix
        base = x_ref if s == 0 else acc
        descs = []
        for d, peer in enumerate(peers, start=1):
            u = (v + d) % radix
            give = pl.multiple_of(lo + u * part, 16)
            send[pl.ds(give, part), :] = base[pl.ds(give, part), :].astype(jnp.bfloat16)
            c = pltpu.make_async_remote_copy(
                src_ref=send.at[pl.ds(give, part)],
                dst_ref=recv[s].at[d - 1],
                send_sem=rs_send.at[slot + d - 1],
                recv_sem=rs_recv.at[slot + d - 1],
                device_id=peer,
                device_id_type=MESH,
            )
            c.start()
            descs.append(c)
        keep = pl.multiple_of(lo + v * part, 16)
        total = base[pl.ds(keep, part), :]
        for d, c in enumerate(descs, start=1):
            c.wait_recv()
            total = total + recv[s][d - 1].astype(jnp.float32)
        acc[pl.ds(keep, part), :] = total
        pending += descs
        slot += radix - 1
        lo = keep
        length = part
    mine = pl.ds(pl.multiple_of(lo, 16), length)
    o_ref[mine, :] = (acc[mine, :] * scale).astype(o_ref.dtype)
    for s in reversed(range(steps)):
        radix, peers, v = plan[s]
        slot -= radix - 1
        mine = pl.ds(pl.multiple_of(lo, 16), length)
        start = lo - v * length
        descs = []
        for d, peer in enumerate(peers, start=1):
            c = pltpu.make_async_remote_copy(
                src_ref=o_ref.at[mine],
                dst_ref=o_ref.at[mine],
                send_sem=ag_send.at[slot + d - 1],
                recv_sem=ag_recv.at[slot + d - 1],
                device_id=peer,
                device_id_type=MESH,
            )
            c.start()
            descs.append(c)
        for d, peer in enumerate(peers, start=1):
            w = (v - d + radix) % radix
            theirs = pl.ds(pl.multiple_of(start + w * length, 16), length)
            pltpu.make_async_remote_copy(
                src_ref=o_ref.at[theirs],
                dst_ref=o_ref.at[theirs],
                send_sem=ag_send.at[slot + d - 1],
                recv_sem=ag_recv.at[slot + d - 1],
                device_id=peer,
                device_id_type=MESH,
            ).wait_recv()
        pending += descs
        lo = start
        length = radix * length
    for c in pending:
        c.wait_send()


def all_sum(x, n_copy, n_space, scale):
    rows, cols = x.shape
    orders = _digit_orders(n_copy, n_space)[0]
    radices = [1 << len(d) for d in orders]
    recv = []
    length = rows
    for r in radices:
        length //= r
        recv.append(pltpu.VMEM((r - 1, length, cols), jnp.bfloat16))
    links = sum(r - 1 for r in radices)
    return pl.pallas_call(
        functools.partial(_all_sum_kernel, n_copy, n_space, rows, scale),
        out_shape=jax.ShapeDtypeStruct((rows, cols), jnp.bfloat16),
        in_specs=[pl.BlockSpec(memory_space=pltpu.VMEM)],
        out_specs=pl.BlockSpec(memory_space=pltpu.VMEM),
        scratch_shapes=[
            pltpu.VMEM((rows, cols), jnp.float32),
            pltpu.VMEM((rows, cols), jnp.bfloat16),
        ]
        + recv
        + [pltpu.SemaphoreType.DMA((links,)) for _ in range(4)],
        compiler_params=pltpu.CompilerParams(
            collective_id=3, has_side_effects=True, vmem_limit_bytes=56 * 1024 * 1024
        ),
        cost_estimate=pl.CostEstimate(
            flops=rows * cols, transcendentals=0, bytes_accessed=12 * rows * cols
        ),
    )(x)


def dft_parts(length):
    index = jnp.arange(length, dtype=jnp.int32)
    phase = index[:, None] * index[None, :] % length
    angle = phase.astype(jnp.float32) * (2.0 * math.pi / length)
    factor = 1.0 / math.sqrt(length)
    return (
        (jnp.cos(angle) * factor).astype(jnp.bfloat16),
        (jnp.sin(angle) * factor).astype(jnp.bfloat16),
    )


def row_table(length):
    cosine, sine = dft_parts(length)
    return jnp.stack([cosine, -sine])


def column_table(length, direction):
    cosine, sine = dft_parts(length)
    upper = jnp.stack([cosine, direction * sine], axis=1)
    lower = jnp.stack([-direction * sine, cosine], axis=1)
    return jnp.stack([upper, lower])


def layer_norm(values):
    centre = jnp.mean(values, axis=-1, keepdims=True)
    centred = values - centre
    variance = jnp.mean(centred * centred, axis=-1, keepdims=True)
    rstd_value = lax.rsqrt(variance + EPS)
    return (centred * rstd_value, rstd_value)


def norm_backward(upstream, normed, rstd_value, gain):
    scaled = upstream * gain
    result = (
        scaled
        - jnp.mean(scaled, axis=-1, keepdims=True)
        - normed * jnp.mean(scaled * normed, axis=-1, keepdims=True)
    ) * rstd_value
    lead = tuple(range(upstream.ndim - 1))
    return (result, jnp.sum(upstream * normed, axis=lead))


def apply_filter(spectrum, filter_weight, direction):
    real_part = spectrum[0].astype(jnp.float32)
    imag_part = spectrum[1].astype(jnp.float32)
    kernel_real = filter_weight[0].astype(jnp.float32)
    kernel_imag = direction * filter_weight[1].astype(jnp.float32)
    return jnp.stack(
        [
            kernel_real * real_part - kernel_imag * imag_part,
            kernel_real * imag_part + kernel_imag * real_part,
        ]
    )


def exact_gelu(values):
    return jax.nn.gelu(values, approximate=False)


def spectral(values, filter_weight, direction, early=None, late=None):
    width = values.shape[2]
    rows_tab = row_table(width)
    rows = jnp.einsum(
        "pkw,bhwc->pbhkc", rows_tab, values, preferred_element_type=jnp.float32
    ).astype(jnp.bfloat16)
    columns = lax.all_to_all(rows, "space", split_axis=3, concat_axis=2, tiled=True)
    held = None
    if early is not None:
        columns, held = lax.optimization_barrier((columns, early()))
    height = columns.shape[2]
    spectrum = jnp.einsum(
        "qmph,pbhkc->qbmkc", column_table(height, 1), columns, preferred_element_type=jnp.float32
    ).astype(jnp.bfloat16)
    weighted = apply_filter(spectrum, filter_weight[:, None], direction).astype(jnp.bfloat16)
    returned = jnp.einsum(
        "qmph,pbhkc->qbmkc", column_table(height, -1), weighted, preferred_element_type=jnp.float32
    ).astype(jnp.bfloat16)
    back_rows = lax.all_to_all(returned, "space", split_axis=2, concat_axis=3, tiled=True)
    tail = None
    if late is not None:
        back_rows, tail = lax.optimization_barrier((back_rows, late(spectrum)))
    output = jnp.einsum("pkw,pbhkc->bhwc", rows_tab, back_rows, preferred_element_type=jnp.float32)
    return (output, spectrum, held, tail)


def body(noisy_tokens, grad_out, filter_weight, weight_in, weight_out, gain_one, gain_two):
    batch, rows_dev, width, chans = noisy_tokens.shape
    inputs = noisy_tokens.astype(jnp.float32)
    normed_one, rstd_one = layer_norm(inputs)
    mixed_in = (normed_one * gain_one).astype(jnp.bfloat16)
    spatial, spectrum, _, _ = spectral(mixed_in, filter_weight, 1)
    normed_two, rstd_two = layer_norm(spatial)
    mlp_in = (normed_two * gain_two).astype(jnp.bfloat16).reshape(-1, chans)
    preact = jnp.dot(mlp_in, weight_in, preferred_element_type=jnp.float32)
    activated = exact_gelu(preact).astype(jnp.bfloat16)
    mlp_out = jnp.dot(activated, weight_out, preferred_element_type=jnp.float32)
    block_out = (inputs + mlp_out.reshape(inputs.shape)).astype(jnp.bfloat16)
    upstream = grad_out.reshape(-1, chans)
    grad_act = jnp.dot(upstream, weight_out.T, preferred_element_type=jnp.float32)
    grad_pre = jax.vjp(exact_gelu, preact)[1](grad_act)[0].astype(jnp.bfloat16)
    sum_out = jnp.dot(activated.T, upstream, preferred_element_type=jnp.float32)
    sum_in = jnp.dot(mlp_in.T, grad_pre, preferred_element_type=jnp.float32)
    grad_mlp = jnp.dot(grad_pre, weight_in.T, preferred_element_type=jnp.float32).reshape(
        inputs.shape
    )
    grad_spatial, sum_gain_two = norm_backward(grad_mlp, normed_two, rstd_two, gain_two)
    total_tokens = batch * lax.axis_size("copy") * rows_dev * lax.axis_size("space") * width
    factor = 1.0 / math.sqrt(total_tokens)
    n_copy, n_space = lax.axis_size("copy"), lax.axis_size("space")
    parts = [sum_in.reshape(-1), sum_out.reshape(-1), sum_gain_two]

    def weight_sums():
        flat = jnp.concatenate(parts)
        lanes = 128
        block = lanes * 16 << (n_copy * n_space).bit_length() - 1
        padded = -(-flat.size // block) * block
        flat = jnp.pad(flat, (0, padded - flat.size)).reshape(padded // lanes, lanes)
        return all_sum(flat, n_copy, n_space, factor).reshape(-1)

    def filter_grad(adjoint):
        spec_f = spectrum.astype(jnp.float32)
        adj_f = adjoint.astype(jnp.float32)
        filter_terms = jnp.stack(
            [
                jnp.sum(adj_f[0] * spec_f[0] + adj_f[1] * spec_f[1], axis=0),
                jnp.sum(adj_f[1] * spec_f[0] - adj_f[0] * spec_f[1], axis=0),
            ]
        )
        fshape = filter_terms.shape
        return filter_sum(
            filter_terms.astype(jnp.bfloat16).reshape(
                fshape[0] * fshape[1], fshape[2] * fshape[3]
            )
        ).reshape(fshape)

    back_spatial, _, total, grad_filter = spectral(
        grad_spatial.astype(jnp.bfloat16), filter_weight, -1, weight_sums, filter_grad
    )
    grad_normed, sum_gain_one = norm_backward(back_spatial, normed_one, rstd_one, gain_one)
    grad_tokens = (grad_out.astype(jnp.float32) + grad_normed).astype(jnp.bfloat16)
    gain_one_sum = tree_sum(sum_gain_one.reshape(1, -1), n_copy, n_space).reshape(-1)
    outs = []
    at = 0
    for p in parts:
        outs.append(total[at : at + p.size])
        at += p.size
    return (
        block_out,
        grad_tokens,
        grad_filter,
        outs[0].reshape(sum_in.shape),
        outs[1].reshape(sum_out.shape),
        gain_one_sum * factor,
        outs[2].astype(jnp.float32),
    )


def solution(mesh):
    return jax.shard_map(
        body,
        mesh=mesh,
        in_specs=(
            P("copy", "space", None, None),
            P("copy", "space", None, None),
            P(None, None, "space", None),
            P(),
            P(),
            P(),
            P(),
        ),
        out_specs=(
            P("copy", "space", None, None),
            P("copy", "space", None, None),
            P(None, None, "space", None),
            P(),
            P(),
            P(),
            P(),
        ),
        check_vma=False,
    )
```

```python
import functools
import math

import jax
import jax.numpy as jnp
from jax import lax
from jax.experimental import pallas as pl
from jax.experimental.pallas import tpu as pltpu
from jax.sharding import PartitionSpec as P

MESH = pl.DeviceIdType.MESH

EPS = 1e-06


def _filter_sum_kernel(rows, x_ref, o_ref, half_in, part, other, full_in, sems):
    me_c = lax.axis_index("copy")
    me_s = lax.axis_index("space")
    core = me_c % 2
    hi = me_c // 2
    mate = (me_c + 1 - 2 * core, me_s)
    far = (me_c + 2 - 4 * hi, me_s)
    half = rows // 2
    barrier = pltpu.get_barrier_semaphore()
    pl.semaphore_signal(barrier, inc=1, device_id=mate, device_id_type=MESH)
    pl.semaphore_signal(barrier, inc=1, device_id=far, device_id_type=MESH)
    pl.semaphore_wait(barrier, 2)
    mine = pl.ds(pl.multiple_of(core * half, 8), half)
    theirs = pl.ds(pl.multiple_of((1 - core) * half, 8), half)
    c1 = pltpu.make_async_remote_copy(
        src_ref=x_ref.at[theirs], dst_ref=half_in, send_sem=sems.at[0], recv_sem=sems.at[1],
        device_id=mate, device_id_type=MESH)
    c1.start()
    c1.wait_recv()
    own = x_ref[mine, :].astype(jnp.float32)
    got = half_in[...].astype(jnp.float32)
    first = jnp.where(core == 0, own, got)
    second = jnp.where(core == 0, got, own)
    part[...] = (first + second).astype(jnp.bfloat16)
    c2 = pltpu.make_async_remote_copy(
        src_ref=part, dst_ref=other, send_sem=sems.at[2], recv_sem=sems.at[3],
        device_id=far, device_id_type=MESH)
    c2.start()
    c2.wait_recv()
    mine_p = part[...].astype(jnp.float32)
    got_p = other[...].astype(jnp.float32)
    total = jnp.where(hi == 0, mine_p + got_p, got_p + mine_p)
    o_ref[mine, :] = total
    c3 = pltpu.make_async_remote_copy(
        src_ref=o_ref.at[mine], dst_ref=full_in, send_sem=sems.at[4], recv_sem=sems.at[5],
        device_id=mate, device_id_type=MESH)
    c3.start()
    c3.wait_recv()
    o_ref[theirs, :] = full_in[...]
    c1.wait_send()
    c2.wait_send()
    c3.wait_send()


def filter_sum(x):
    rows, cols = x.shape
    half = rows // 2
    return pl.pallas_call(
        functools.partial(_filter_sum_kernel, rows),
        out_shape=jax.ShapeDtypeStruct((rows, cols), jnp.float32),
        in_specs=[pl.BlockSpec(memory_space=pltpu.VMEM)],
        out_specs=pl.BlockSpec(memory_space=pltpu.VMEM),
        scratch_shapes=[
            pltpu.VMEM((half, cols), x.dtype),
            pltpu.VMEM((half, cols), jnp.bfloat16),
            pltpu.VMEM((half, cols), jnp.bfloat16),
            pltpu.VMEM((half, cols), jnp.float32),
            pltpu.SemaphoreType.DMA((6,)),
        ],
        compiler_params=pltpu.CompilerParams(
            collective_id=1, has_side_effects=True, vmem_limit_bytes=48 * 1024 * 1024
        ),
        cost_estimate=pl.CostEstimate(
            flops=2 * rows * cols, transcendentals=0, bytes_accessed=10 * rows * cols
        ),
    )(x)


def _digit_orders(n_copy, n_space):
    c0, xh = ("copy", 0), ("copy", 1)
    if (n_copy, n_space) == (4, 64):
        xl, z1, z2, z4, y1, y2 = [("space", b) for b in range(6)]
        first = [[c0], [xl, z1], [y1, z2], [y2, xh], [z4]]
        second = [[c0], [y1, y2], [xl, z1], [z2, xh], [z4]]
        return first, second
    sb = [("space", b) for b in range(n_space.bit_length() - 1)]
    cb = [("copy", b) for b in range(1, n_copy.bit_length() - 1)]
    rest = sb + cb
    first = [[c0]] + [rest[i : i + 2] for i in range(0, len(rest), 2)]
    rest = rest[::-1]
    second = [[c0]] + [rest[i : i + 2] for i in range(0, len(rest), 2)]
    return first, second


def _plan(n_copy, n_space, split=True):
    orders = _digit_orders(n_copy, n_space)
    if not split:
        orders = (orders[0], orders[0])
    me_c = lax.axis_index("copy")
    me_s = lax.axis_index("space")
    core = me_c % 2
    plan = []
    for s in range(len(orders[0])):
        per_core = []
        for order in orders:
            digit = order[s]
            radix = 1 << len(digit)
            bits = []
            for axis, b in digit:
                idx = me_c if axis == "copy" else me_s
                bits.append((idx // (1 << b)) % 2)
            v = sum(bit << i for i, bit in enumerate(bits))
            peers = []
            for d in range(1, radix):
                u = (v + d) % radix
                pc, ps = me_c, me_s
                for i, (axis, b) in enumerate(digit):
                    delta = ((u // (1 << i)) % 2 - bits[i]) * (1 << b)
                    if axis == "copy":
                        pc = pc + delta
                    else:
                        ps = ps + delta
                peers.append((pc, ps))
            per_core.append((radix, peers, v))
        (r0, p0, v0), (r1, p1, v1) = per_core
        assert r0 == r1
        peers = [
            ((1 - core) * a[0] + core * b[0], (1 - core) * a[1] + core * b[1])
            for a, b in zip(p0, p1)
        ]
        plan.append((r0, peers, (1 - core) * v0 + core * v1))
    return plan


def _all_sum_kernel(n_copy, n_space, rows, scale, x_ref, o_ref, acc, send, *rest):
    plan = _plan(n_copy, n_space)
    steps = len(plan)
    recv = rest[:steps]
    rs_send, rs_recv, ag_send, ag_recv = rest[steps:]
    barrier = pltpu.get_barrier_semaphore()
    count = 0
    for radix, peers, _ in plan:
        for peer in peers:
            pl.semaphore_signal(barrier, inc=1, device_id=peer, device_id_type=MESH)
            count += 1
    pl.semaphore_wait(barrier, count)

    pending = []
    lo = 0
    length = rows
    slot = 0
    for s, (radix, peers, v) in enumerate(plan):
        part = length // radix
        base = x_ref if s == 0 else acc
        descs = []
        for d, peer in enumerate(peers, start=1):
            u = (v + d) % radix
            give = pl.multiple_of(lo + u * part, 16)
            send[pl.ds(give, part), :] = base[pl.ds(give, part), :].astype(jnp.bfloat16)
            c = pltpu.make_async_remote_copy(
                src_ref=send.at[pl.ds(give, part)],
                dst_ref=recv[s].at[d - 1],
                send_sem=rs_send.at[slot + d - 1],
                recv_sem=rs_recv.at[slot + d - 1],
                device_id=peer,
                device_id_type=MESH,
            )
            c.start()
            descs.append(c)
        keep = pl.multiple_of(lo + v * part, 16)
        total = base[pl.ds(keep, part), :]
        for d, c in enumerate(descs, start=1):
            c.wait_recv()
            total = total + recv[s][d - 1].astype(jnp.float32)
        acc[pl.ds(keep, part), :] = total
        pending += descs
        slot += radix - 1
        lo = keep
        length = part
    mine = pl.ds(pl.multiple_of(lo, 16), length)
    o_ref[mine, :] = (acc[mine, :] * scale).astype(o_ref.dtype)
    for s in reversed(range(steps)):
        radix, peers, v = plan[s]
        slot -= radix - 1
        mine = pl.ds(pl.multiple_of(lo, 16), length)
        start = lo - v * length
        descs = []
        for d, peer in enumerate(peers, start=1):
            c = pltpu.make_async_remote_copy(
                src_ref=o_ref.at[mine],
                dst_ref=o_ref.at[mine],
                send_sem=ag_send.at[slot + d - 1],
                recv_sem=ag_recv.at[slot + d - 1],
                device_id=peer,
                device_id_type=MESH,
            )
            c.start()
            descs.append(c)
        for d, peer in enumerate(peers, start=1):
            w = (v - d + radix) % radix
            theirs = pl.ds(pl.multiple_of(start + w * length, 16), length)
            pltpu.make_async_remote_copy(
                src_ref=o_ref.at[theirs],
                dst_ref=o_ref.at[theirs],
                send_sem=ag_send.at[slot + d - 1],
                recv_sem=ag_recv.at[slot + d - 1],
                device_id=peer,
                device_id_type=MESH,
            ).wait_recv()
        pending += descs
        lo = start
        length = radix * length
    for c in pending:
        c.wait_send()


def all_sum(x, n_copy, n_space, scale):
    rows, cols = x.shape
    orders = _digit_orders(n_copy, n_space)[0]
    radices = [1 << len(d) for d in orders]
    recv = []
    length = rows
    for r in radices:
        length //= r
        recv.append(pltpu.VMEM((r - 1, length, cols), jnp.bfloat16))
    links = sum(r - 1 for r in radices)
    return pl.pallas_call(
        functools.partial(_all_sum_kernel, n_copy, n_space, rows, scale),
        out_shape=jax.ShapeDtypeStruct((rows, cols), jnp.bfloat16),
        in_specs=[pl.BlockSpec(memory_space=pltpu.VMEM)],
        out_specs=pl.BlockSpec(memory_space=pltpu.VMEM),
        scratch_shapes=[
            pltpu.VMEM((rows, cols), jnp.float32),
            pltpu.VMEM((rows, cols), jnp.bfloat16),
        ]
        + recv
        + [pltpu.SemaphoreType.DMA((links,)) for _ in range(4)],
        compiler_params=pltpu.CompilerParams(
            collective_id=3, has_side_effects=True, vmem_limit_bytes=56 * 1024 * 1024
        ),
        cost_estimate=pl.CostEstimate(
            flops=rows * cols, transcendentals=0, bytes_accessed=12 * rows * cols
        ),
    )(x)


def _tree_sum_kernel(n_copy, n_space, x_ref, o_ref, *rest):
    plan = _plan(n_copy, n_space, split=False)
    steps = len(plan)
    slots = rest[:steps]
    send_sem, recv_sem = rest[steps:]
    barrier = pltpu.get_barrier_semaphore()
    count = 0
    for _, peers, _ in plan:
        for peer in peers:
            pl.semaphore_signal(barrier, inc=1, device_id=peer, device_id_type=MESH)
            count += 1
    pl.semaphore_wait(barrier, count)
    acc = x_ref[...]
    pending = []
    slot = 0
    for s, (radix, peers, v) in enumerate(plan):
        slots[s][0] = acc
        descs = []
        for d, peer in enumerate(peers, start=1):
            c = pltpu.make_async_remote_copy(
                src_ref=slots[s].at[0],
                dst_ref=slots[s].at[d],
                send_sem=send_sem.at[slot + d - 1],
                recv_sem=recv_sem.at[slot + d - 1],
                device_id=peer,
                device_id_type=MESH,
            )
            c.start()
            descs.append(c)
        for c in descs:
            c.wait_recv()
        total = slots[s][(v + radix) % radix]
        for u in range(1, radix):
            total = total + slots[s][(v - u + radix) % radix]
        acc = total
        pending += descs
        slot += radix - 1
    for c in pending:
        c.wait_send()
    o_ref[...] = acc


def tree_sum(x, n_copy, n_space):
    radices = [1 << len(d) for d in _digit_orders(n_copy, n_space)[0]]
    links = sum(r - 1 for r in radices)
    return pl.pallas_call(
        functools.partial(_tree_sum_kernel, n_copy, n_space),
        out_shape=jax.ShapeDtypeStruct(x.shape, jnp.float32),
        in_specs=[pl.BlockSpec(memory_space=pltpu.VMEM)],
        out_specs=pl.BlockSpec(memory_space=pltpu.VMEM),
        scratch_shapes=[pltpu.VMEM((r,) + x.shape, jnp.float32) for r in radices]
        + [pltpu.SemaphoreType.DMA((links,)), pltpu.SemaphoreType.DMA((links,))],
        compiler_params=pltpu.CompilerParams(collective_id=2, has_side_effects=True),
        cost_estimate=pl.CostEstimate(
            flops=links * x.size, transcendentals=0, bytes_accessed=8 * links * x.size
        ),
    )(x)


def dft_parts(length):
    index = jnp.arange(length, dtype=jnp.int32)
    phase = index[:, None] * index[None, :] % length
    angle = phase.astype(jnp.float32) * (2.0 * math.pi / length)
    factor = 1.0 / math.sqrt(length)
    return (
        (jnp.cos(angle) * factor).astype(jnp.bfloat16),
        (jnp.sin(angle) * factor).astype(jnp.bfloat16),
    )


def row_table(length):
    cosine, sine = dft_parts(length)
    return jnp.stack([cosine, -sine])


def column_table(length, direction):
    cosine, sine = dft_parts(length)
    upper = jnp.stack([cosine, direction * sine], axis=1)
    lower = jnp.stack([-direction * sine, cosine], axis=1)
    return jnp.stack([upper, lower])


def layer_norm(values):
    centre = jnp.mean(values, axis=-1, keepdims=True)
    centred = values - centre
    variance = jnp.mean(centred * centred, axis=-1, keepdims=True)
    rstd_value = lax.rsqrt(variance + EPS)
    return (centred * rstd_value, rstd_value)


def norm_backward(upstream, normed, rstd_value, gain):
    scaled = upstream * gain
    result = (
        scaled
        - jnp.mean(scaled, axis=-1, keepdims=True)
        - normed * jnp.mean(scaled * normed, axis=-1, keepdims=True)
    ) * rstd_value
    lead = tuple(range(upstream.ndim - 1))
    return (result, jnp.sum(upstream * normed, axis=lead))


def apply_filter(spectrum, filter_weight, direction):
    real_part = spectrum[0].astype(jnp.float32)
    imag_part = spectrum[1].astype(jnp.float32)
    kernel_real = filter_weight[0].astype(jnp.float32)
    kernel_imag = direction * filter_weight[1].astype(jnp.float32)
    return jnp.stack(
        [
            kernel_real * real_part - kernel_imag * imag_part,
            kernel_real * imag_part + kernel_imag * real_part,
        ]
    )


def exact_gelu(values):
    return jax.nn.gelu(values, approximate=False)


def spectral(values, filter_weight, direction, early=None, late=None):
    width = values.shape[2]
    rows_tab = row_table(width)
    rows = jnp.einsum(
        "pkw,bhwc->pbhkc", rows_tab, values, preferred_element_type=jnp.float32
    ).astype(jnp.bfloat16)
    columns = lax.all_to_all(rows, "space", split_axis=3, concat_axis=2, tiled=True)
    held = None
    if early is not None:
        columns, held = lax.optimization_barrier((columns, early()))
    height = columns.shape[2]
    spectrum = jnp.einsum(
        "qmph,pbhkc->qbmkc", column_table(height, 1), columns, preferred_element_type=jnp.float32
    ).astype(jnp.bfloat16)
    weighted = apply_filter(spectrum, filter_weight[:, None], direction).astype(jnp.bfloat16)
    returned = jnp.einsum(
        "qmph,pbhkc->qbmkc", column_table(height, -1), weighted, preferred_element_type=jnp.float32
    ).astype(jnp.bfloat16)
    back_rows = lax.all_to_all(returned, "space", split_axis=2, concat_axis=3, tiled=True)
    tail = None
    if late is not None:
        back_rows, tail = lax.optimization_barrier((back_rows, late(spectrum)))
    output = jnp.einsum("pkw,pbhkc->bhwc", rows_tab, back_rows, preferred_element_type=jnp.float32)
    return (output, spectrum, held, tail)


def body(noisy_tokens, grad_out, filter_weight, weight_in, weight_out, gain_one, gain_two):
    batch, rows_dev, width, chans = noisy_tokens.shape
    inputs = noisy_tokens.astype(jnp.float32)
    normed_one, rstd_one = layer_norm(inputs)
    mixed_in = (normed_one * gain_one).astype(jnp.bfloat16)
    spatial, spectrum, _, _ = spectral(mixed_in, filter_weight, 1)
    normed_two, rstd_two = layer_norm(spatial)
    mlp_in = (normed_two * gain_two).astype(jnp.bfloat16).reshape(-1, chans)
    preact = jnp.dot(mlp_in, weight_in, preferred_element_type=jnp.float32)
    activated = exact_gelu(preact).astype(jnp.bfloat16)
    mlp_out = jnp.dot(activated, weight_out, preferred_element_type=jnp.float32)
    block_out = (inputs + mlp_out.reshape(inputs.shape)).astype(jnp.bfloat16)
    upstream = grad_out.reshape(-1, chans)
    grad_act = jnp.dot(upstream, weight_out.T, preferred_element_type=jnp.float32)
    grad_pre = jax.vjp(exact_gelu, preact)[1](grad_act)[0].astype(jnp.bfloat16)
    sum_out = jnp.dot(activated.T, upstream, preferred_element_type=jnp.float32)
    sum_in = jnp.dot(mlp_in.T, grad_pre, preferred_element_type=jnp.float32)
    grad_mlp = jnp.dot(grad_pre, weight_in.T, preferred_element_type=jnp.float32).reshape(
        inputs.shape
    )
    grad_spatial, sum_gain_two = norm_backward(grad_mlp, normed_two, rstd_two, gain_two)
    total_tokens = batch * lax.axis_size("copy") * rows_dev * lax.axis_size("space") * width
    factor = 1.0 / math.sqrt(total_tokens)
    n_copy, n_space = lax.axis_size("copy"), lax.axis_size("space")
    parts = [sum_in.reshape(-1), sum_out.reshape(-1), sum_gain_two]

    def weight_sums():
        flat = jnp.concatenate(parts)
        lanes = 128
        block = lanes * 16 << (n_copy * n_space).bit_length() - 1
        padded = -(-flat.size // block) * block
        flat = jnp.pad(flat, (0, padded - flat.size)).reshape(padded // lanes, lanes)
        return all_sum(flat, n_copy, n_space, factor).reshape(-1)

    def filter_grad(adjoint):
        spec_f = spectrum.astype(jnp.float32)
        adj_f = adjoint.astype(jnp.float32)
        filter_terms = jnp.stack(
            [
                jnp.sum(adj_f[0] * spec_f[0] + adj_f[1] * spec_f[1], axis=0),
                jnp.sum(adj_f[1] * spec_f[0] - adj_f[0] * spec_f[1], axis=0),
            ]
        )
        fshape = filter_terms.shape
        return filter_sum(
            filter_terms.astype(jnp.bfloat16).reshape(
                fshape[0] * fshape[1], fshape[2] * fshape[3]
            )
        ).reshape(fshape)

    back_spatial, _, total, grad_filter = spectral(
        grad_spatial.astype(jnp.bfloat16), filter_weight, -1, weight_sums, filter_grad
    )
    grad_normed, sum_gain_one = norm_backward(back_spatial, normed_one, rstd_one, gain_one)
    grad_tokens = (grad_out.astype(jnp.float32) + grad_normed).astype(jnp.bfloat16)
    gain_one_sum = tree_sum(sum_gain_one.reshape(1, -1), n_copy, n_space).reshape(-1)
    outs = []
    at = 0
    for p in parts:
        outs.append(total[at : at + p.size])
        at += p.size
    return (
        block_out,
        grad_tokens,
        grad_filter,
        outs[0].reshape(sum_in.shape),
        outs[1].reshape(sum_out.shape),
        gain_one_sum * factor,
        outs[2].astype(jnp.float32),
    )


def solution(mesh):
    return jax.shard_map(
        body,
        mesh=mesh,
        in_specs=(
            P("copy", "space", None, None),
            P("copy", "space", None, None),
            P(None, None, "space", None),
            P(),
            P(),
            P(),
            P(),
        ),
        out_specs=(
            P("copy", "space", None, None),
            P("copy", "space", None, None),
            P(None, None, "space", None),
            P(),
            P(),
            P(),
            P(),
        ),
        check_vma=False,
    )
```

```python
import functools
import math

import jax
import jax.numpy as jnp
from jax import lax
from jax.experimental import pallas as pl
from jax.experimental.pallas import tpu as pltpu
from jax.sharding import PartitionSpec as P

MESH = pl.DeviceIdType.MESH

EPS = 1e-06


def _filter_sum_kernel(rows, x_ref, o_ref, half_in, part, other, full_in, sems):
    me_c = lax.axis_index("copy")
    me_s = lax.axis_index("space")
    core = me_c % 2
    hi = me_c // 2
    mate = (me_c + 1 - 2 * core, me_s)
    far = (me_c + 2 - 4 * hi, me_s)
    half = rows // 2
    barrier = pltpu.get_barrier_semaphore()
    pl.semaphore_signal(barrier, inc=1, device_id=mate, device_id_type=MESH)
    pl.semaphore_signal(barrier, inc=1, device_id=far, device_id_type=MESH)
    pl.semaphore_wait(barrier, 2)
    mine = pl.ds(pl.multiple_of(core * half, 8), half)
    theirs = pl.ds(pl.multiple_of((1 - core) * half, 8), half)
    c1 = pltpu.make_async_remote_copy(
        src_ref=x_ref.at[theirs], dst_ref=half_in, send_sem=sems.at[0], recv_sem=sems.at[1],
        device_id=mate, device_id_type=MESH)
    c1.start()
    c1.wait_recv()
    own = x_ref[mine, :].astype(jnp.float32)
    got = half_in[...].astype(jnp.float32)
    first = jnp.where(core == 0, own, got)
    second = jnp.where(core == 0, got, own)
    part[...] = (first + second).astype(jnp.bfloat16)
    c2 = pltpu.make_async_remote_copy(
        src_ref=part, dst_ref=other, send_sem=sems.at[2], recv_sem=sems.at[3],
        device_id=far, device_id_type=MESH)
    c2.start()
    c2.wait_recv()
    mine_p = part[...].astype(jnp.float32)
    got_p = other[...].astype(jnp.float32)
    total = jnp.where(hi == 0, mine_p + got_p, got_p + mine_p)
    o_ref[mine, :] = total
    c3 = pltpu.make_async_remote_copy(
        src_ref=o_ref.at[mine], dst_ref=full_in, send_sem=sems.at[4], recv_sem=sems.at[5],
        device_id=mate, device_id_type=MESH)
    c3.start()
    c3.wait_recv()
    o_ref[theirs, :] = full_in[...]
    c1.wait_send()
    c2.wait_send()
    c3.wait_send()


def filter_sum(x):
    rows, cols = x.shape
    half = rows // 2
    return pl.pallas_call(
        functools.partial(_filter_sum_kernel, rows),
        out_shape=jax.ShapeDtypeStruct((rows, cols), jnp.float32),
        in_specs=[pl.BlockSpec(memory_space=pltpu.VMEM)],
        out_specs=pl.BlockSpec(memory_space=pltpu.VMEM),
        scratch_shapes=[
            pltpu.VMEM((half, cols), x.dtype),
            pltpu.VMEM((half, cols), jnp.bfloat16),
            pltpu.VMEM((half, cols), jnp.bfloat16),
            pltpu.VMEM((half, cols), jnp.float32),
            pltpu.SemaphoreType.DMA((6,)),
        ],
        compiler_params=pltpu.CompilerParams(
            collective_id=1, has_side_effects=True, vmem_limit_bytes=48 * 1024 * 1024
        ),
        cost_estimate=pl.CostEstimate(
            flops=2 * rows * cols, transcendentals=0, bytes_accessed=10 * rows * cols
        ),
    )(x)


def _digit_orders(n_copy, n_space):
    c0, xh = ("copy", 0), ("copy", 1)
    if (n_copy, n_space) == (4, 64):
        xl, z1, z2, z4, y1, y2 = [("space", b) for b in range(6)]
        first = [[c0], [xl, z1], [y1, z2], [y2, xh], [z4]]
        second = [[c0], [y1, y2], [xl, z1], [z2, xh], [z4]]
        return first, second
    sb = [("space", b) for b in range(n_space.bit_length() - 1)]
    cb = [("copy", b) for b in range(1, n_copy.bit_length() - 1)]
    rest = sb + cb
    first = [[c0]] + [rest[i : i + 2] for i in range(0, len(rest), 2)]
    rest = rest[::-1]
    second = [[c0]] + [rest[i : i + 2] for i in range(0, len(rest), 2)]
    return first, second


def _plan(n_copy, n_space, split=True):
    orders = _digit_orders(n_copy, n_space)
    if not split:
        orders = (orders[0], orders[0])
    me_c = lax.axis_index("copy")
    me_s = lax.axis_index("space")
    core = me_c % 2
    plan = []
    for s in range(len(orders[0])):
        per_core = []
        for order in orders:
            digit = order[s]
            radix = 1 << len(digit)
            bits = []
            for axis, b in digit:
                idx = me_c if axis == "copy" else me_s
                bits.append((idx // (1 << b)) % 2)
            v = sum(bit << i for i, bit in enumerate(bits))
            peers = []
            for d in range(1, radix):
                u = (v + d) % radix
                pc, ps = me_c, me_s
                for i, (axis, b) in enumerate(digit):
                    delta = ((u // (1 << i)) % 2 - bits[i]) * (1 << b)
                    if axis == "copy":
                        pc = pc + delta
                    else:
                        ps = ps + delta
                peers.append((pc, ps))
            per_core.append((radix, peers, v))
        (r0, p0, v0), (r1, p1, v1) = per_core
        assert r0 == r1
        peers = [
            ((1 - core) * a[0] + core * b[0], (1 - core) * a[1] + core * b[1])
            for a, b in zip(p0, p1)
        ]
        plan.append((r0, peers, (1 - core) * v0 + core * v1))
    return plan


def _split_axes(n_copy, n_space):
    radices = [1 << len(d) for d in _digit_orders(n_copy, n_space)[0]]
    if (n_copy, n_space) == (4, 64):
        return radices, [0, 0, 0, 1, 0]
    return radices, [0] * len(radices)


def _all_sum_kernel(n_copy, n_space, scale, a_ref, b_ref, c_ref, o_ref, acc, send, *rest):
    plan = _plan(n_copy, n_space)
    _, axes = _split_axes(n_copy, n_space)
    steps = len(plan)
    recv = rest[:steps]
    rs_send, rs_recv, ag_send, ag_recv, local = rest[steps:]
    rows, cols = acc.shape
    at = 0
    loads = []
    for i, part_ref in enumerate((a_ref, b_ref, c_ref)):
        n = part_ref.shape[0]
        cp = pltpu.make_async_copy(part_ref, acc.at[pl.ds(at, n)], local.at[i])
        cp.start()
        loads.append(cp)
        at += n
    barrier = pltpu.get_barrier_semaphore()
    count = 0
    for radix, peers, _ in plan:
        for peer in peers:
            pl.semaphore_signal(barrier, inc=1, device_id=peer, device_id_type=MESH)
            count += 1
    for cp in loads:
        cp.wait()
    pl.semaphore_wait(barrier, count)

    def window(r0, rl, c0, cl):
        return (pl.ds(pl.multiple_of(r0, 16), rl), pl.ds(pl.multiple_of(c0, 128), cl))

    pending = []
    box = [0, rows, 0, cols]
    slot = 0
    for s, (radix, peers, v) in enumerate(plan):
        r0, rl, c0, cl = box
        if axes[s] == 0:
            part = rl // radix

            def piece(u, r0=r0, c0=c0, cl=cl, part=part):
                return window(r0 + u * part, part, c0, cl)
        else:
            part = cl // radix

            def piece(u, r0=r0, rl=rl, c0=c0, part=part):
                return window(r0, rl, c0 + u * part, part)
        descs = []
        for d, peer in enumerate(peers, start=1):
            u = (v + d) % radix
            w = piece(u)
            send[w] = acc[w].astype(jnp.bfloat16)
            c = pltpu.make_async_remote_copy(
                src_ref=send.at[w],
                dst_ref=recv[s].at[d - 1],
                send_sem=rs_send.at[slot + d - 1],
                recv_sem=rs_recv.at[slot + d - 1],
                device_id=peer,
                device_id_type=MESH,
            )
            c.start()
            descs.append(c)
        keep = piece(v)
        total = acc[keep]
        for d, c in enumerate(descs, start=1):
            c.wait_recv()
            total = total + recv[s][d - 1].astype(jnp.float32)
        acc[keep] = total
        pending += descs
        slot += radix - 1
        if axes[s] == 0:
            box = [r0 + v * part, part, c0, cl]
        else:
            box = [r0, rl, c0 + v * part, part]
    r0, rl, c0, cl = box
    mine = window(r0, rl, c0, cl)
    o_ref[mine] = (acc[mine] * scale).astype(o_ref.dtype)
    for s in reversed(range(steps)):
        radix, peers, v = plan[s]
        slot -= radix - 1
        r0, rl, c0, cl = box
        if axes[s] == 0:
            first = r0 - v * rl

            def piece(u, first=first, rl=rl, c0=c0, cl=cl):
                return window(first + u * rl, rl, c0, cl)

            box = [first, radix * rl, c0, cl]
        else:
            first = c0 - v * cl

            def piece(u, first=first, r0=r0, rl=rl, cl=cl):
                return window(r0, rl, first + u * cl, cl)

            box = [r0, rl, first, radix * cl]
        mine = piece(v)
        descs = []
        for d, peer in enumerate(peers, start=1):
            c = pltpu.make_async_remote_copy(
                src_ref=o_ref.at[mine],
                dst_ref=o_ref.at[mine],
                send_sem=ag_send.at[slot + d - 1],
                recv_sem=ag_recv.at[slot + d - 1],
                device_id=peer,
                device_id_type=MESH,
            )
            c.start()
            descs.append(c)
        for d, peer in enumerate(peers, start=1):
            theirs = piece((v - d + radix) % radix)
            pltpu.make_async_remote_copy(
                src_ref=o_ref.at[theirs],
                dst_ref=o_ref.at[theirs],
                send_sem=ag_send.at[slot + d - 1],
                recv_sem=ag_recv.at[slot + d - 1],
                device_id=peer,
                device_id_type=MESH,
            ).wait_recv()
        pending += descs
    for c in pending:
        c.wait_send()


def all_sum(parts, n_copy, n_space, scale):
    rows = sum(p.shape[0] for p in parts)
    cols = parts[0].shape[1]
    radices, axes = _split_axes(n_copy, n_space)
    recv = []
    rl, cl = rows, cols
    for r, a in zip(radices, axes):
        if a == 0:
            rl //= r
        else:
            cl //= r
        recv.append(pltpu.VMEM((r - 1, rl, cl), jnp.bfloat16))
    links = sum(r - 1 for r in radices)
    return pl.pallas_call(
        functools.partial(_all_sum_kernel, n_copy, n_space, scale),
        out_shape=jax.ShapeDtypeStruct((rows, cols), jnp.bfloat16),
        in_specs=[pl.BlockSpec(memory_space=pltpu.VMEM)] * len(parts),
        out_specs=pl.BlockSpec(memory_space=pltpu.VMEM),
        scratch_shapes=[
            pltpu.VMEM((rows, cols), jnp.float32),
            pltpu.VMEM((rows, cols), jnp.bfloat16),
        ]
        + recv
        + [pltpu.SemaphoreType.DMA((links,)) for _ in range(4)]
        + [pltpu.SemaphoreType.DMA((len(parts),))],
        compiler_params=pltpu.CompilerParams(
            collective_id=3, has_side_effects=True, vmem_limit_bytes=56 * 1024 * 1024
        ),
        cost_estimate=pl.CostEstimate(
            flops=rows * cols, transcendentals=0, bytes_accessed=12 * rows * cols
        ),
    )(*parts)


def _tree_sum_kernel(n_copy, n_space, x_ref, o_ref, *rest):
    plan = _plan(n_copy, n_space, split=False)
    steps = len(plan)
    slots = rest[:steps]
    send_sem, recv_sem = rest[steps:]
    barrier = pltpu.get_barrier_semaphore()
    count = 0
    for _, peers, _ in plan:
        for peer in peers:
            pl.semaphore_signal(barrier, inc=1, device_id=peer, device_id_type=MESH)
            count += 1
    pl.semaphore_wait(barrier, count)
    acc = x_ref[...]
    pending = []
    slot = 0
    for s, (radix, peers, v) in enumerate(plan):
        slots[s][0] = acc
        descs = []
        for d, peer in enumerate(peers, start=1):
            c = pltpu.make_async_remote_copy(
                src_ref=slots[s].at[0],
                dst_ref=slots[s].at[d],
                send_sem=send_sem.at[slot + d - 1],
                recv_sem=recv_sem.at[slot + d - 1],
                device_id=peer,
                device_id_type=MESH,
            )
            c.start()
            descs.append(c)
        for c in descs:
            c.wait_recv()
        total = slots[s][(v + radix) % radix]
        for u in range(1, radix):
            total = total + slots[s][(v - u + radix) % radix]
        acc = total
        pending += descs
        slot += radix - 1
    for c in pending:
        c.wait_send()
    o_ref[...] = acc


def tree_sum(x, n_copy, n_space):
    radices = [1 << len(d) for d in _digit_orders(n_copy, n_space)[0]]
    links = sum(r - 1 for r in radices)
    return pl.pallas_call(
        functools.partial(_tree_sum_kernel, n_copy, n_space),
        out_shape=jax.ShapeDtypeStruct(x.shape, jnp.float32),
        in_specs=[pl.BlockSpec(memory_space=pltpu.VMEM)],
        out_specs=pl.BlockSpec(memory_space=pltpu.VMEM),
        scratch_shapes=[pltpu.VMEM((r,) + x.shape, jnp.float32) for r in radices]
        + [pltpu.SemaphoreType.DMA((links,)), pltpu.SemaphoreType.DMA((links,))],
        compiler_params=pltpu.CompilerParams(collective_id=2, has_side_effects=True),
        cost_estimate=pl.CostEstimate(
            flops=links * x.size, transcendentals=0, bytes_accessed=8 * links * x.size
        ),
    )(x)


def dft_parts(length):
    index = jnp.arange(length, dtype=jnp.int32)
    phase = index[:, None] * index[None, :] % length
    angle = phase.astype(jnp.float32) * (2.0 * math.pi / length)
    factor = 1.0 / math.sqrt(length)
    return (
        (jnp.cos(angle) * factor).astype(jnp.bfloat16),
        (jnp.sin(angle) * factor).astype(jnp.bfloat16),
    )


def row_table(length):
    cosine, sine = dft_parts(length)
    return jnp.stack([cosine, -sine])


def column_table(length, direction):
    cosine, sine = dft_parts(length)
    upper = jnp.stack([cosine, direction * sine], axis=1)
    lower = jnp.stack([-direction * sine, cosine], axis=1)
    return jnp.stack([upper, lower])


def layer_norm(values):
    centre = jnp.mean(values, axis=-1, keepdims=True)
    centred = values - centre
    variance = jnp.mean(centred * centred, axis=-1, keepdims=True)
    rstd_value = lax.rsqrt(variance + EPS)
    return (centred * rstd_value, rstd_value)


def norm_backward(upstream, normed, rstd_value, gain):
    scaled = upstream * gain
    result = (
        scaled
        - jnp.mean(scaled, axis=-1, keepdims=True)
        - normed * jnp.mean(scaled * normed, axis=-1, keepdims=True)
    ) * rstd_value
    lead = tuple(range(upstream.ndim - 1))
    return (result, jnp.sum(upstream * normed, axis=lead))


def apply_filter(spectrum, filter_weight, direction):
    real_part = spectrum[0].astype(jnp.float32)
    imag_part = spectrum[1].astype(jnp.float32)
    kernel_real = filter_weight[0].astype(jnp.float32)
    kernel_imag = direction * filter_weight[1].astype(jnp.float32)
    return jnp.stack(
        [
            kernel_real * real_part - kernel_imag * imag_part,
            kernel_real * imag_part + kernel_imag * real_part,
        ]
    )


def exact_gelu(values):
    return jax.nn.gelu(values, approximate=False)


def spectral(values, filter_weight, direction, early=None, late=None):
    width = values.shape[2]
    rows_tab = row_table(width)
    rows = jnp.einsum(
        "pkw,bhwc->pbhkc", rows_tab, values, preferred_element_type=jnp.float32
    ).astype(jnp.bfloat16)
    columns = lax.all_to_all(rows, "space", split_axis=3, concat_axis=2, tiled=True)
    held = None
    if early is not None:
        columns, held = lax.optimization_barrier((columns, early()))
    height = columns.shape[2]
    spectrum = jnp.einsum(
        "qmph,pbhkc->qbmkc", column_table(height, 1), columns, preferred_element_type=jnp.float32
    ).astype(jnp.bfloat16)
    weighted = apply_filter(spectrum, filter_weight[:, None], direction).astype(jnp.bfloat16)
    returned = jnp.einsum(
        "qmph,pbhkc->qbmkc", column_table(height, -1), weighted, preferred_element_type=jnp.float32
    ).astype(jnp.bfloat16)
    back_rows = lax.all_to_all(returned, "space", split_axis=2, concat_axis=3, tiled=True)
    tail = None
    if late is not None:
        back_rows, tail = lax.optimization_barrier((back_rows, late(spectrum)))
    output = jnp.einsum("pkw,pbhkc->bhwc", rows_tab, back_rows, preferred_element_type=jnp.float32)
    return (output, spectrum, held, tail)


def body(noisy_tokens, grad_out, filter_weight, weight_in, weight_out, gain_one, gain_two):
    batch, rows_dev, width, chans = noisy_tokens.shape
    inputs = noisy_tokens.astype(jnp.float32)
    normed_one, rstd_one = layer_norm(inputs)
    mixed_in = (normed_one * gain_one).astype(jnp.bfloat16)
    spatial, spectrum, _, _ = spectral(mixed_in, filter_weight, 1)
    normed_two, rstd_two = layer_norm(spatial)
    mlp_in = (normed_two * gain_two).astype(jnp.bfloat16).reshape(-1, chans)
    preact = jnp.dot(mlp_in, weight_in, preferred_element_type=jnp.float32)
    activated = exact_gelu(preact).astype(jnp.bfloat16)
    mlp_out = jnp.dot(activated, weight_out, preferred_element_type=jnp.float32)
    block_out = (inputs + mlp_out.reshape(inputs.shape)).astype(jnp.bfloat16)
    upstream = grad_out.reshape(-1, chans)
    grad_act = jnp.dot(upstream, weight_out.T, preferred_element_type=jnp.float32)
    grad_pre = jax.vjp(exact_gelu, preact)[1](grad_act)[0].astype(jnp.bfloat16)
    sum_out_t = jnp.dot(upstream.T, activated, preferred_element_type=jnp.float32)
    sum_in = jnp.dot(mlp_in.T, grad_pre, preferred_element_type=jnp.float32)
    grad_mlp = jnp.dot(grad_pre, weight_in.T, preferred_element_type=jnp.float32).reshape(
        inputs.shape
    )
    grad_spatial, sum_gain_two = norm_backward(grad_mlp, normed_two, rstd_two, gain_two)
    total_tokens = batch * lax.axis_size("copy") * rows_dev * lax.axis_size("space") * width
    factor = 1.0 / math.sqrt(total_tokens)
    n_copy, n_space = lax.axis_size("copy"), lax.axis_size("space")
    lanes = sum_in.shape[1]
    radices, axes = _split_axes(n_copy, n_space)
    row_div = 16 * math.prod(r for r, a in zip(radices, axes) if a == 0)
    extra = -(-(2 * sum_in.shape[0] + 1) // row_div) * row_div - 2 * sum_in.shape[0]

    def weight_sums():
        gains_block = jnp.pad(
            sum_gain_two[None, :], ((0, extra - 1), (0, lanes - sum_gain_two.shape[0]))
        )
        return all_sum([sum_in, sum_out_t, gains_block], n_copy, n_space, factor)

    def filter_grad(adjoint):
        spec_f = spectrum.astype(jnp.float32)
        adj_f = adjoint.astype(jnp.float32)
        filter_terms = jnp.stack(
            [
                jnp.sum(adj_f[0] * spec_f[0] + adj_f[1] * spec_f[1], axis=0),
                jnp.sum(adj_f[1] * spec_f[0] - adj_f[0] * spec_f[1], axis=0),
            ]
        )
        fshape = filter_terms.shape
        return filter_sum(
            filter_terms.astype(jnp.bfloat16).reshape(
                fshape[0] * fshape[1], fshape[2] * fshape[3]
            )
        ).reshape(fshape)

    back_spatial, _, total, grad_filter = spectral(
        grad_spatial.astype(jnp.bfloat16), filter_weight, -1, weight_sums, filter_grad
    )
    grad_normed, sum_gain_one = norm_backward(back_spatial, normed_one, rstd_one, gain_one)
    grad_tokens = (grad_out.astype(jnp.float32) + grad_normed).astype(jnp.bfloat16)
    gain_one_sum = tree_sum(sum_gain_one.reshape(1, -1), n_copy, n_space).reshape(-1)
    return (
        block_out,
        grad_tokens,
        grad_filter,
        total[: sum_in.shape[0]],
        total[sum_in.shape[0] : 2 * sum_in.shape[0]].T,
        gain_one_sum * factor,
        total[2 * sum_in.shape[0], : sum_gain_two.shape[0]].astype(jnp.float32),
    )


def solution(mesh):
    return jax.shard_map(
        body,
        mesh=mesh,
        in_specs=(
            P("copy", "space", None, None),
            P("copy", "space", None, None),
            P(None, None, "space", None),
            P(),
            P(),
            P(),
            P(),
        ),
        out_specs=(
            P("copy", "space", None, None),
            P("copy", "space", None, None),
            P(None, None, "space", None),
            P(),
            P(),
            P(),
            P(),
        ),
        check_vma=False,
    )
```

```python
import functools
import math

import jax
import jax.numpy as jnp
from jax import lax
from jax.experimental import pallas as pl
from jax.experimental.pallas import tpu as pltpu
from jax.sharding import PartitionSpec as P

MESH = pl.DeviceIdType.MESH

EPS = 1e-06


def _filter_sum_kernel(rows, x_ref, o_ref, half_in, part, other, full_in, sems):
    me_c = lax.axis_index("copy")
    me_s = lax.axis_index("space")
    core = me_c % 2
    hi = me_c // 2
    mate = (me_c + 1 - 2 * core, me_s)
    far = (me_c + 2 - 4 * hi, me_s)
    half = rows // 2
    barrier = pltpu.get_barrier_semaphore()
    pl.semaphore_signal(barrier, inc=1, device_id=mate, device_id_type=MESH)
    pl.semaphore_signal(barrier, inc=1, device_id=far, device_id_type=MESH)
    pl.semaphore_wait(barrier, 2)
    mine = pl.ds(pl.multiple_of(core * half, 8), half)
    theirs = pl.ds(pl.multiple_of((1 - core) * half, 8), half)
    c1 = pltpu.make_async_remote_copy(
        src_ref=x_ref.at[theirs], dst_ref=half_in, send_sem=sems.at[0], recv_sem=sems.at[1],
        device_id=mate, device_id_type=MESH)
    c1.start()
    c1.wait_recv()
    own = x_ref[mine, :].astype(jnp.float32)
    got = half_in[...].astype(jnp.float32)
    first = jnp.where(core == 0, own, got)
    second = jnp.where(core == 0, got, own)
    part[...] = (first + second).astype(jnp.bfloat16)
    c2 = pltpu.make_async_remote_copy(
        src_ref=part, dst_ref=other, send_sem=sems.at[2], recv_sem=sems.at[3],
        device_id=far, device_id_type=MESH)
    c2.start()
    c2.wait_recv()
    mine_p = part[...].astype(jnp.float32)
    got_p = other[...].astype(jnp.float32)
    total = jnp.where(hi == 0, mine_p + got_p, got_p + mine_p)
    o_ref[mine, :] = total
    c3 = pltpu.make_async_remote_copy(
        src_ref=o_ref.at[mine], dst_ref=full_in, send_sem=sems.at[4], recv_sem=sems.at[5],
        device_id=mate, device_id_type=MESH)
    c3.start()
    c3.wait_recv()
    o_ref[theirs, :] = full_in[...]
    c1.wait_send()
    c2.wait_send()
    c3.wait_send()


def filter_sum(x):
    rows, cols = x.shape
    half = rows // 2
    return pl.pallas_call(
        functools.partial(_filter_sum_kernel, rows),
        out_shape=jax.ShapeDtypeStruct((rows, cols), jnp.float32),
        in_specs=[pl.BlockSpec(memory_space=pltpu.VMEM)],
        out_specs=pl.BlockSpec(memory_space=pltpu.VMEM),
        scratch_shapes=[
            pltpu.VMEM((half, cols), x.dtype),
            pltpu.VMEM((half, cols), jnp.bfloat16),
            pltpu.VMEM((half, cols), jnp.bfloat16),
            pltpu.VMEM((half, cols), jnp.float32),
            pltpu.SemaphoreType.DMA((6,)),
        ],
        compiler_params=pltpu.CompilerParams(
            collective_id=1, has_side_effects=True, vmem_limit_bytes=48 * 1024 * 1024
        ),
        cost_estimate=pl.CostEstimate(
            flops=2 * rows * cols, transcendentals=0, bytes_accessed=10 * rows * cols
        ),
    )(x)


def _digit_orders(n_copy, n_space):
    c0, xh = ("copy", 0), ("copy", 1)
    if (n_copy, n_space) == (4, 64):
        xl, z1, z2, z4, y1, y2 = [("space", b) for b in range(6)]
        first = [[c0], [xl, z1], [y1, z2], [y2, xh], [z4]]
        second = [[c0], [y1, y2], [xl, z1], [z2, xh], [z4]]
        return first, second
    sb = [("space", b) for b in range(n_space.bit_length() - 1)]
    cb = [("copy", b) for b in range(1, n_copy.bit_length() - 1)]
    rest = sb + cb
    first = [[c0]] + [rest[i : i + 2] for i in range(0, len(rest), 2)]
    rest = rest[::-1]
    second = [[c0]] + [rest[i : i + 2] for i in range(0, len(rest), 2)]
    return first, second


def _tree_order(n_copy, n_space):
    if (n_copy, n_space) == (4, 64):
        xl, z1, z2, z4, y1, y2 = [("space", b) for b in range(6)]
        return [[("copy", 0), ("copy", 1), xl], [z1, z2, z4], [y1, y2]]
    return _digit_orders(n_copy, n_space)[0]


def _plan(n_copy, n_space, split=True):
    orders = _digit_orders(n_copy, n_space)
    if not split:
        orders = (_tree_order(n_copy, n_space),) * 2
    me_c = lax.axis_index("copy")
    me_s = lax.axis_index("space")
    core = me_c % 2
    plan = []
    for s in range(len(orders[0])):
        per_core = []
        for order in orders:
            digit = order[s]
            radix = 1 << len(digit)
            bits = []
            for axis, b in digit:
                idx = me_c if axis == "copy" else me_s
                bits.append((idx // (1 << b)) % 2)
            v = sum(bit << i for i, bit in enumerate(bits))
            peers = []
            for d in range(1, radix):
                u = (v + d) % radix
                pc, ps = me_c, me_s
                for i, (axis, b) in enumerate(digit):
                    delta = ((u // (1 << i)) % 2 - bits[i]) * (1 << b)
                    if axis == "copy":
                        pc = pc + delta
                    else:
                        ps = ps + delta
                peers.append((pc, ps))
            per_core.append((radix, peers, v))
        (r0, p0, v0), (r1, p1, v1) = per_core
        assert r0 == r1
        peers = [
            ((1 - core) * a[0] + core * b[0], (1 - core) * a[1] + core * b[1])
            for a, b in zip(p0, p1)
        ]
        plan.append((r0, peers, (1 - core) * v0 + core * v1))
    return plan


def _split_axes(n_copy, n_space):
    radices = [1 << len(d) for d in _digit_orders(n_copy, n_space)[0]]
    if (n_copy, n_space) == (4, 64):
        return radices, [0, 0, 0, 1, 0]
    return radices, [0] * len(radices)


def _all_sum_kernel(n_copy, n_space, scale, a_ref, b_ref, c_ref, o_ref, acc, send, *rest):
    plan = _plan(n_copy, n_space)
    _, axes = _split_axes(n_copy, n_space)
    steps = len(plan)
    recv = rest[:steps]
    rs_send, rs_recv, ag_send, ag_recv, local = rest[steps:]
    rows, cols = acc.shape
    at = 0
    loads = []
    for i, part_ref in enumerate((a_ref, b_ref, c_ref)):
        n = part_ref.shape[0]
        cp = pltpu.make_async_copy(part_ref, acc.at[pl.ds(at, n)], local.at[i])
        cp.start()
        loads.append(cp)
        at += n
    barrier = pltpu.get_barrier_semaphore()
    count = 0
    for radix, peers, _ in plan:
        for peer in peers:
            pl.semaphore_signal(barrier, inc=1, device_id=peer, device_id_type=MESH)
            count += 1
    for cp in loads:
        cp.wait()
    pl.semaphore_wait(barrier, count)

    def window(r0, rl, c0, cl):
        return (pl.ds(pl.multiple_of(r0, 16), rl), pl.ds(pl.multiple_of(c0, 128), cl))

    pending = []
    box = [0, rows, 0, cols]
    slot = 0
    for s, (radix, peers, v) in enumerate(plan):
        r0, rl, c0, cl = box
        if axes[s] == 0:
            part = rl // radix

            def piece(u, r0=r0, c0=c0, cl=cl, part=part):
                return window(r0 + u * part, part, c0, cl)
        else:
            part = cl // radix

            def piece(u, r0=r0, rl=rl, c0=c0, part=part):
                return window(r0, rl, c0 + u * part, part)
        descs = []
        for d, peer in enumerate(peers, start=1):
            u = (v + d) % radix
            w = piece(u)
            send[w] = acc[w].astype(jnp.bfloat16)
            c = pltpu.make_async_remote_copy(
                src_ref=send.at[w],
                dst_ref=recv[s].at[d - 1],
                send_sem=rs_send.at[slot + d - 1],
                recv_sem=rs_recv.at[slot + d - 1],
                device_id=peer,
                device_id_type=MESH,
            )
            c.start()
            descs.append(c)
        keep = piece(v)
        total = acc[keep]
        for d, c in enumerate(descs, start=1):
            c.wait_recv()
            total = total + recv[s][d - 1].astype(jnp.float32)
        acc[keep] = total
        pending += descs
        slot += radix - 1
        if axes[s] == 0:
            box = [r0 + v * part, part, c0, cl]
        else:
            box = [r0, rl, c0 + v * part, part]
    r0, rl, c0, cl = box
    mine = window(r0, rl, c0, cl)
    o_ref[mine] = (acc[mine] * scale).astype(o_ref.dtype)
    for s in reversed(range(steps)):
        radix, peers, v = plan[s]
        slot -= radix - 1
        r0, rl, c0, cl = box
        if axes[s] == 0:
            first = r0 - v * rl

            def piece(u, first=first, rl=rl, c0=c0, cl=cl):
                return window(first + u * rl, rl, c0, cl)

            box = [first, radix * rl, c0, cl]
        else:
            first = c0 - v * cl

            def piece(u, first=first, r0=r0, rl=rl, cl=cl):
                return window(r0, rl, first + u * cl, cl)

            box = [r0, rl, first, radix * cl]
        mine = piece(v)
        descs = []
        for d, peer in enumerate(peers, start=1):
            c = pltpu.make_async_remote_copy(
                src_ref=o_ref.at[mine],
                dst_ref=o_ref.at[mine],
                send_sem=ag_send.at[slot + d - 1],
                recv_sem=ag_recv.at[slot + d - 1],
                device_id=peer,
                device_id_type=MESH,
            )
            c.start()
            descs.append(c)
        for d, peer in enumerate(peers, start=1):
            theirs = piece((v - d + radix) % radix)
            pltpu.make_async_remote_copy(
                src_ref=o_ref.at[theirs],
                dst_ref=o_ref.at[theirs],
                send_sem=ag_send.at[slot + d - 1],
                recv_sem=ag_recv.at[slot + d - 1],
                device_id=peer,
                device_id_type=MESH,
            ).wait_recv()
        pending += descs
    for c in pending:
        c.wait_send()


def all_sum(parts, n_copy, n_space, scale):
    rows = sum(p.shape[0] for p in parts)
    cols = parts[0].shape[1]
    radices, axes = _split_axes(n_copy, n_space)
    recv = []
    rl, cl = rows, cols
    for r, a in zip(radices, axes):
        if a == 0:
            rl //= r
        else:
            cl //= r
        recv.append(pltpu.VMEM((r - 1, rl, cl), jnp.bfloat16))
    links = sum(r - 1 for r in radices)
    return pl.pallas_call(
        functools.partial(_all_sum_kernel, n_copy, n_space, scale),
        out_shape=jax.ShapeDtypeStruct((rows, cols), jnp.bfloat16),
        in_specs=[pl.BlockSpec(memory_space=pltpu.VMEM)] * len(parts),
        out_specs=pl.BlockSpec(memory_space=pltpu.VMEM),
        scratch_shapes=[
            pltpu.VMEM((rows, cols), jnp.float32),
            pltpu.VMEM((rows, cols), jnp.bfloat16),
        ]
        + recv
        + [pltpu.SemaphoreType.DMA((links,)) for _ in range(4)]
        + [pltpu.SemaphoreType.DMA((len(parts),))],
        compiler_params=pltpu.CompilerParams(
            collective_id=3, has_side_effects=True, vmem_limit_bytes=56 * 1024 * 1024
        ),
        cost_estimate=pl.CostEstimate(
            flops=rows * cols, transcendentals=0, bytes_accessed=12 * rows * cols
        ),
    )(*parts)


def _tree_sum_kernel(n_copy, n_space, x_ref, o_ref, *rest):
    plan = _plan(n_copy, n_space, split=False)
    steps = len(plan)
    slots = rest[:steps]
    send_sem, recv_sem = rest[steps:]
    barrier = pltpu.get_barrier_semaphore()
    count = 0
    for _, peers, _ in plan:
        for peer in peers:
            pl.semaphore_signal(barrier, inc=1, device_id=peer, device_id_type=MESH)
            count += 1
    pl.semaphore_wait(barrier, count)
    acc = x_ref[...]
    pending = []
    slot = 0
    for s, (radix, peers, v) in enumerate(plan):
        slots[s][0] = acc
        descs = []
        for d, peer in enumerate(peers, start=1):
            c = pltpu.make_async_remote_copy(
                src_ref=slots[s].at[0],
                dst_ref=slots[s].at[d],
                send_sem=send_sem.at[slot + d - 1],
                recv_sem=recv_sem.at[slot + d - 1],
                device_id=peer,
                device_id_type=MESH,
            )
            c.start()
            descs.append(c)
        for c in descs:
            c.wait_recv()
        total = slots[s][(v + radix) % radix]
        for u in range(1, radix):
            total = total + slots[s][(v - u + radix) % radix]
        acc = total
        pending += descs
        slot += radix - 1
    for c in pending:
        c.wait_send()
    o_ref[...] = acc


def tree_sum(x, n_copy, n_space):
    radices = [1 << len(d) for d in _tree_order(n_copy, n_space)]
    links = sum(r - 1 for r in radices)
    return pl.pallas_call(
        functools.partial(_tree_sum_kernel, n_copy, n_space),
        out_shape=jax.ShapeDtypeStruct(x.shape, jnp.float32),
        in_specs=[pl.BlockSpec(memory_space=pltpu.VMEM)],
        out_specs=pl.BlockSpec(memory_space=pltpu.VMEM),
        scratch_shapes=[pltpu.VMEM((r,) + x.shape, jnp.float32) for r in radices]
        + [pltpu.SemaphoreType.DMA((links,)), pltpu.SemaphoreType.DMA((links,))],
        compiler_params=pltpu.CompilerParams(collective_id=2, has_side_effects=True),
        cost_estimate=pl.CostEstimate(
            flops=links * x.size, transcendentals=0, bytes_accessed=8 * links * x.size
        ),
    )(x)


def dft_parts(length):
    index = jnp.arange(length, dtype=jnp.int32)
    phase = index[:, None] * index[None, :] % length
    angle = phase.astype(jnp.float32) * (2.0 * math.pi / length)
    factor = 1.0 / math.sqrt(length)
    return (
        (jnp.cos(angle) * factor).astype(jnp.bfloat16),
        (jnp.sin(angle) * factor).astype(jnp.bfloat16),
    )


def row_table(length):
    cosine, sine = dft_parts(length)
    return jnp.stack([cosine, -sine])


def column_table(length, direction):
    cosine, sine = dft_parts(length)
    upper = jnp.stack([cosine, direction * sine], axis=1)
    lower = jnp.stack([-direction * sine, cosine], axis=1)
    return jnp.stack([upper, lower])


def layer_norm(values):
    centre = jnp.mean(values, axis=-1, keepdims=True)
    centred = values - centre
    variance = jnp.mean(centred * centred, axis=-1, keepdims=True)
    rstd_value = lax.rsqrt(variance + EPS)
    return (centred * rstd_value, rstd_value)


def norm_backward(upstream, normed, rstd_value, gain):
    scaled = upstream * gain
    result = (
        scaled
        - jnp.mean(scaled, axis=-1, keepdims=True)
        - normed * jnp.mean(scaled * normed, axis=-1, keepdims=True)
    ) * rstd_value
    lead = tuple(range(upstream.ndim - 1))
    return (result, jnp.sum(upstream * normed, axis=lead))


def apply_filter(spectrum, filter_weight, direction):
    real_part = spectrum[0].astype(jnp.float32)
    imag_part = spectrum[1].astype(jnp.float32)
    kernel_real = filter_weight[0].astype(jnp.float32)
    kernel_imag = direction * filter_weight[1].astype(jnp.float32)
    return jnp.stack(
        [
            kernel_real * real_part - kernel_imag * imag_part,
            kernel_real * imag_part + kernel_imag * real_part,
        ]
    )


def exact_gelu(values):
    return jax.nn.gelu(values, approximate=False)


def spectral(values, filter_weight, direction, early=None, late=None):
    width = values.shape[2]
    rows_tab = row_table(width)
    rows = jnp.einsum(
        "pkw,bhwc->pbhkc", rows_tab, values, preferred_element_type=jnp.float32
    ).astype(jnp.bfloat16)
    columns = lax.all_to_all(rows, "space", split_axis=3, concat_axis=2, tiled=True)
    held = None
    if early is not None:
        columns, held = lax.optimization_barrier((columns, early()))
    height = columns.shape[2]
    spectrum = jnp.einsum(
        "qmph,pbhkc->qbmkc", column_table(height, 1), columns, preferred_element_type=jnp.float32
    ).astype(jnp.bfloat16)
    weighted = apply_filter(spectrum, filter_weight[:, None], direction).astype(jnp.bfloat16)
    returned = jnp.einsum(
        "qmph,pbhkc->qbmkc", column_table(height, -1), weighted, preferred_element_type=jnp.float32
    ).astype(jnp.bfloat16)
    back_rows = lax.all_to_all(returned, "space", split_axis=2, concat_axis=3, tiled=True)
    tail = None
    if late is not None:
        back_rows, tail = lax.optimization_barrier((back_rows, late(spectrum)))
    output = jnp.einsum("pkw,pbhkc->bhwc", rows_tab, back_rows, preferred_element_type=jnp.float32)
    return (output, spectrum, held, tail)


def body(noisy_tokens, grad_out, filter_weight, weight_in, weight_out, gain_one, gain_two):
    batch, rows_dev, width, chans = noisy_tokens.shape
    inputs = noisy_tokens.astype(jnp.float32)
    normed_one, rstd_one = layer_norm(inputs)
    mixed_in = (normed_one * gain_one).astype(jnp.bfloat16)
    spatial, spectrum, _, _ = spectral(mixed_in, filter_weight, 1)
    normed_two, rstd_two = layer_norm(spatial)
    mlp_in = (normed_two * gain_two).astype(jnp.bfloat16).reshape(-1, chans)
    preact = jnp.dot(mlp_in, weight_in, preferred_element_type=jnp.float32)
    activated = exact_gelu(preact).astype(jnp.bfloat16)
    mlp_out = jnp.dot(activated, weight_out, preferred_element_type=jnp.float32)
    block_out = (inputs + mlp_out.reshape(inputs.shape)).astype(jnp.bfloat16)
    upstream = grad_out.reshape(-1, chans)
    grad_act = jnp.dot(upstream, weight_out.T, preferred_element_type=jnp.float32)
    grad_pre = jax.vjp(exact_gelu, preact)[1](grad_act)[0].astype(jnp.bfloat16)
    sum_out_t = jnp.dot(upstream.T, activated, preferred_element_type=jnp.float32)
    sum_in = jnp.dot(mlp_in.T, grad_pre, preferred_element_type=jnp.float32)
    grad_mlp = jnp.dot(grad_pre, weight_in.T, preferred_element_type=jnp.float32).reshape(
        inputs.shape
    )
    grad_spatial, sum_gain_two = norm_backward(grad_mlp, normed_two, rstd_two, gain_two)
    total_tokens = batch * lax.axis_size("copy") * rows_dev * lax.axis_size("space") * width
    factor = 1.0 / math.sqrt(total_tokens)
    n_copy, n_space = lax.axis_size("copy"), lax.axis_size("space")
    lanes = sum_in.shape[1]
    radices, axes = _split_axes(n_copy, n_space)
    row_div = 16 * math.prod(r for r, a in zip(radices, axes) if a == 0)
    extra = -(-(2 * sum_in.shape[0] + 1) // row_div) * row_div - 2 * sum_in.shape[0]

    def weight_sums():
        gains_block = jnp.pad(
            sum_gain_two[None, :], ((0, extra - 1), (0, lanes - sum_gain_two.shape[0]))
        )
        return all_sum([sum_in, sum_out_t, gains_block], n_copy, n_space, factor)

    def filter_grad(adjoint):
        spec_f = spectrum.astype(jnp.float32)
        adj_f = adjoint.astype(jnp.float32)
        filter_terms = jnp.stack(
            [
                jnp.sum(adj_f[0] * spec_f[0] + adj_f[1] * spec_f[1], axis=0),
                jnp.sum(adj_f[1] * spec_f[0] - adj_f[0] * spec_f[1], axis=0),
            ]
        )
        fshape = filter_terms.shape
        return filter_sum(
            filter_terms.astype(jnp.bfloat16).reshape(
                fshape[0] * fshape[1], fshape[2] * fshape[3]
            )
        ).reshape(fshape)

    back_spatial, _, total, grad_filter = spectral(
        grad_spatial.astype(jnp.bfloat16), filter_weight, -1, weight_sums, filter_grad
    )
    grad_normed, sum_gain_one = norm_backward(back_spatial, normed_one, rstd_one, gain_one)
    grad_tokens = (grad_out.astype(jnp.float32) + grad_normed).astype(jnp.bfloat16)
    gain_one_sum = tree_sum(sum_gain_one.reshape(1, -1), n_copy, n_space).reshape(-1)
    return (
        block_out,
        grad_tokens,
        grad_filter,
        total[: sum_in.shape[0]],
        total[sum_in.shape[0] : 2 * sum_in.shape[0]].T,
        gain_one_sum * factor,
        total[2 * sum_in.shape[0], : sum_gain_two.shape[0]].astype(jnp.float32),
    )


def solution(mesh):
    return jax.shard_map(
        body,
        mesh=mesh,
        in_specs=(
            P("copy", "space", None, None),
            P("copy", "space", None, None),
            P(None, None, "space", None),
            P(),
            P(),
            P(),
            P(),
        ),
        out_specs=(
            P("copy", "space", None, None),
            P("copy", "space", None, None),
            P(None, None, "space", None),
            P(),
            P(),
            P(),
            P(),
        ),
        check_vma=False,
    )
```

```python
import functools
import math

import jax
import jax.numpy as jnp
from jax import lax
from jax.experimental import pallas as pl
from jax.experimental.pallas import tpu as pltpu
from jax.sharding import PartitionSpec as P

MESH = pl.DeviceIdType.MESH

EPS = 1e-06


def _filter_sum_kernel(rows, x_ref, o_ref, half_in, part, other, full_in, sems):
    me_c = lax.axis_index("copy")
    me_s = lax.axis_index("space")
    core = me_c % 2
    hi = me_c // 2
    mate = (me_c + 1 - 2 * core, me_s)
    far = (me_c + 2 - 4 * hi, me_s)
    half = rows // 2
    barrier = pltpu.get_barrier_semaphore()
    pl.semaphore_signal(barrier, inc=1, device_id=mate, device_id_type=MESH)
    pl.semaphore_signal(barrier, inc=1, device_id=far, device_id_type=MESH)
    pl.semaphore_wait(barrier, 2)
    mine = pl.ds(pl.multiple_of(core * half, 8), half)
    theirs = pl.ds(pl.multiple_of((1 - core) * half, 8), half)
    c1 = pltpu.make_async_remote_copy(
        src_ref=x_ref.at[theirs], dst_ref=half_in, send_sem=sems.at[0], recv_sem=sems.at[1],
        device_id=mate, device_id_type=MESH)
    c1.start()
    c1.wait_recv()
    own = x_ref[mine, :].astype(jnp.float32)
    got = half_in[...].astype(jnp.float32)
    first = jnp.where(core == 0, own, got)
    second = jnp.where(core == 0, got, own)
    part[...] = (first + second).astype(jnp.bfloat16)
    c2 = pltpu.make_async_remote_copy(
        src_ref=part, dst_ref=other, send_sem=sems.at[2], recv_sem=sems.at[3],
        device_id=far, device_id_type=MESH)
    c2.start()
    c2.wait_recv()
    mine_p = part[...].astype(jnp.float32)
    got_p = other[...].astype(jnp.float32)
    total = jnp.where(hi == 0, mine_p + got_p, got_p + mine_p)
    o_ref[mine, :] = total
    c3 = pltpu.make_async_remote_copy(
        src_ref=o_ref.at[mine], dst_ref=full_in, send_sem=sems.at[4], recv_sem=sems.at[5],
        device_id=mate, device_id_type=MESH)
    c3.start()
    c3.wait_recv()
    o_ref[theirs, :] = full_in[...]
    c1.wait_send()
    c2.wait_send()
    c3.wait_send()


def filter_sum(x):
    rows, cols = x.shape
    half = rows // 2
    return pl.pallas_call(
        functools.partial(_filter_sum_kernel, rows),
        out_shape=jax.ShapeDtypeStruct((rows, cols), jnp.float32),
        in_specs=[pl.BlockSpec(memory_space=pltpu.VMEM)],
        out_specs=pl.BlockSpec(memory_space=pltpu.VMEM),
        scratch_shapes=[
            pltpu.VMEM((half, cols), x.dtype),
            pltpu.VMEM((half, cols), jnp.bfloat16),
            pltpu.VMEM((half, cols), jnp.bfloat16),
            pltpu.VMEM((half, cols), jnp.float32),
            pltpu.SemaphoreType.DMA((6,)),
        ],
        compiler_params=pltpu.CompilerParams(
            collective_id=1, has_side_effects=True, vmem_limit_bytes=48 * 1024 * 1024
        ),
        cost_estimate=pl.CostEstimate(
            flops=2 * rows * cols, transcendentals=0, bytes_accessed=10 * rows * cols
        ),
    )(x)


def _digit_orders(n_copy, n_space):
    c0, xh = ("copy", 0), ("copy", 1)
    if (n_copy, n_space) == (4, 64):
        xl, z1, z2, z4, y1, y2 = [("space", b) for b in range(6)]
        first = [[c0], [xl, z1], [y1, z2], [y2, xh, z4]]
        second = [[c0], [y1, y2], [xl, z1], [z2, xh, z4]]
        return first, second
    sb = [("space", b) for b in range(n_space.bit_length() - 1)]
    cb = [("copy", b) for b in range(1, n_copy.bit_length() - 1)]
    rest = sb + cb
    first = [[c0]] + [rest[i : i + 2] for i in range(0, len(rest), 2)]
    rest = rest[::-1]
    second = [[c0]] + [rest[i : i + 2] for i in range(0, len(rest), 2)]
    return first, second


def _tree_order(n_copy, n_space):
    if (n_copy, n_space) == (4, 64):
        xl, z1, z2, z4, y1, y2 = [("space", b) for b in range(6)]
        return [[("copy", 0), ("copy", 1), xl], [z1, z2, z4], [y1, y2]]
    return _digit_orders(n_copy, n_space)[0]


def _plan(n_copy, n_space, split=True):
    orders = _digit_orders(n_copy, n_space)
    if not split:
        orders = (_tree_order(n_copy, n_space),) * 2
    me_c = lax.axis_index("copy")
    me_s = lax.axis_index("space")
    core = me_c % 2
    plan = []
    for s in range(len(orders[0])):
        per_core = []
        for order in orders:
            digit = order[s]
            radix = 1 << len(digit)
            bits = []
            for axis, b in digit:
                idx = me_c if axis == "copy" else me_s
                bits.append((idx // (1 << b)) % 2)
            v = sum(bit << i for i, bit in enumerate(bits))
            peers = []
            for d in range(1, radix):
                u = (v + d) % radix
                pc, ps = me_c, me_s
                for i, (axis, b) in enumerate(digit):
                    delta = ((u // (1 << i)) % 2 - bits[i]) * (1 << b)
                    if axis == "copy":
                        pc = pc + delta
                    else:
                        ps = ps + delta
                peers.append((pc, ps))
            per_core.append((radix, peers, v))
        (r0, p0, v0), (r1, p1, v1) = per_core
        assert r0 == r1
        peers = [
            ((1 - core) * a[0] + core * b[0], (1 - core) * a[1] + core * b[1])
            for a, b in zip(p0, p1)
        ]
        plan.append((r0, peers, (1 - core) * v0 + core * v1))
    return plan


def _split_axes(n_copy, n_space):
    radices = [1 << len(d) for d in _digit_orders(n_copy, n_space)[0]]
    if (n_copy, n_space) == (4, 64):
        return radices, [0, 0, 1, 0]
    return radices, [0] * len(radices)


def _all_sum_kernel(n_copy, n_space, scale, a_ref, b_ref, c_ref, o_ref, acc, send, *rest):
    plan = _plan(n_copy, n_space)
    _, axes = _split_axes(n_copy, n_space)
    steps = len(plan)
    recv = rest[:steps]
    rs_send, rs_recv, ag_send, ag_recv, local = rest[steps:]
    rows, cols = acc.shape
    at = 0
    loads = []
    for i, part_ref in enumerate((a_ref, b_ref, c_ref)):
        n = part_ref.shape[0]
        cp = pltpu.make_async_copy(part_ref, acc.at[pl.ds(at, n)], local.at[i])
        cp.start()
        loads.append(cp)
        at += n
    barrier = pltpu.get_barrier_semaphore()
    count = 0
    for radix, peers, _ in plan:
        for peer in peers:
            pl.semaphore_signal(barrier, inc=1, device_id=peer, device_id_type=MESH)
            count += 1
    for cp in loads:
        cp.wait()
    pl.semaphore_wait(barrier, count)

    def window(r0, rl, c0, cl):
        return (pl.ds(pl.multiple_of(r0, 16), rl), pl.ds(pl.multiple_of(c0, 128), cl))

    pending = []
    box = [0, rows, 0, cols]
    slot = 0
    for s, (radix, peers, v) in enumerate(plan):
        r0, rl, c0, cl = box
        if axes[s] == 0:
            part = rl // radix

            def piece(u, r0=r0, c0=c0, cl=cl, part=part):
                return window(r0 + u * part, part, c0, cl)
        else:
            part = cl // radix

            def piece(u, r0=r0, rl=rl, c0=c0, part=part):
                return window(r0, rl, c0 + u * part, part)
        descs = []
        for d, peer in enumerate(peers, start=1):
            u = (v + d) % radix
            w = piece(u)
            send[w] = acc[w].astype(jnp.bfloat16)
            c = pltpu.make_async_remote_copy(
                src_ref=send.at[w],
                dst_ref=recv[s].at[d - 1],
                send_sem=rs_send.at[slot + d - 1],
                recv_sem=rs_recv.at[slot + d - 1],
                device_id=peer,
                device_id_type=MESH,
            )
            c.start()
            descs.append(c)
        keep = piece(v)
        total = acc[keep]
        for d, c in enumerate(descs, start=1):
            c.wait_recv()
            total = total + recv[s][d - 1].astype(jnp.float32)
        acc[keep] = total
        pending += descs
        slot += radix - 1
        if axes[s] == 0:
            box = [r0 + v * part, part, c0, cl]
        else:
            box = [r0, rl, c0 + v * part, part]
    r0, rl, c0, cl = box
    mine = window(r0, rl, c0, cl)
    o_ref[mine] = (acc[mine] * scale).astype(o_ref.dtype)
    for s in reversed(range(steps)):
        radix, peers, v = plan[s]
        slot -= radix - 1
        r0, rl, c0, cl = box
        if axes[s] == 0:
            first = r0 - v * rl

            def piece(u, first=first, rl=rl, c0=c0, cl=cl):
                return window(first + u * rl, rl, c0, cl)

            box = [first, radix * rl, c0, cl]
        else:
            first = c0 - v * cl

            def piece(u, first=first, r0=r0, rl=rl, cl=cl):
                return window(r0, rl, first + u * cl, cl)

            box = [r0, rl, first, radix * cl]
        mine = piece(v)
        descs = []
        for d, peer in enumerate(peers, start=1):
            c = pltpu.make_async_remote_copy(
                src_ref=o_ref.at[mine],
                dst_ref=o_ref.at[mine],
                send_sem=ag_send.at[slot + d - 1],
                recv_sem=ag_recv.at[slot + d - 1],
                device_id=peer,
                device_id_type=MESH,
            )
            c.start()
            descs.append(c)
        for d, peer in enumerate(peers, start=1):
            theirs = piece((v - d + radix) % radix)
            pltpu.make_async_remote_copy(
                src_ref=o_ref.at[theirs],
                dst_ref=o_ref.at[theirs],
                send_sem=ag_send.at[slot + d - 1],
                recv_sem=ag_recv.at[slot + d - 1],
                device_id=peer,
                device_id_type=MESH,
            ).wait_recv()
        pending += descs
    for c in pending:
        c.wait_send()


def all_sum(parts, n_copy, n_space, scale):
    rows = sum(p.shape[0] for p in parts)
    cols = parts[0].shape[1]
    radices, axes = _split_axes(n_copy, n_space)
    recv = []
    rl, cl = rows, cols
    for r, a in zip(radices, axes):
        if a == 0:
            rl //= r
        else:
            cl //= r
        recv.append(pltpu.VMEM((r - 1, rl, cl), jnp.bfloat16))
    links = sum(r - 1 for r in radices)
    return pl.pallas_call(
        functools.partial(_all_sum_kernel, n_copy, n_space, scale),
        out_shape=jax.ShapeDtypeStruct((rows, cols), jnp.bfloat16),
        in_specs=[pl.BlockSpec(memory_space=pltpu.VMEM)] * len(parts),
        out_specs=pl.BlockSpec(memory_space=pltpu.VMEM),
        scratch_shapes=[
            pltpu.VMEM((rows, cols), jnp.float32),
            pltpu.VMEM((rows, cols), jnp.bfloat16),
        ]
        + recv
        + [pltpu.SemaphoreType.DMA((links,)) for _ in range(4)]
        + [pltpu.SemaphoreType.DMA((len(parts),))],
        compiler_params=pltpu.CompilerParams(
            collective_id=3, has_side_effects=True, vmem_limit_bytes=56 * 1024 * 1024
        ),
        cost_estimate=pl.CostEstimate(
            flops=rows * cols, transcendentals=0, bytes_accessed=12 * rows * cols
        ),
    )(*parts)


def _tree_sum_kernel(n_copy, n_space, x_ref, o_ref, *rest):
    plan = _plan(n_copy, n_space, split=False)
    steps = len(plan)
    slots = rest[:steps]
    send_sem, recv_sem = rest[steps:]
    barrier = pltpu.get_barrier_semaphore()
    count = 0
    for _, peers, _ in plan:
        for peer in peers:
            pl.semaphore_signal(barrier, inc=1, device_id=peer, device_id_type=MESH)
            count += 1
    pl.semaphore_wait(barrier, count)
    acc = x_ref[...]
    pending = []
    slot = 0
    for s, (radix, peers, v) in enumerate(plan):
        slots[s][0] = acc
        descs = []
        for d, peer in enumerate(peers, start=1):
            c = pltpu.make_async_remote_copy(
                src_ref=slots[s].at[0],
                dst_ref=slots[s].at[d],
                send_sem=send_sem.at[slot + d - 1],
                recv_sem=recv_sem.at[slot + d - 1],
                device_id=peer,
                device_id_type=MESH,
            )
            c.start()
            descs.append(c)
        for c in descs:
            c.wait_recv()
        total = slots[s][(v + radix) % radix]
        for u in range(1, radix):
            total = total + slots[s][(v - u + radix) % radix]
        acc = total
        pending += descs
        slot += radix - 1
    for c in pending:
        c.wait_send()
    o_ref[...] = acc


def tree_sum(x, n_copy, n_space):
    radices = [1 << len(d) for d in _tree_order(n_copy, n_space)]
    links = sum(r - 1 for r in radices)
    return pl.pallas_call(
        functools.partial(_tree_sum_kernel, n_copy, n_space),
        out_shape=jax.ShapeDtypeStruct(x.shape, jnp.float32),
        in_specs=[pl.BlockSpec(memory_space=pltpu.VMEM)],
        out_specs=pl.BlockSpec(memory_space=pltpu.VMEM),
        scratch_shapes=[pltpu.VMEM((r,) + x.shape, jnp.float32) for r in radices]
        + [pltpu.SemaphoreType.DMA((links,)), pltpu.SemaphoreType.DMA((links,))],
        compiler_params=pltpu.CompilerParams(collective_id=2, has_side_effects=True),
        cost_estimate=pl.CostEstimate(
            flops=links * x.size, transcendentals=0, bytes_accessed=8 * links * x.size
        ),
    )(x)


def dft_parts(length):
    index = jnp.arange(length, dtype=jnp.int32)
    phase = index[:, None] * index[None, :] % length
    angle = phase.astype(jnp.float32) * (2.0 * math.pi / length)
    factor = 1.0 / math.sqrt(length)
    return (
        (jnp.cos(angle) * factor).astype(jnp.bfloat16),
        (jnp.sin(angle) * factor).astype(jnp.bfloat16),
    )


def row_table(length):
    cosine, sine = dft_parts(length)
    return jnp.stack([cosine, -sine])


def column_table(length, direction):
    cosine, sine = dft_parts(length)
    upper = jnp.stack([cosine, direction * sine], axis=1)
    lower = jnp.stack([-direction * sine, cosine], axis=1)
    return jnp.stack([upper, lower])


def layer_norm(values):
    centre = jnp.mean(values, axis=-1, keepdims=True)
    centred = values - centre
    variance = jnp.mean(centred * centred, axis=-1, keepdims=True)
    rstd_value = lax.rsqrt(variance + EPS)
    return (centred * rstd_value, rstd_value)


def norm_backward(upstream, normed, rstd_value, gain):
    scaled = upstream * gain
    result = (
        scaled
        - jnp.mean(scaled, axis=-1, keepdims=True)
        - normed * jnp.mean(scaled * normed, axis=-1, keepdims=True)
    ) * rstd_value
    lead = tuple(range(upstream.ndim - 1))
    return (result, jnp.sum(upstream * normed, axis=lead))


def apply_filter(spectrum, filter_weight, direction):
    real_part = spectrum[0].astype(jnp.float32)
    imag_part = spectrum[1].astype(jnp.float32)
    kernel_real = filter_weight[0].astype(jnp.float32)
    kernel_imag = direction * filter_weight[1].astype(jnp.float32)
    return jnp.stack(
        [
            kernel_real * real_part - kernel_imag * imag_part,
            kernel_real * imag_part + kernel_imag * real_part,
        ]
    )


def exact_gelu(values):
    return jax.nn.gelu(values, approximate=False)


def spectral(values, filter_weight, direction, early=None, late=None):
    width = values.shape[2]
    rows_tab = row_table(width)
    rows = jnp.einsum(
        "pkw,bhwc->pbhkc", rows_tab, values, preferred_element_type=jnp.float32
    ).astype(jnp.bfloat16)
    columns = lax.all_to_all(rows, "space", split_axis=3, concat_axis=2, tiled=True)
    held = None
    if early is not None:
        columns, held = lax.optimization_barrier((columns, early()))
    height = columns.shape[2]
    spectrum = jnp.einsum(
        "qmph,pbhkc->qbmkc", column_table(height, 1), columns, preferred_element_type=jnp.float32
    ).astype(jnp.bfloat16)
    weighted = apply_filter(spectrum, filter_weight[:, None], direction).astype(jnp.bfloat16)
    returned = jnp.einsum(
        "qmph,pbhkc->qbmkc", column_table(height, -1), weighted, preferred_element_type=jnp.float32
    ).astype(jnp.bfloat16)
    back_rows = lax.all_to_all(returned, "space", split_axis=2, concat_axis=3, tiled=True)
    tail = None
    if late is not None:
        back_rows, tail = lax.optimization_barrier((back_rows, late(spectrum)))
    output = jnp.einsum("pkw,pbhkc->bhwc", rows_tab, back_rows, preferred_element_type=jnp.float32)
    return (output, spectrum, held, tail)


def body(noisy_tokens, grad_out, filter_weight, weight_in, weight_out, gain_one, gain_two):
    batch, rows_dev, width, chans = noisy_tokens.shape
    inputs = noisy_tokens.astype(jnp.float32)
    normed_one, rstd_one = layer_norm(inputs)
    mixed_in = (normed_one * gain_one).astype(jnp.bfloat16)
    spatial, spectrum, _, _ = spectral(mixed_in, filter_weight, 1)
    normed_two, rstd_two = layer_norm(spatial)
    mlp_in = (normed_two * gain_two).astype(jnp.bfloat16).reshape(-1, chans)
    preact = jnp.dot(mlp_in, weight_in, preferred_element_type=jnp.float32)
    activated = exact_gelu(preact).astype(jnp.bfloat16)
    mlp_out = jnp.dot(activated, weight_out, preferred_element_type=jnp.float32)
    block_out = (inputs + mlp_out.reshape(inputs.shape)).astype(jnp.bfloat16)
    upstream = grad_out.reshape(-1, chans)
    grad_act = jnp.dot(upstream, weight_out.T, preferred_element_type=jnp.float32)
    grad_pre = jax.vjp(exact_gelu, preact)[1](grad_act)[0].astype(jnp.bfloat16)
    sum_out_t = jnp.dot(upstream.T, activated, preferred_element_type=jnp.float32)
    sum_in = jnp.dot(mlp_in.T, grad_pre, preferred_element_type=jnp.float32)
    grad_mlp = jnp.dot(grad_pre, weight_in.T, preferred_element_type=jnp.float32).reshape(
        inputs.shape
    )
    grad_spatial, sum_gain_two = norm_backward(grad_mlp, normed_two, rstd_two, gain_two)
    total_tokens = batch * lax.axis_size("copy") * rows_dev * lax.axis_size("space") * width
    factor = 1.0 / math.sqrt(total_tokens)
    n_copy, n_space = lax.axis_size("copy"), lax.axis_size("space")
    lanes = sum_in.shape[1]
    radices, axes = _split_axes(n_copy, n_space)
    row_div = 16 * math.prod(r for r, a in zip(radices, axes) if a == 0)
    extra = -(-(2 * sum_in.shape[0] + 1) // row_div) * row_div - 2 * sum_in.shape[0]

    def weight_sums():
        gains_block = jnp.pad(
            sum_gain_two[None, :], ((0, extra - 1), (0, lanes - sum_gain_two.shape[0]))
        )
        return all_sum([sum_in, sum_out_t, gains_block], n_copy, n_space, factor)

    def filter_grad(adjoint):
        spec_f = spectrum.astype(jnp.float32)
        adj_f = adjoint.astype(jnp.float32)
        filter_terms = jnp.stack(
            [
                jnp.sum(adj_f[0] * spec_f[0] + adj_f[1] * spec_f[1], axis=0),
                jnp.sum(adj_f[1] * spec_f[0] - adj_f[0] * spec_f[1], axis=0),
            ]
        )
        fshape = filter_terms.shape
        return filter_sum(
            filter_terms.astype(jnp.bfloat16).reshape(
                fshape[0] * fshape[1], fshape[2] * fshape[3]
            )
        ).reshape(fshape)

    back_spatial, _, total, grad_filter = spectral(
        grad_spatial.astype(jnp.bfloat16), filter_weight, -1, weight_sums, filter_grad
    )
    grad_normed, sum_gain_one = norm_backward(back_spatial, normed_one, rstd_one, gain_one)
    grad_tokens = (grad_out.astype(jnp.float32) + grad_normed).astype(jnp.bfloat16)
    gain_one_sum = tree_sum(sum_gain_one.reshape(1, -1), n_copy, n_space).reshape(-1)
    return (
        block_out,
        grad_tokens,
        grad_filter,
        total[: sum_in.shape[0]],
        total[sum_in.shape[0] : 2 * sum_in.shape[0]].T,
        gain_one_sum * factor,
        total[2 * sum_in.shape[0], : sum_gain_two.shape[0]].astype(jnp.float32),
    )


def solution(mesh):
    return jax.shard_map(
        body,
        mesh=mesh,
        in_specs=(
            P("copy", "space", None, None),
            P("copy", "space", None, None),
            P(None, None, "space", None),
            P(),
            P(),
            P(),
            P(),
        ),
        out_specs=(
            P("copy", "space", None, None),
            P("copy", "space", None, None),
            P(None, None, "space", None),
            P(),
            P(),
            P(),
            P(),
        ),
        check_vma=False,
    )
```

```python
import functools
import math

import jax
import jax.numpy as jnp
from jax import lax
from jax.experimental import pallas as pl
from jax.experimental.pallas import tpu as pltpu
from jax.sharding import PartitionSpec as P

MESH = pl.DeviceIdType.MESH

EPS = 1e-06


def _filter_sum_kernel(rows, x_ref, o_ref, half_in, part, other, full_in, sems):
    me_c = lax.axis_index("copy")
    me_s = lax.axis_index("space")
    core = me_c % 2
    hi = me_c // 2
    mate = (me_c + 1 - 2 * core, me_s)
    far = (me_c + 2 - 4 * hi, me_s)
    half = rows // 2
    barrier = pltpu.get_barrier_semaphore()
    pl.semaphore_signal(barrier, inc=1, device_id=mate, device_id_type=MESH)
    pl.semaphore_signal(barrier, inc=1, device_id=far, device_id_type=MESH)
    pl.semaphore_wait(barrier, 2)
    mine = pl.ds(pl.multiple_of(core * half, 8), half)
    theirs = pl.ds(pl.multiple_of((1 - core) * half, 8), half)
    c1 = pltpu.make_async_remote_copy(
        src_ref=x_ref.at[theirs], dst_ref=half_in, send_sem=sems.at[0], recv_sem=sems.at[1],
        device_id=mate, device_id_type=MESH)
    c1.start()
    c1.wait_recv()
    own = x_ref[mine, :].astype(jnp.float32)
    got = half_in[...].astype(jnp.float32)
    first = jnp.where(core == 0, own, got)
    second = jnp.where(core == 0, got, own)
    part[...] = (first + second).astype(jnp.bfloat16)
    c2 = pltpu.make_async_remote_copy(
        src_ref=part, dst_ref=other, send_sem=sems.at[2], recv_sem=sems.at[3],
        device_id=far, device_id_type=MESH)
    c2.start()
    c2.wait_recv()
    mine_p = part[...].astype(jnp.float32)
    got_p = other[...].astype(jnp.float32)
    total = jnp.where(hi == 0, mine_p + got_p, got_p + mine_p)
    o_ref[mine, :] = total
    c3 = pltpu.make_async_remote_copy(
        src_ref=o_ref.at[mine], dst_ref=full_in, send_sem=sems.at[4], recv_sem=sems.at[5],
        device_id=mate, device_id_type=MESH)
    c3.start()
    c3.wait_recv()
    o_ref[theirs, :] = full_in[...]
    c1.wait_send()
    c2.wait_send()
    c3.wait_send()


def filter_sum(x):
    rows, cols = x.shape
    half = rows // 2
    return pl.pallas_call(
        functools.partial(_filter_sum_kernel, rows),
        out_shape=jax.ShapeDtypeStruct((rows, cols), jnp.float32),
        in_specs=[pl.BlockSpec(memory_space=pltpu.VMEM)],
        out_specs=pl.BlockSpec(memory_space=pltpu.VMEM),
        scratch_shapes=[
            pltpu.VMEM((half, cols), x.dtype),
            pltpu.VMEM((half, cols), jnp.bfloat16),
            pltpu.VMEM((half, cols), jnp.bfloat16),
            pltpu.VMEM((half, cols), jnp.float32),
            pltpu.SemaphoreType.DMA((6,)),
        ],
        compiler_params=pltpu.CompilerParams(
            collective_id=1, has_side_effects=True, vmem_limit_bytes=48 * 1024 * 1024
        ),
        cost_estimate=pl.CostEstimate(
            flops=2 * rows * cols, transcendentals=0, bytes_accessed=10 * rows * cols
        ),
    )(x)


def _digit_orders(n_copy, n_space):
    c0, xh = ("copy", 0), ("copy", 1)
    if (n_copy, n_space) == (4, 64):
        xl, z1, z2, z4, y1, y2 = [("space", b) for b in range(6)]
        first = [[c0], [xl, z1], [y1, z2], [y2, xh, z4]]
        second = [[c0], [y1, y2], [xl, z1], [z2, xh, z4]]
        return first, second
    sb = [("space", b) for b in range(n_space.bit_length() - 1)]
    cb = [("copy", b) for b in range(1, n_copy.bit_length() - 1)]
    rest = sb + cb
    first = [[c0]] + [rest[i : i + 2] for i in range(0, len(rest), 2)]
    rest = rest[::-1]
    second = [[c0]] + [rest[i : i + 2] for i in range(0, len(rest), 2)]
    return first, second


def _tree_order(n_copy, n_space):
    if (n_copy, n_space) == (4, 64):
        xl, z1, z2, z4, y1, y2 = [("space", b) for b in range(6)]
        return [[("copy", 0), ("copy", 1), xl, y1, y2], [z1, z2, z4]]
    return _digit_orders(n_copy, n_space)[0]


def _plan(n_copy, n_space, split=True):
    orders = _digit_orders(n_copy, n_space)
    if not split:
        orders = (_tree_order(n_copy, n_space),) * 2
    me_c = lax.axis_index("copy")
    me_s = lax.axis_index("space")
    core = me_c % 2
    plan = []
    for s in range(len(orders[0])):
        per_core = []
        for order in orders:
            digit = order[s]
            radix = 1 << len(digit)
            bits = []
            for axis, b in digit:
                idx = me_c if axis == "copy" else me_s
                bits.append((idx // (1 << b)) % 2)
            v = sum(bit << i for i, bit in enumerate(bits))
            peers = []
            for d in range(1, radix):
                u = (v + d) % radix
                pc, ps = me_c, me_s
                for i, (axis, b) in enumerate(digit):
                    delta = ((u // (1 << i)) % 2 - bits[i]) * (1 << b)
                    if axis == "copy":
                        pc = pc + delta
                    else:
                        ps = ps + delta
                peers.append((pc, ps))
            per_core.append((radix, peers, v))
        (r0, p0, v0), (r1, p1, v1) = per_core
        assert r0 == r1
        peers = [
            ((1 - core) * a[0] + core * b[0], (1 - core) * a[1] + core * b[1])
            for a, b in zip(p0, p1)
        ]
        plan.append((r0, peers, (1 - core) * v0 + core * v1))
    return plan


def _split_axes(n_copy, n_space):
    radices = [1 << len(d) for d in _digit_orders(n_copy, n_space)[0]]
    if (n_copy, n_space) == (4, 64):
        return radices, [0, 0, 1, 0]
    return radices, [0] * len(radices)


def _all_sum_kernel(n_copy, n_space, scale, a_ref, b_ref, c_ref, o_ref, acc, send, *rest):
    plan = _plan(n_copy, n_space)
    _, axes = _split_axes(n_copy, n_space)
    steps = len(plan)
    recv = rest[:steps]
    rs_send, rs_recv, ag_send, ag_recv, local = rest[steps:]
    rows, cols = acc.shape
    at = 0
    loads = []
    for i, part_ref in enumerate((a_ref, b_ref, c_ref)):
        n = part_ref.shape[0]
        cp = pltpu.make_async_copy(part_ref, acc.at[pl.ds(at, n)], local.at[i])
        cp.start()
        loads.append(cp)
        at += n
    barrier = pltpu.get_barrier_semaphore()
    count = 0
    for radix, peers, _ in plan:
        for peer in peers:
            pl.semaphore_signal(barrier, inc=1, device_id=peer, device_id_type=MESH)
            count += 1
    for cp in loads:
        cp.wait()
    pl.semaphore_wait(barrier, count)

    def window(r0, rl, c0, cl):
        return (pl.ds(pl.multiple_of(r0, 16), rl), pl.ds(pl.multiple_of(c0, 128), cl))

    pending = []
    box = [0, rows, 0, cols]
    slot = 0
    for s, (radix, peers, v) in enumerate(plan):
        r0, rl, c0, cl = box
        if axes[s] == 0:
            part = rl // radix

            def piece(u, r0=r0, c0=c0, cl=cl, part=part):
                return window(r0 + u * part, part, c0, cl)
        else:
            part = cl // radix

            def piece(u, r0=r0, rl=rl, c0=c0, part=part):
                return window(r0, rl, c0 + u * part, part)
        descs = []
        for d, peer in enumerate(peers, start=1):
            u = (v + d) % radix
            w = piece(u)
            send[w] = acc[w].astype(jnp.bfloat16)
            c = pltpu.make_async_remote_copy(
                src_ref=send.at[w],
                dst_ref=recv[s].at[d - 1],
                send_sem=rs_send.at[slot + d - 1],
                recv_sem=rs_recv.at[slot + d - 1],
                device_id=peer,
                device_id_type=MESH,
            )
            c.start()
            descs.append(c)
        keep = piece(v)
        total = acc[keep]
        for d, c in enumerate(descs, start=1):
            c.wait_recv()
            total = total + recv[s][d - 1].astype(jnp.float32)
        acc[keep] = total
        pending += descs
        slot += radix - 1
        if axes[s] == 0:
            box = [r0 + v * part, part, c0, cl]
        else:
            box = [r0, rl, c0 + v * part, part]
    r0, rl, c0, cl = box
    mine = window(r0, rl, c0, cl)
    o_ref[mine] = (acc[mine] * scale).astype(o_ref.dtype)
    for s in reversed(range(steps)):
        radix, peers, v = plan[s]
        slot -= radix - 1
        r0, rl, c0, cl = box
        if axes[s] == 0:
            first = r0 - v * rl

            def piece(u, first=first, rl=rl, c0=c0, cl=cl):
                return window(first + u * rl, rl, c0, cl)

            box = [first, radix * rl, c0, cl]
        else:
            first = c0 - v * cl

            def piece(u, first=first, r0=r0, rl=rl, cl=cl):
                return window(r0, rl, first + u * cl, cl)

            box = [r0, rl, first, radix * cl]
        mine = piece(v)
        descs = []
        for d, peer in enumerate(peers, start=1):
            c = pltpu.make_async_remote_copy(
                src_ref=o_ref.at[mine],
                dst_ref=o_ref.at[mine],
                send_sem=ag_send.at[slot + d - 1],
                recv_sem=ag_recv.at[slot + d - 1],
                device_id=peer,
                device_id_type=MESH,
            )
            c.start()
            descs.append(c)
        for d, peer in enumerate(peers, start=1):
            theirs = piece((v - d + radix) % radix)
            pltpu.make_async_remote_copy(
                src_ref=o_ref.at[theirs],
                dst_ref=o_ref.at[theirs],
                send_sem=ag_send.at[slot + d - 1],
                recv_sem=ag_recv.at[slot + d - 1],
                device_id=peer,
                device_id_type=MESH,
            ).wait_recv()
        pending += descs
    for c in pending:
        c.wait_send()


def all_sum(parts, n_copy, n_space, scale):
    rows = sum(p.shape[0] for p in parts)
    cols = parts[0].shape[1]
    radices, axes = _split_axes(n_copy, n_space)
    recv = []
    rl, cl = rows, cols
    for r, a in zip(radices, axes):
        if a == 0:
            rl //= r
        else:
            cl //= r
        recv.append(pltpu.VMEM((r - 1, rl, cl), jnp.bfloat16))
    links = sum(r - 1 for r in radices)
    return pl.pallas_call(
        functools.partial(_all_sum_kernel, n_copy, n_space, scale),
        out_shape=jax.ShapeDtypeStruct((rows, cols), jnp.bfloat16),
        in_specs=[pl.BlockSpec(memory_space=pltpu.VMEM)] * len(parts),
        out_specs=pl.BlockSpec(memory_space=pltpu.VMEM),
        scratch_shapes=[
            pltpu.VMEM((rows, cols), jnp.float32),
            pltpu.VMEM((rows, cols), jnp.bfloat16),
        ]
        + recv
        + [pltpu.SemaphoreType.DMA((links,)) for _ in range(4)]
        + [pltpu.SemaphoreType.DMA((len(parts),))],
        compiler_params=pltpu.CompilerParams(
            collective_id=3, has_side_effects=True, vmem_limit_bytes=56 * 1024 * 1024
        ),
        cost_estimate=pl.CostEstimate(
            flops=rows * cols, transcendentals=0, bytes_accessed=12 * rows * cols
        ),
    )(*parts)


def _tree_sum_kernel(n_copy, n_space, x_ref, o_ref, *rest):
    plan = _plan(n_copy, n_space, split=False)
    steps = len(plan)
    slots = rest[:steps]
    send_sem, recv_sem = rest[steps:]
    barrier = pltpu.get_barrier_semaphore()
    count = 0
    for _, peers, _ in plan:
        for peer in peers:
            pl.semaphore_signal(barrier, inc=1, device_id=peer, device_id_type=MESH)
            count += 1
    pl.semaphore_wait(barrier, count)
    acc = x_ref[...]
    pending = []
    slot = 0
    for s, (radix, peers, v) in enumerate(plan):
        slots[s][0] = acc
        descs = []
        for d, peer in enumerate(peers, start=1):
            c = pltpu.make_async_remote_copy(
                src_ref=slots[s].at[0],
                dst_ref=slots[s].at[d],
                send_sem=send_sem.at[slot + d - 1],
                recv_sem=recv_sem.at[slot + d - 1],
                device_id=peer,
                device_id_type=MESH,
            )
            c.start()
            descs.append(c)
        for c in descs:
            c.wait_recv()
        total = slots[s][(v + radix) % radix]
        for u in range(1, radix):
            total = total + slots[s][(v - u + radix) % radix]
        acc = total
        pending += descs
        slot += radix - 1
    for c in pending:
        c.wait_send()
    o_ref[...] = acc


def tree_sum(x, n_copy, n_space):
    radices = [1 << len(d) for d in _tree_order(n_copy, n_space)]
    links = sum(r - 1 for r in radices)
    return pl.pallas_call(
        functools.partial(_tree_sum_kernel, n_copy, n_space),
        out_shape=jax.ShapeDtypeStruct(x.shape, jnp.float32),
        in_specs=[pl.BlockSpec(memory_space=pltpu.VMEM)],
        out_specs=pl.BlockSpec(memory_space=pltpu.VMEM),
        scratch_shapes=[pltpu.VMEM((r,) + x.shape, jnp.float32) for r in radices]
        + [pltpu.SemaphoreType.DMA((links,)), pltpu.SemaphoreType.DMA((links,))],
        compiler_params=pltpu.CompilerParams(collective_id=2, has_side_effects=True),
        cost_estimate=pl.CostEstimate(
            flops=links * x.size, transcendentals=0, bytes_accessed=8 * links * x.size
        ),
    )(x)


def dft_parts(length):
    index = jnp.arange(length, dtype=jnp.int32)
    phase = index[:, None] * index[None, :] % length
    angle = phase.astype(jnp.float32) * (2.0 * math.pi / length)
    factor = 1.0 / math.sqrt(length)
    return (
        (jnp.cos(angle) * factor).astype(jnp.bfloat16),
        (jnp.sin(angle) * factor).astype(jnp.bfloat16),
    )


def row_table(length):
    cosine, sine = dft_parts(length)
    return jnp.stack([cosine, -sine])


def column_table(length, direction):
    cosine, sine = dft_parts(length)
    upper = jnp.stack([cosine, direction * sine], axis=1)
    lower = jnp.stack([-direction * sine, cosine], axis=1)
    return jnp.stack([upper, lower])


def layer_norm(values):
    centre = jnp.mean(values, axis=-1, keepdims=True)
    centred = values - centre
    variance = jnp.mean(centred * centred, axis=-1, keepdims=True)
    rstd_value = lax.rsqrt(variance + EPS)
    return (centred * rstd_value, rstd_value)


def norm_backward(upstream, normed, rstd_value, gain):
    scaled = upstream * gain
    result = (
        scaled
        - jnp.mean(scaled, axis=-1, keepdims=True)
        - normed * jnp.mean(scaled * normed, axis=-1, keepdims=True)
    ) * rstd_value
    lead = tuple(range(upstream.ndim - 1))
    return (result, jnp.sum(upstream * normed, axis=lead))


def apply_filter(spectrum, filter_weight, direction):
    real_part = spectrum[0].astype(jnp.float32)
    imag_part = spectrum[1].astype(jnp.float32)
    kernel_real = filter_weight[0].astype(jnp.float32)
    kernel_imag = direction * filter_weight[1].astype(jnp.float32)
    return jnp.stack(
        [
            kernel_real * real_part - kernel_imag * imag_part,
            kernel_real * imag_part + kernel_imag * real_part,
        ]
    )


def exact_gelu(values):
    return jax.nn.gelu(values, approximate=False)


def spectral(values, filter_weight, direction, early=None, late=None):
    width = values.shape[2]
    rows_tab = row_table(width)
    rows = jnp.einsum(
        "pkw,bhwc->pbhkc", rows_tab, values, preferred_element_type=jnp.float32
    ).astype(jnp.bfloat16)
    columns = lax.all_to_all(rows, "space", split_axis=3, concat_axis=2, tiled=True)
    held = None
    if early is not None:
        columns, held = lax.optimization_barrier((columns, early()))
    height = columns.shape[2]
    spectrum = jnp.einsum(
        "qmph,pbhkc->qbmkc", column_table(height, 1), columns, preferred_element_type=jnp.float32
    ).astype(jnp.bfloat16)
    weighted = apply_filter(spectrum, filter_weight[:, None], direction).astype(jnp.bfloat16)
    returned = jnp.einsum(
        "qmph,pbhkc->qbmkc", column_table(height, -1), weighted, preferred_element_type=jnp.float32
    ).astype(jnp.bfloat16)
    back_rows = lax.all_to_all(returned, "space", split_axis=2, concat_axis=3, tiled=True)
    tail = None
    if late is not None:
        back_rows, tail = lax.optimization_barrier((back_rows, late(spectrum)))
    output = jnp.einsum("pkw,pbhkc->bhwc", rows_tab, back_rows, preferred_element_type=jnp.float32)
    return (output, spectrum, held, tail)


def body(noisy_tokens, grad_out, filter_weight, weight_in, weight_out, gain_one, gain_two):
    batch, rows_dev, width, chans = noisy_tokens.shape
    inputs = noisy_tokens.astype(jnp.float32)
    normed_one, rstd_one = layer_norm(inputs)
    mixed_in = (normed_one * gain_one).astype(jnp.bfloat16)
    spatial, spectrum, _, _ = spectral(mixed_in, filter_weight, 1)
    normed_two, rstd_two = layer_norm(spatial)
    mlp_in = (normed_two * gain_two).astype(jnp.bfloat16).reshape(-1, chans)
    preact = jnp.dot(mlp_in, weight_in, preferred_element_type=jnp.float32)
    activated = exact_gelu(preact).astype(jnp.bfloat16)
    mlp_out = jnp.dot(activated, weight_out, preferred_element_type=jnp.float32)
    block_out = (inputs + mlp_out.reshape(inputs.shape)).astype(jnp.bfloat16)
    upstream = grad_out.reshape(-1, chans)
    grad_act = jnp.dot(upstream, weight_out.T, preferred_element_type=jnp.float32)
    grad_pre = jax.vjp(exact_gelu, preact)[1](grad_act)[0].astype(jnp.bfloat16)
    sum_out_t = jnp.dot(upstream.T, activated, preferred_element_type=jnp.float32)
    sum_in = jnp.dot(mlp_in.T, grad_pre, preferred_element_type=jnp.float32)
    grad_mlp = jnp.dot(grad_pre, weight_in.T, preferred_element_type=jnp.float32).reshape(
        inputs.shape
    )
    grad_spatial, sum_gain_two = norm_backward(grad_mlp, normed_two, rstd_two, gain_two)
    total_tokens = batch * lax.axis_size("copy") * rows_dev * lax.axis_size("space") * width
    factor = 1.0 / math.sqrt(total_tokens)
    n_copy, n_space = lax.axis_size("copy"), lax.axis_size("space")
    lanes = sum_in.shape[1]
    radices, axes = _split_axes(n_copy, n_space)
    row_div = 16 * math.prod(r for r, a in zip(radices, axes) if a == 0)
    extra = -(-(2 * sum_in.shape[0] + 1) // row_div) * row_div - 2 * sum_in.shape[0]

    def weight_sums():
        gains_block = jnp.pad(
            sum_gain_two[None, :], ((0, extra - 1), (0, lanes - sum_gain_two.shape[0]))
        )
        return all_sum([sum_in, sum_out_t, gains_block], n_copy, n_space, factor)

    def filter_grad(adjoint):
        spec_f = spectrum.astype(jnp.float32)
        adj_f = adjoint.astype(jnp.float32)
        filter_terms = jnp.stack(
            [
                jnp.sum(adj_f[0] * spec_f[0] + adj_f[1] * spec_f[1], axis=0),
                jnp.sum(adj_f[1] * spec_f[0] - adj_f[0] * spec_f[1], axis=0),
            ]
        )
        fshape = filter_terms.shape
        return filter_sum(
            filter_terms.astype(jnp.bfloat16).reshape(
                fshape[0] * fshape[1], fshape[2] * fshape[3]
            )
        ).reshape(fshape)

    back_spatial, _, total, grad_filter = spectral(
        grad_spatial.astype(jnp.bfloat16), filter_weight, -1, weight_sums, filter_grad
    )
    grad_normed, sum_gain_one = norm_backward(back_spatial, normed_one, rstd_one, gain_one)
    grad_tokens = (grad_out.astype(jnp.float32) + grad_normed).astype(jnp.bfloat16)
    gain_one_sum = tree_sum(sum_gain_one.reshape(1, -1), n_copy, n_space).reshape(-1)
    return (
        block_out,
        grad_tokens,
        grad_filter,
        total[: sum_in.shape[0]],
        total[sum_in.shape[0] : 2 * sum_in.shape[0]].T,
        gain_one_sum * factor,
        total[2 * sum_in.shape[0], : sum_gain_two.shape[0]].astype(jnp.float32),
    )


def solution(mesh):
    return jax.shard_map(
        body,
        mesh=mesh,
        in_specs=(
            P("copy", "space", None, None),
            P("copy", "space", None, None),
            P(None, None, "space", None),
            P(),
            P(),
            P(),
            P(),
        ),
        out_specs=(
            P("copy", "space", None, None),
            P("copy", "space", None, None),
            P(None, None, "space", None),
            P(),
            P(),
            P(),
            P(),
        ),
        check_vma=False,
    )
```

```python
import functools
import math

import jax
import jax.numpy as jnp
from jax import lax
from jax.experimental import pallas as pl
from jax.experimental.pallas import tpu as pltpu
from jax.sharding import PartitionSpec as P

MESH = pl.DeviceIdType.MESH

EPS = 1e-06


def _filter_sum_kernel(rows, x_ref, o_ref, half_in, part, other, sems):
    me_c = lax.axis_index("copy")
    me_s = lax.axis_index("space")
    core = me_c % 2
    hi = me_c // 2
    mate = (me_c + 1 - 2 * core, me_s)
    far = (me_c + 2 - 4 * hi, me_s)
    half = rows // 2
    barrier = pltpu.get_barrier_semaphore()
    pl.semaphore_signal(barrier, inc=1, device_id=mate, device_id_type=MESH)
    pl.semaphore_signal(barrier, inc=1, device_id=far, device_id_type=MESH)
    pl.semaphore_wait(barrier, 2)
    mine = pl.ds(pl.multiple_of(core * half, 8), half)
    theirs = pl.ds(pl.multiple_of((1 - core) * half, 8), half)
    c1 = pltpu.make_async_remote_copy(
        src_ref=x_ref.at[theirs], dst_ref=half_in, send_sem=sems.at[0], recv_sem=sems.at[1],
        device_id=mate, device_id_type=MESH)
    c1.start()
    c1.wait_recv()
    own = x_ref[mine, :].astype(jnp.float32)
    got = half_in[...].astype(jnp.float32)
    first = jnp.where(core == 0, own, got)
    second = jnp.where(core == 0, got, own)
    part[...] = (first + second).astype(jnp.bfloat16)
    c2 = pltpu.make_async_remote_copy(
        src_ref=part, dst_ref=other, send_sem=sems.at[2], recv_sem=sems.at[3],
        device_id=far, device_id_type=MESH)
    c2.start()
    c2.wait_recv()
    mine_p = part[...].astype(jnp.float32)
    got_p = other[...].astype(jnp.float32)
    total = jnp.where(hi == 0, mine_p + got_p, got_p + mine_p)
    o_ref[mine, :] = total
    c3 = pltpu.make_async_remote_copy(
        src_ref=o_ref.at[mine], dst_ref=o_ref.at[mine], send_sem=sems.at[4], recv_sem=sems.at[5],
        device_id=mate, device_id_type=MESH)
    c3.start()
    pltpu.make_async_remote_copy(
        src_ref=o_ref.at[theirs], dst_ref=o_ref.at[theirs], send_sem=sems.at[4],
        recv_sem=sems.at[5], device_id=mate, device_id_type=MESH).wait_recv()
    c1.wait_send()
    c2.wait_send()
    c3.wait_send()


def filter_sum(x):
    rows, cols = x.shape
    half = rows // 2
    return pl.pallas_call(
        functools.partial(_filter_sum_kernel, rows),
        out_shape=jax.ShapeDtypeStruct((rows, cols), jnp.float32),
        in_specs=[pl.BlockSpec(memory_space=pltpu.VMEM)],
        out_specs=pl.BlockSpec(memory_space=pltpu.VMEM),
        scratch_shapes=[
            pltpu.VMEM((half, cols), x.dtype),
            pltpu.VMEM((half, cols), jnp.bfloat16),
            pltpu.VMEM((half, cols), jnp.bfloat16),
            pltpu.SemaphoreType.DMA((6,)),
        ],
        compiler_params=pltpu.CompilerParams(
            collective_id=1, has_side_effects=True, vmem_limit_bytes=48 * 1024 * 1024
        ),
        cost_estimate=pl.CostEstimate(
            flops=2 * rows * cols, transcendentals=0, bytes_accessed=10 * rows * cols
        ),
    )(x)


def _digit_orders(n_copy, n_space):
    c0, xh = ("copy", 0), ("copy", 1)
    if (n_copy, n_space) == (4, 64):
        xl, z1, z2, z4, y1, y2 = [("space", b) for b in range(6)]
        first = [[c0], [xl, z1], [y1, z2], [y2, xh, z4]]
        second = [[c0], [y1, y2], [xl, z1], [z2, xh, z4]]
        return first, second
    sb = [("space", b) for b in range(n_space.bit_length() - 1)]
    cb = [("copy", b) for b in range(1, n_copy.bit_length() - 1)]
    rest = sb + cb
    first = [[c0]] + [rest[i : i + 2] for i in range(0, len(rest), 2)]
    rest = rest[::-1]
    second = [[c0]] + [rest[i : i + 2] for i in range(0, len(rest), 2)]
    return first, second


def _tree_order(n_copy, n_space):
    if (n_copy, n_space) == (4, 64):
        xl, z1, z2, z4, y1, y2 = [("space", b) for b in range(6)]
        return [[("copy", 0), ("copy", 1), xl], [z1, z2, z4], [y1, y2]]
    return _digit_orders(n_copy, n_space)[0]


def _plan(n_copy, n_space, split=True):
    orders = _digit_orders(n_copy, n_space)
    if not split:
        orders = (_tree_order(n_copy, n_space),) * 2
    me_c = lax.axis_index("copy")
    me_s = lax.axis_index("space")
    core = me_c % 2
    plan = []
    for s in range(len(orders[0])):
        per_core = []
        for order in orders:
            digit = order[s]
            radix = 1 << len(digit)
            bits = []
            for axis, b in digit:
                idx = me_c if axis == "copy" else me_s
                bits.append((idx // (1 << b)) % 2)
            v = sum(bit << i for i, bit in enumerate(bits))
            peers = []
            for d in range(1, radix):
                u = (v + d) % radix
                pc, ps = me_c, me_s
                for i, (axis, b) in enumerate(digit):
                    delta = ((u // (1 << i)) % 2 - bits[i]) * (1 << b)
                    if axis == "copy":
                        pc = pc + delta
                    else:
                        ps = ps + delta
                peers.append((pc, ps))
            per_core.append((radix, peers, v))
        (r0, p0, v0), (r1, p1, v1) = per_core
        assert r0 == r1
        peers = [
            ((1 - core) * a[0] + core * b[0], (1 - core) * a[1] + core * b[1])
            for a, b in zip(p0, p1)
        ]
        plan.append((r0, peers, (1 - core) * v0 + core * v1))
    return plan


def _split_axes(n_copy, n_space):
    radices = [1 << len(d) for d in _digit_orders(n_copy, n_space)[0]]
    if (n_copy, n_space) == (4, 64):
        return radices, [0, 0, 1, 0]
    return radices, [0] * len(radices)


def _all_sum_kernel(n_copy, n_space, scale, a_ref, b_ref, c_ref, o_ref, acc, send, *rest):
    plan = _plan(n_copy, n_space)
    _, axes = _split_axes(n_copy, n_space)
    steps = len(plan)
    recv = rest[:steps]
    rs_send, rs_recv, ag_send, ag_recv, local = rest[steps:]
    rows, cols = acc.shape
    at = 0
    loads = []
    for i, part_ref in enumerate((a_ref, b_ref, c_ref)):
        n = part_ref.shape[0]
        cp = pltpu.make_async_copy(part_ref, acc.at[pl.ds(at, n)], local.at[i])
        cp.start()
        loads.append(cp)
        at += n
    barrier = pltpu.get_barrier_semaphore()
    count = 0
    for radix, peers, _ in plan:
        for peer in peers:
            pl.semaphore_signal(barrier, inc=1, device_id=peer, device_id_type=MESH)
            count += 1
    for cp in loads:
        cp.wait()
    pl.semaphore_wait(barrier, count)

    def window(r0, rl, c0, cl):
        return (pl.ds(pl.multiple_of(r0, 16), rl), pl.ds(pl.multiple_of(c0, 128), cl))

    pending = []
    box = [0, rows, 0, cols]
    slot = 0
    for s, (radix, peers, v) in enumerate(plan):
        r0, rl, c0, cl = box
        if axes[s] == 0:
            part = rl // radix

            def piece(u, r0=r0, c0=c0, cl=cl, part=part):
                return window(r0 + u * part, part, c0, cl)
        else:
            part = cl // radix

            def piece(u, r0=r0, rl=rl, c0=c0, part=part):
                return window(r0, rl, c0 + u * part, part)
        descs = []
        for d, peer in enumerate(peers, start=1):
            u = (v + d) % radix
            w = piece(u)
            send[w] = acc[w].astype(jnp.bfloat16)
            c = pltpu.make_async_remote_copy(
                src_ref=send.at[w],
                dst_ref=recv[s].at[d - 1],
                send_sem=rs_send.at[slot + d - 1],
                recv_sem=rs_recv.at[slot + d - 1],
                device_id=peer,
                device_id_type=MESH,
            )
            c.start()
            descs.append(c)
        keep = piece(v)
        total = acc[keep]
        for d, c in enumerate(descs, start=1):
            c.wait_recv()
            total = total + recv[s][d - 1].astype(jnp.float32)
        acc[keep] = total
        pending += descs
        slot += radix - 1
        if axes[s] == 0:
            box = [r0 + v * part, part, c0, cl]
        else:
            box = [r0, rl, c0 + v * part, part]
    r0, rl, c0, cl = box
    mine = window(r0, rl, c0, cl)
    o_ref[mine] = (acc[mine] * scale).astype(o_ref.dtype)
    for s in reversed(range(steps)):
        radix, peers, v = plan[s]
        slot -= radix - 1
        r0, rl, c0, cl = box
        if axes[s] == 0:
            first = r0 - v * rl

            def piece(u, first=first, rl=rl, c0=c0, cl=cl):
                return window(first + u * rl, rl, c0, cl)

            box = [first, radix * rl, c0, cl]
        else:
            first = c0 - v * cl

            def piece(u, first=first, r0=r0, rl=rl, cl=cl):
                return window(r0, rl, first + u * cl, cl)

            box = [r0, rl, first, radix * cl]
        mine = piece(v)
        descs = []
        for d, peer in enumerate(peers, start=1):
            c = pltpu.make_async_remote_copy(
                src_ref=o_ref.at[mine],
                dst_ref=o_ref.at[mine],
                send_sem=ag_send.at[slot + d - 1],
                recv_sem=ag_recv.at[slot + d - 1],
                device_id=peer,
                device_id_type=MESH,
            )
            c.start()
            descs.append(c)
        for d, peer in enumerate(peers, start=1):
            theirs = piece((v - d + radix) % radix)
            pltpu.make_async_remote_copy(
                src_ref=o_ref.at[theirs],
                dst_ref=o_ref.at[theirs],
                send_sem=ag_send.at[slot + d - 1],
                recv_sem=ag_recv.at[slot + d - 1],
                device_id=peer,
                device_id_type=MESH,
            ).wait_recv()
        pending += descs
    for c in pending:
        c.wait_send()


def all_sum(parts, n_copy, n_space, scale):
    rows = sum(p.shape[0] for p in parts)
    cols = parts[0].shape[1]
    radices, axes = _split_axes(n_copy, n_space)
    recv = []
    rl, cl = rows, cols
    for r, a in zip(radices, axes):
        if a == 0:
            rl //= r
        else:
            cl //= r
        recv.append(pltpu.VMEM((r - 1, rl, cl), jnp.bfloat16))
    links = sum(r - 1 for r in radices)
    return pl.pallas_call(
        functools.partial(_all_sum_kernel, n_copy, n_space, scale),
        out_shape=jax.ShapeDtypeStruct((rows, cols), jnp.bfloat16),
        in_specs=[pl.BlockSpec(memory_space=pltpu.VMEM)] * len(parts),
        out_specs=pl.BlockSpec(memory_space=pltpu.VMEM),
        scratch_shapes=[
            pltpu.VMEM((rows, cols), jnp.float32),
            pltpu.VMEM((rows, cols), jnp.bfloat16),
        ]
        + recv
        + [pltpu.SemaphoreType.DMA((links,)) for _ in range(4)]
        + [pltpu.SemaphoreType.DMA((len(parts),))],
        compiler_params=pltpu.CompilerParams(
            collective_id=3, has_side_effects=True, vmem_limit_bytes=56 * 1024 * 1024
        ),
        cost_estimate=pl.CostEstimate(
            flops=rows * cols, transcendentals=0, bytes_accessed=12 * rows * cols
        ),
    )(*parts)


def _tree_sum_kernel(n_copy, n_space, x_ref, o_ref, *rest):
    plan = _plan(n_copy, n_space, split=False)
    steps = len(plan)
    slots = rest[:steps]
    send_sem, recv_sem = rest[steps:]
    barrier = pltpu.get_barrier_semaphore()
    count = 0
    for _, peers, _ in plan:
        for peer in peers:
            pl.semaphore_signal(barrier, inc=1, device_id=peer, device_id_type=MESH)
            count += 1
    pl.semaphore_wait(barrier, count)
    acc = x_ref[...]
    pending = []
    slot = 0
    for s, (radix, peers, v) in enumerate(plan):
        slots[s][0] = acc
        descs = []
        for d, peer in enumerate(peers, start=1):
            c = pltpu.make_async_remote_copy(
                src_ref=slots[s].at[0],
                dst_ref=slots[s].at[d],
                send_sem=send_sem.at[slot + d - 1],
                recv_sem=recv_sem.at[slot + d - 1],
                device_id=peer,
                device_id_type=MESH,
            )
            c.start()
            descs.append(c)
        for c in descs:
            c.wait_recv()
        total = slots[s][(v + radix) % radix]
        for u in range(1, radix):
            total = total + slots[s][(v - u + radix) % radix]
        acc = total
        pending += descs
        slot += radix - 1
    for c in pending:
        c.wait_send()
    o_ref[...] = acc


def tree_sum(x, n_copy, n_space):
    radices = [1 << len(d) for d in _tree_order(n_copy, n_space)]
    links = sum(r - 1 for r in radices)
    return pl.pallas_call(
        functools.partial(_tree_sum_kernel, n_copy, n_space),
        out_shape=jax.ShapeDtypeStruct(x.shape, jnp.float32),
        in_specs=[pl.BlockSpec(memory_space=pltpu.VMEM)],
        out_specs=pl.BlockSpec(memory_space=pltpu.VMEM),
        scratch_shapes=[pltpu.VMEM((r,) + x.shape, jnp.float32) for r in radices]
        + [pltpu.SemaphoreType.DMA((links,)), pltpu.SemaphoreType.DMA((links,))],
        compiler_params=pltpu.CompilerParams(collective_id=2, has_side_effects=True),
        cost_estimate=pl.CostEstimate(
            flops=links * x.size, transcendentals=0, bytes_accessed=8 * links * x.size
        ),
    )(x)


def dft_parts(length):
    index = jnp.arange(length, dtype=jnp.int32)
    phase = index[:, None] * index[None, :] % length
    angle = phase.astype(jnp.float32) * (2.0 * math.pi / length)
    factor = 1.0 / math.sqrt(length)
    return (
        (jnp.cos(angle) * factor).astype(jnp.bfloat16),
        (jnp.sin(angle) * factor).astype(jnp.bfloat16),
    )


def row_table(length):
    cosine, sine = dft_parts(length)
    return jnp.stack([cosine, -sine])


def column_table(length, direction):
    cosine, sine = dft_parts(length)
    upper = jnp.stack([cosine, direction * sine], axis=1)
    lower = jnp.stack([-direction * sine, cosine], axis=1)
    return jnp.stack([upper, lower])


def layer_norm(values):
    centre = jnp.mean(values, axis=-1, keepdims=True)
    centred = values - centre
    variance = jnp.mean(centred * centred, axis=-1, keepdims=True)
    rstd_value = lax.rsqrt(variance + EPS)
    return (centred * rstd_value, rstd_value)


def norm_backward(upstream, normed, rstd_value, gain):
    scaled = upstream * gain
    result = (
        scaled
        - jnp.mean(scaled, axis=-1, keepdims=True)
        - normed * jnp.mean(scaled * normed, axis=-1, keepdims=True)
    ) * rstd_value
    lead = tuple(range(upstream.ndim - 1))
    return (result, jnp.sum(upstream * normed, axis=lead))


def apply_filter(spectrum, filter_weight, direction):
    real_part = spectrum[0].astype(jnp.float32)
    imag_part = spectrum[1].astype(jnp.float32)
    kernel_real = filter_weight[0].astype(jnp.float32)
    kernel_imag = direction * filter_weight[1].astype(jnp.float32)
    return jnp.stack(
        [
            kernel_real * real_part - kernel_imag * imag_part,
            kernel_real * imag_part + kernel_imag * real_part,
        ]
    )


def exact_gelu(values):
    return jax.nn.gelu(values, approximate=False)


def spectral(values, filter_weight, direction, early=None, late=None):
    width = values.shape[2]
    rows_tab = row_table(width)
    rows = jnp.einsum(
        "pkw,bhwc->pbhkc", rows_tab, values, preferred_element_type=jnp.float32
    ).astype(jnp.bfloat16)
    columns = lax.all_to_all(rows, "space", split_axis=3, concat_axis=2, tiled=True)
    held = None
    if early is not None:
        columns, held = lax.optimization_barrier((columns, early()))
    height = columns.shape[2]
    spectrum = jnp.einsum(
        "qmph,pbhkc->qbmkc", column_table(height, 1), columns, preferred_element_type=jnp.float32
    ).astype(jnp.bfloat16)
    weighted = apply_filter(spectrum, filter_weight[:, None], direction).astype(jnp.bfloat16)
    returned = jnp.einsum(
        "qmph,pbhkc->qbmkc", column_table(height, -1), weighted, preferred_element_type=jnp.float32
    ).astype(jnp.bfloat16)
    back_rows = lax.all_to_all(returned, "space", split_axis=2, concat_axis=3, tiled=True)
    tail = None
    if late is not None:
        back_rows, tail = lax.optimization_barrier((back_rows, late(spectrum)))
    output = jnp.einsum("pkw,pbhkc->bhwc", rows_tab, back_rows, preferred_element_type=jnp.float32)
    return (output, spectrum, held, tail)


def body(noisy_tokens, grad_out, filter_weight, weight_in, weight_out, gain_one, gain_two):
    batch, rows_dev, width, chans = noisy_tokens.shape
    inputs = noisy_tokens.astype(jnp.float32)
    normed_one, rstd_one = layer_norm(inputs)
    mixed_in = (normed_one * gain_one).astype(jnp.bfloat16)
    spatial, spectrum, _, _ = spectral(mixed_in, filter_weight, 1)
    normed_two, rstd_two = layer_norm(spatial)
    mlp_in = (normed_two * gain_two).astype(jnp.bfloat16).reshape(-1, chans)
    preact = jnp.dot(mlp_in, weight_in, preferred_element_type=jnp.float32)
    activated = exact_gelu(preact).astype(jnp.bfloat16)
    mlp_out = jnp.dot(activated, weight_out, preferred_element_type=jnp.float32)
    block_out = (inputs + mlp_out.reshape(inputs.shape)).astype(jnp.bfloat16)
    upstream = grad_out.reshape(-1, chans)
    grad_act = jnp.dot(upstream, weight_out.T, preferred_element_type=jnp.float32)
    grad_pre = jax.vjp(exact_gelu, preact)[1](grad_act)[0].astype(jnp.bfloat16)
    sum_out_t = jnp.dot(upstream.T, activated, preferred_element_type=jnp.float32)
    sum_in = jnp.dot(mlp_in.T, grad_pre, preferred_element_type=jnp.float32)
    grad_mlp = jnp.dot(grad_pre, weight_in.T, preferred_element_type=jnp.float32).reshape(
        inputs.shape
    )
    grad_spatial, sum_gain_two = norm_backward(grad_mlp, normed_two, rstd_two, gain_two)
    total_tokens = batch * lax.axis_size("copy") * rows_dev * lax.axis_size("space") * width
    factor = 1.0 / math.sqrt(total_tokens)
    n_copy, n_space = lax.axis_size("copy"), lax.axis_size("space")
    lanes = sum_in.shape[1]
    radices, axes = _split_axes(n_copy, n_space)
    row_div = 16 * math.prod(r for r, a in zip(radices, axes) if a == 0)
    extra = -(-(2 * sum_in.shape[0] + 1) // row_div) * row_div - 2 * sum_in.shape[0]

    def weight_sums():
        gains_block = jnp.pad(
            sum_gain_two[None, :], ((0, extra - 1), (0, lanes - sum_gain_two.shape[0]))
        )
        return all_sum([sum_in, sum_out_t, gains_block], n_copy, n_space, factor)

    def filter_grad(adjoint):
        spec_f = spectrum.astype(jnp.float32)
        adj_f = adjoint.astype(jnp.float32)
        filter_terms = jnp.stack(
            [
                jnp.sum(adj_f[0] * spec_f[0] + adj_f[1] * spec_f[1], axis=0),
                jnp.sum(adj_f[1] * spec_f[0] - adj_f[0] * spec_f[1], axis=0),
            ]
        )
        fshape = filter_terms.shape
        return filter_sum(
            filter_terms.astype(jnp.bfloat16).reshape(
                fshape[0] * fshape[1], fshape[2] * fshape[3]
            )
        ).reshape(fshape)

    back_spatial, _, total, grad_filter = spectral(
        grad_spatial.astype(jnp.bfloat16), filter_weight, -1, weight_sums, filter_grad
    )
    grad_normed, sum_gain_one = norm_backward(back_spatial, normed_one, rstd_one, gain_one)
    grad_tokens = (grad_out.astype(jnp.float32) + grad_normed).astype(jnp.bfloat16)
    gain_one_sum = tree_sum(sum_gain_one.reshape(1, -1), n_copy, n_space).reshape(-1)
    return (
        block_out,
        grad_tokens,
        grad_filter,
        total[: sum_in.shape[0]],
        total[sum_in.shape[0] : 2 * sum_in.shape[0]].T,
        gain_one_sum * factor,
        total[2 * sum_in.shape[0], : sum_gain_two.shape[0]].astype(jnp.float32),
    )


def solution(mesh):
    return jax.shard_map(
        body,
        mesh=mesh,
        in_specs=(
            P("copy", "space", None, None),
            P("copy", "space", None, None),
            P(None, None, "space", None),
            P(),
            P(),
            P(),
            P(),
        ),
        out_specs=(
            P("copy", "space", None, None),
            P("copy", "space", None, None),
            P(None, None, "space", None),
            P(),
            P(),
            P(),
            P(),
        ),
        check_vma=False,
    )
```

```python
import functools
import math

import jax
import jax.numpy as jnp
from jax import lax
from jax.experimental import pallas as pl
from jax.experimental.pallas import tpu as pltpu
from jax.sharding import PartitionSpec as P

MESH = pl.DeviceIdType.MESH

EPS = 1e-06


def _filter_sum_kernel(rows, x_ref, o_ref, half_in, part, other, sems):
    me_c = lax.axis_index("copy")
    me_s = lax.axis_index("space")
    core = me_c % 2
    hi = me_c // 2
    mate = (me_c + 1 - 2 * core, me_s)
    far = (me_c + 2 - 4 * hi, me_s)
    half = rows // 2
    barrier = pltpu.get_barrier_semaphore()
    pl.semaphore_signal(barrier, inc=1, device_id=mate, device_id_type=MESH)
    pl.semaphore_signal(barrier, inc=1, device_id=far, device_id_type=MESH)
    pl.semaphore_wait(barrier, 2)
    mine = pl.ds(pl.multiple_of(core * half, 8), half)
    theirs = pl.ds(pl.multiple_of((1 - core) * half, 8), half)
    c1 = pltpu.make_async_remote_copy(
        src_ref=x_ref.at[theirs], dst_ref=half_in, send_sem=sems.at[0], recv_sem=sems.at[1],
        device_id=mate, device_id_type=MESH)
    c1.start()
    c1.wait_recv()
    own = x_ref[mine, :].astype(jnp.float32)
    got = half_in[...].astype(jnp.float32)
    first = jnp.where(core == 0, own, got)
    second = jnp.where(core == 0, got, own)
    part[...] = (first + second).astype(jnp.bfloat16)
    c2 = pltpu.make_async_remote_copy(
        src_ref=part, dst_ref=other, send_sem=sems.at[2], recv_sem=sems.at[3],
        device_id=far, device_id_type=MESH)
    c2.start()
    c2.wait_recv()
    mine_p = part[...].astype(jnp.float32)
    got_p = other[...].astype(jnp.float32)
    total = jnp.where(hi == 0, mine_p + got_p, got_p + mine_p)
    o_ref[mine, :] = total
    c3 = pltpu.make_async_remote_copy(
        src_ref=o_ref.at[mine], dst_ref=o_ref.at[mine], send_sem=sems.at[4], recv_sem=sems.at[5],
        device_id=mate, device_id_type=MESH)
    c3.start()
    pltpu.make_async_remote_copy(
        src_ref=o_ref.at[theirs], dst_ref=o_ref.at[theirs], send_sem=sems.at[4],
        recv_sem=sems.at[5], device_id=mate, device_id_type=MESH).wait_recv()
    c1.wait_send()
    c2.wait_send()
    c3.wait_send()


def filter_sum(x):
    rows, cols = x.shape
    half = rows // 2
    return pl.pallas_call(
        functools.partial(_filter_sum_kernel, rows),
        out_shape=jax.ShapeDtypeStruct((rows, cols), jnp.float32),
        in_specs=[pl.BlockSpec(memory_space=pltpu.VMEM)],
        out_specs=pl.BlockSpec(memory_space=pltpu.VMEM),
        scratch_shapes=[
            pltpu.VMEM((half, cols), x.dtype),
            pltpu.VMEM((half, cols), jnp.bfloat16),
            pltpu.VMEM((half, cols), jnp.bfloat16),
            pltpu.SemaphoreType.DMA((6,)),
        ],
        compiler_params=pltpu.CompilerParams(
            collective_id=1, has_side_effects=True, vmem_limit_bytes=48 * 1024 * 1024
        ),
        cost_estimate=pl.CostEstimate(
            flops=2 * rows * cols, transcendentals=0, bytes_accessed=10 * rows * cols
        ),
    )(x)


def _digit_orders(n_copy, n_space):
    c0, xh = ("copy", 0), ("copy", 1)
    if (n_copy, n_space) == (4, 64):
        xl, z1, z2, z4, y1, y2 = [("space", b) for b in range(6)]
        first = [[c0], [xl, z1], [y1, z2], [y2, xh, z4]]
        second = [[c0], [y1, y2], [xl, z1], [z2, xh, z4]]
        return first, second
    sb = [("space", b) for b in range(n_space.bit_length() - 1)]
    cb = [("copy", b) for b in range(1, n_copy.bit_length() - 1)]
    rest = sb + cb
    first = [[c0]] + [rest[i : i + 2] for i in range(0, len(rest), 2)]
    rest = rest[::-1]
    second = [[c0]] + [rest[i : i + 2] for i in range(0, len(rest), 2)]
    return first, second


def _tree_order(n_copy, n_space):
    if (n_copy, n_space) == (4, 64):
        xl, z1, z2, z4, y1, y2 = [("space", b) for b in range(6)]
        return [[("copy", 0), ("copy", 1), xl], [z1, z2, z4], [y1, y2]]
    return _digit_orders(n_copy, n_space)[0]


def _plan(n_copy, n_space, split=True):
    orders = _digit_orders(n_copy, n_space)
    if not split:
        orders = (_tree_order(n_copy, n_space),) * 2
    me_c = lax.axis_index("copy")
    me_s = lax.axis_index("space")
    core = me_c % 2
    plan = []
    for s in range(len(orders[0])):
        per_core = []
        for order in orders:
            digit = order[s]
            radix = 1 << len(digit)
            bits = []
            for axis, b in digit:
                idx = me_c if axis == "copy" else me_s
                bits.append((idx // (1 << b)) % 2)
            v = sum(bit << i for i, bit in enumerate(bits))
            peers = []
            for d in range(1, radix):
                u = (v + d) % radix
                pc, ps = me_c, me_s
                for i, (axis, b) in enumerate(digit):
                    delta = ((u // (1 << i)) % 2 - bits[i]) * (1 << b)
                    if axis == "copy":
                        pc = pc + delta
                    else:
                        ps = ps + delta
                peers.append((pc, ps))
            per_core.append((radix, peers, v))
        (r0, p0, v0), (r1, p1, v1) = per_core
        assert r0 == r1
        peers = [
            ((1 - core) * a[0] + core * b[0], (1 - core) * a[1] + core * b[1])
            for a, b in zip(p0, p1)
        ]
        plan.append((r0, peers, (1 - core) * v0 + core * v1))
    return plan


def _split_axes(n_copy, n_space):
    radices = [1 << len(d) for d in _digit_orders(n_copy, n_space)[0]]
    if (n_copy, n_space) == (4, 64):
        return radices, [0, 0, 1, 0]
    return radices, [0] * len(radices)


def _all_sum_kernel(n_copy, n_space, scale, a_ref, b_ref, c_ref, o_ref, acc, send, *rest):
    plan = _plan(n_copy, n_space)
    _, axes = _split_axes(n_copy, n_space)
    steps = len(plan)
    recv = rest[:steps]
    rs_send, rs_recv, ag_send, ag_recv, local = rest[steps:]
    rows, cols = acc.shape
    at = 0
    loads = []
    for i, part_ref in enumerate((a_ref, b_ref, c_ref)):
        n = part_ref.shape[0]
        cp = pltpu.make_async_copy(part_ref, acc.at[pl.ds(at, n)], local.at[i])
        cp.start()
        loads.append(cp)
        at += n
    barrier = pltpu.get_barrier_semaphore()
    count = 0
    for radix, peers, _ in plan:
        for peer in peers:
            pl.semaphore_signal(barrier, inc=1, device_id=peer, device_id_type=MESH)
            count += 1
    for cp in loads:
        cp.wait()
    pl.semaphore_wait(barrier, count)

    def window(r0, rl, c0, cl):
        return (pl.ds(pl.multiple_of(r0, 16), rl), pl.ds(pl.multiple_of(c0, 128), cl))

    pending = []
    box = [0, rows, 0, cols]
    slot = 0
    for s, (radix, peers, v) in enumerate(plan):
        r0, rl, c0, cl = box
        if axes[s] == 0:
            part = rl // radix

            def piece(u, r0=r0, c0=c0, cl=cl, part=part):
                return window(r0 + u * part, part, c0, cl)
        else:
            part = cl // radix

            def piece(u, r0=r0, rl=rl, c0=c0, part=part):
                return window(r0, rl, c0 + u * part, part)
        descs = []
        for d, peer in enumerate(peers, start=1):
            u = (v + d) % radix
            w = piece(u)
            send[w] = acc[w].astype(jnp.bfloat16)
            c = pltpu.make_async_remote_copy(
                src_ref=send.at[w],
                dst_ref=recv[s].at[d - 1],
                send_sem=rs_send.at[slot + d - 1],
                recv_sem=rs_recv.at[slot + d - 1],
                device_id=peer,
                device_id_type=MESH,
            )
            c.start()
            descs.append(c)
        keep = piece(v)
        total = acc[keep]
        for d, c in enumerate(descs, start=1):
            c.wait_recv()
            total = total + recv[s][d - 1].astype(jnp.float32)
        acc[keep] = total
        pending += descs
        slot += radix - 1
        if axes[s] == 0:
            box = [r0 + v * part, part, c0, cl]
        else:
            box = [r0, rl, c0 + v * part, part]
    r0, rl, c0, cl = box
    mine = window(r0, rl, c0, cl)
    o_ref[mine] = (acc[mine] * scale).astype(o_ref.dtype)
    for s in reversed(range(steps)):
        radix, peers, v = plan[s]
        slot -= radix - 1
        r0, rl, c0, cl = box
        if axes[s] == 0:
            first = r0 - v * rl

            def piece(u, first=first, rl=rl, c0=c0, cl=cl):
                return window(first + u * rl, rl, c0, cl)

            box = [first, radix * rl, c0, cl]
        else:
            first = c0 - v * cl

            def piece(u, first=first, r0=r0, rl=rl, cl=cl):
                return window(r0, rl, first + u * cl, cl)

            box = [r0, rl, first, radix * cl]
        mine = piece(v)
        descs = []
        for d, peer in enumerate(peers, start=1):
            c = pltpu.make_async_remote_copy(
                src_ref=o_ref.at[mine],
                dst_ref=o_ref.at[mine],
                send_sem=ag_send.at[slot + d - 1],
                recv_sem=ag_recv.at[slot + d - 1],
                device_id=peer,
                device_id_type=MESH,
            )
            c.start()
            descs.append(c)
        for d, peer in enumerate(peers, start=1):
            theirs = piece((v - d + radix) % radix)
            pltpu.make_async_remote_copy(
                src_ref=o_ref.at[theirs],
                dst_ref=o_ref.at[theirs],
                send_sem=ag_send.at[slot + d - 1],
                recv_sem=ag_recv.at[slot + d - 1],
                device_id=peer,
                device_id_type=MESH,
            ).wait_recv()
        pending += descs
    for c in pending:
        c.wait_send()


def all_sum(parts, n_copy, n_space, scale):
    rows = sum(p.shape[0] for p in parts)
    cols = parts[0].shape[1]
    radices, axes = _split_axes(n_copy, n_space)
    recv = []
    rl, cl = rows, cols
    for r, a in zip(radices, axes):
        if a == 0:
            rl //= r
        else:
            cl //= r
        recv.append(pltpu.VMEM((r - 1, rl, cl), jnp.bfloat16))
    links = sum(r - 1 for r in radices)
    return pl.pallas_call(
        functools.partial(_all_sum_kernel, n_copy, n_space, scale),
        out_shape=jax.ShapeDtypeStruct((rows, cols), jnp.bfloat16),
        in_specs=[pl.BlockSpec(memory_space=pltpu.VMEM)] * len(parts),
        out_specs=pl.BlockSpec(memory_space=pltpu.VMEM),
        scratch_shapes=[
            pltpu.VMEM((rows, cols), jnp.float32),
            pltpu.VMEM((rows, cols), jnp.bfloat16),
        ]
        + recv
        + [pltpu.SemaphoreType.DMA((links,)) for _ in range(4)]
        + [pltpu.SemaphoreType.DMA((len(parts),))],
        compiler_params=pltpu.CompilerParams(
            collective_id=3, has_side_effects=True, vmem_limit_bytes=56 * 1024 * 1024
        ),
        cost_estimate=pl.CostEstimate(
            flops=rows * cols, transcendentals=0, bytes_accessed=12 * rows * cols
        ),
    )(*parts)


def _tree_sum_kernel(n_copy, n_space, x_ref, o_ref, *rest):
    plan = _plan(n_copy, n_space, split=False)
    steps = len(plan)
    slots = rest[:steps]
    send_sem, recv_sem = rest[steps:]
    barrier = pltpu.get_barrier_semaphore()
    count = 0
    for _, peers, _ in plan:
        for peer in peers:
            pl.semaphore_signal(barrier, inc=1, device_id=peer, device_id_type=MESH)
            count += 1
    pl.semaphore_wait(barrier, count)
    acc = x_ref[...]
    pending = []
    slot = 0
    for s, (radix, peers, v) in enumerate(plan):
        slots[s][0] = acc
        descs = []
        for d, peer in enumerate(peers, start=1):
            c = pltpu.make_async_remote_copy(
                src_ref=slots[s].at[0],
                dst_ref=slots[s].at[d],
                send_sem=send_sem.at[slot + d - 1],
                recv_sem=recv_sem.at[slot + d - 1],
                device_id=peer,
                device_id_type=MESH,
            )
            c.start()
            descs.append(c)
        for c in descs:
            c.wait_recv()
        total = slots[s][(v + radix) % radix]
        for u in range(1, radix):
            total = total + slots[s][(v - u + radix) % radix]
        acc = total
        pending += descs
        slot += radix - 1
    for c in pending:
        c.wait_send()
    o_ref[...] = acc


def tree_sum(x, n_copy, n_space):
    radices = [1 << len(d) for d in _tree_order(n_copy, n_space)]
    links = sum(r - 1 for r in radices)
    return pl.pallas_call(
        functools.partial(_tree_sum_kernel, n_copy, n_space),
        out_shape=jax.ShapeDtypeStruct(x.shape, jnp.float32),
        in_specs=[pl.BlockSpec(memory_space=pltpu.VMEM)],
        out_specs=pl.BlockSpec(memory_space=pltpu.VMEM),
        scratch_shapes=[pltpu.VMEM((r,) + x.shape, jnp.float32) for r in radices]
        + [pltpu.SemaphoreType.DMA((links,)), pltpu.SemaphoreType.DMA((links,))],
        compiler_params=pltpu.CompilerParams(collective_id=2, has_side_effects=True),
        cost_estimate=pl.CostEstimate(
            flops=links * x.size, transcendentals=0, bytes_accessed=8 * links * x.size
        ),
    )(x)


def dft_parts(length):
    index = jnp.arange(length, dtype=jnp.int32)
    phase = index[:, None] * index[None, :] % length
    angle = phase.astype(jnp.float32) * (2.0 * math.pi / length)
    factor = 1.0 / math.sqrt(length)
    return (
        (jnp.cos(angle) * factor).astype(jnp.bfloat16),
        (jnp.sin(angle) * factor).astype(jnp.bfloat16),
    )


def row_table(length):
    cosine, sine = dft_parts(length)
    return jnp.stack([cosine, -sine])


def column_table(length, direction):
    cosine, sine = dft_parts(length)
    upper = jnp.stack([cosine, direction * sine], axis=1)
    lower = jnp.stack([-direction * sine, cosine], axis=1)
    return jnp.stack([upper, lower])


def layer_norm(values):
    centre = jnp.mean(values, axis=-1, keepdims=True)
    centred = values - centre
    variance = jnp.mean(centred * centred, axis=-1, keepdims=True)
    rstd_value = lax.rsqrt(variance + EPS)
    return (centred * rstd_value, rstd_value)


def norm_backward(upstream, normed, rstd_value, gain):
    scaled = upstream * gain
    result = (
        scaled
        - jnp.mean(scaled, axis=-1, keepdims=True)
        - normed * jnp.mean(scaled * normed, axis=-1, keepdims=True)
    ) * rstd_value
    lead = tuple(range(upstream.ndim - 1))
    return (result, jnp.sum(upstream * normed, axis=lead))


def apply_filter(spectrum, filter_weight, direction):
    real_part = spectrum[0].astype(jnp.float32)
    imag_part = spectrum[1].astype(jnp.float32)
    kernel_real = filter_weight[0].astype(jnp.float32)
    kernel_imag = direction * filter_weight[1].astype(jnp.float32)
    return jnp.stack(
        [
            kernel_real * real_part - kernel_imag * imag_part,
            kernel_real * imag_part + kernel_imag * real_part,
        ]
    )


def exact_gelu(values):
    return jax.nn.gelu(values, approximate=False)


def spectral(values, filter_weight, direction, early=None, late=None):
    width = values.shape[2]
    rows_tab = row_table(width)
    rows = jnp.einsum(
        "pkw,bhwc->pbhkc", rows_tab, values, preferred_element_type=jnp.float32
    ).astype(jnp.bfloat16)
    columns = lax.all_to_all(rows, "space", split_axis=3, concat_axis=2, tiled=True)
    held = None
    if early is not None:
        columns, held = lax.optimization_barrier((columns, early()))
    height = columns.shape[2]
    spectrum = jnp.einsum(
        "qmph,pbhkc->qbmkc", column_table(height, 1), columns, preferred_element_type=jnp.float32
    ).astype(jnp.bfloat16)
    weighted = apply_filter(spectrum, filter_weight[:, None], direction).astype(jnp.bfloat16)
    returned = jnp.einsum(
        "qmph,pbhkc->qbmkc", column_table(height, -1), weighted, preferred_element_type=jnp.float32
    ).astype(jnp.bfloat16)
    back_rows = lax.all_to_all(returned, "space", split_axis=2, concat_axis=3, tiled=True)
    tail = None
    if late is not None:
        back_rows, tail = lax.optimization_barrier((back_rows, late(spectrum)))
    output = jnp.einsum("pkw,pbhkc->bhwc", rows_tab, back_rows, preferred_element_type=jnp.float32)
    return (output, spectrum, held, tail)


def body(noisy_tokens, grad_out, filter_weight, weight_in, weight_out, gain_one, gain_two):
    batch, rows_dev, width, chans = noisy_tokens.shape
    inputs = noisy_tokens.astype(jnp.float32)
    normed_one, rstd_one = layer_norm(inputs)
    mixed_in = (normed_one * gain_one).astype(jnp.bfloat16)
    upstream = grad_out.reshape(-1, chans)
    spatial, spectrum, grad_act, _ = spectral(
        mixed_in,
        filter_weight,
        1,
        lambda: jnp.dot(upstream, weight_out.T, preferred_element_type=jnp.float32),
    )
    normed_two, rstd_two = layer_norm(spatial)
    mlp_in = (normed_two * gain_two).astype(jnp.bfloat16).reshape(-1, chans)
    preact = jnp.dot(mlp_in, weight_in, preferred_element_type=jnp.float32)
    activated = exact_gelu(preact).astype(jnp.bfloat16)
    mlp_out = jnp.dot(activated, weight_out, preferred_element_type=jnp.float32)
    block_out = (inputs + mlp_out.reshape(inputs.shape)).astype(jnp.bfloat16)
    grad_pre = jax.vjp(exact_gelu, preact)[1](grad_act)[0].astype(jnp.bfloat16)
    sum_out_t = jnp.dot(upstream.T, activated, preferred_element_type=jnp.float32)
    sum_in = jnp.dot(mlp_in.T, grad_pre, preferred_element_type=jnp.float32)
    grad_mlp = jnp.dot(grad_pre, weight_in.T, preferred_element_type=jnp.float32).reshape(
        inputs.shape
    )
    grad_spatial, sum_gain_two = norm_backward(grad_mlp, normed_two, rstd_two, gain_two)
    total_tokens = batch * lax.axis_size("copy") * rows_dev * lax.axis_size("space") * width
    factor = 1.0 / math.sqrt(total_tokens)
    n_copy, n_space = lax.axis_size("copy"), lax.axis_size("space")
    lanes = sum_in.shape[1]
    radices, axes = _split_axes(n_copy, n_space)
    row_div = 16 * math.prod(r for r, a in zip(radices, axes) if a == 0)
    extra = -(-(2 * sum_in.shape[0] + 1) // row_div) * row_div - 2 * sum_in.shape[0]

    def weight_sums():
        gains_block = jnp.pad(
            sum_gain_two[None, :], ((0, extra - 1), (0, lanes - sum_gain_two.shape[0]))
        )
        return all_sum([sum_in, sum_out_t, gains_block], n_copy, n_space, factor)

    def filter_grad(adjoint):
        spec_f = spectrum.astype(jnp.float32)
        adj_f = adjoint.astype(jnp.float32)
        filter_terms = jnp.stack(
            [
                jnp.sum(adj_f[0] * spec_f[0] + adj_f[1] * spec_f[1], axis=0),
                jnp.sum(adj_f[1] * spec_f[0] - adj_f[0] * spec_f[1], axis=0),
            ]
        )
        fshape = filter_terms.shape
        return filter_sum(
            filter_terms.astype(jnp.bfloat16).reshape(
                fshape[0] * fshape[1], fshape[2] * fshape[3]
            )
        ).reshape(fshape)

    back_spatial, _, total, grad_filter = spectral(
        grad_spatial.astype(jnp.bfloat16), filter_weight, -1, weight_sums, filter_grad
    )
    grad_normed, sum_gain_one = norm_backward(back_spatial, normed_one, rstd_one, gain_one)
    grad_tokens = (grad_out.astype(jnp.float32) + grad_normed).astype(jnp.bfloat16)
    gain_one_sum = tree_sum(sum_gain_one.reshape(1, -1), n_copy, n_space).reshape(-1)
    return (
        block_out,
        grad_tokens,
        grad_filter,
        total[: sum_in.shape[0]],
        total[sum_in.shape[0] : 2 * sum_in.shape[0]].T,
        gain_one_sum * factor,
        total[2 * sum_in.shape[0], : sum_gain_two.shape[0]].astype(jnp.float32),
    )


def solution(mesh):
    return jax.shard_map(
        body,
        mesh=mesh,
        in_specs=(
            P("copy", "space", None, None),
            P("copy", "space", None, None),
            P(None, None, "space", None),
            P(),
            P(),
            P(),
            P(),
        ),
        out_specs=(
            P("copy", "space", None, None),
            P("copy", "space", None, None),
            P(None, None, "space", None),
            P(),
            P(),
            P(),
            P(),
        ),
        check_vma=False,
    )
```
